32 devices in a mesh: dp: 16 (over z, x, core), tensor: 2 (over y).
Axes of the slice: x: 2, y: 2, z: 4, core: 2. Of those that a mesh axis runs over, the one named last changes fastest.
Arguments:
- inputs: bfloat16 [16384, 1536], P(('dp', 'tensor')), may hold values from -6 to 6
- text_states: bfloat16 [16, 64, 1536], P('dp'), may hold values from -6 to 6
- self_query: bfloat16 [1536, 1536], P('dp', 'tensor'), may hold values from -0.15625 to 0.15625
- self_key: bfloat16 [1536, 1536], P('dp', 'tensor'), may hold values from -0.15625 to 0.15625
- self_value: bfloat16 [1536, 1536], P('dp', 'tensor'), may hold values from -0.15625 to 0.15625
- self_output: bfloat16 [1536, 1536], P('tensor', 'dp'), may hold values from -1.25 to 1.25
- cross_query: bfloat16 [1536, 1536], P('dp', 'tensor'), may hold values from -0.15625 to 0.15625
- cross_key: bfloat16 [1536, 1536], P('dp', 'tensor'), may hold values from -0.15625 to 0.15625
- cross_value: bfloat16 [1536, 1536], P('dp', 'tensor'), may hold values from -0.15625 to 0.15625
- cross_output: bfloat16 [1536, 1536], P('tensor', 'dp'), may hold values from -0.625 to 0.625
- inner_weight: bfloat16 [1536, 6144], P('dp', 'tensor'), may hold values from -0.15625 to 0.15625
- outer_weight: bfloat16 [6144, 1536], P('tensor', 'dp'), may hold values from -0.078125 to 0.078125
- norm_gains: float32 [3, 1536], replicated, may hold values from 0.25 to 1.75
- norm_shifts: float32 [3, 1536], replicated, may hold values from -2 to 2
- cotangent: bfloat16 [16384, 1536], P(('dp', 'tensor')), may hold values from -6 to 6
Outputs:
- output: bfloat16 [16384, 1536], P(('dp', 'tensor'))
- input_grad: float32 [16384, 1536], P(('dp', 'tensor'))
- text_grad: float32 [16, 64, 1536], P('dp', None, 'tensor')
- self_query_grad: float32 [1536, 1536], P('dp', 'tensor')
- self_key_grad: float32 [1536, 1536], P('dp', 'tensor')
- self_value_grad: float32 [1536, 1536], P('dp', 'tensor')
- self_output_grad: float32 [1536, 1536], P('tensor', 'dp')
- cross_query_grad: float32 [1536, 1536], P('dp', 'tensor')
- cross_key_grad: float32 [1536, 1536], P('dp', 'tensor')
- cross_value_grad: float32 [1536, 1536], P('dp', 'tensor')
- cross_output_grad: float32 [1536, 1536], P('tensor', 'dp')
- inner_weight_grad: float32 [1536, 6144], P('dp', 'tensor')
- outer_weight_grad: float32 [6144, 1536], P('tensor', 'dp')
- gains_grad: float32 [3, 1536], replicated
- shifts_grad: float32 [3, 1536], replicated
The draws below stay inside these ranges and needn't reach their ends.
All inputs are finite; a program needn't handle non-finite values.
Results may differ from the reference program's by a relative error of at most 0.02.
Values may be sent and summed in bfloat16 or wider, within the bound.
No kernel may reach another device: no remote copies, remote signals or barrier semaphores. Data moves between devices by JAX's collectives and lax.ppermute only.
A program may use at most 320 MiB of HBM per device.

```python
import math
import jax
import jax.numpy as jnp
from jax import lax

D = 1536
HEADS = 24
HD = 64
FF = 6144
TEXT = 64
LEN = 1024
CLIPS = 16
TOKENS = 16384


def block_scale(stream_key, dims, pieces, low, high):
    def one(position, shards_of):
        steps = jax.random.uniform(jax.random.fold_in(jax.random.fold_in(stream_key, 6), position), (shards_of,), jnp.float32, low / len(pieces), high / len(pieces))
        return jnp.repeat(jnp.exp(steps), dims[position] // shards_of).reshape((-1,) + (1,) * (len(dims) - position - 1))

    level = one(*pieces[0])
    for cut in pieces[1:]:
        level = level * one(*cut)
    return level


def scatter_about(stream_key, dims, scale, bound, cuts=(), dtype=jnp.bfloat16):
    values = scale * jax.random.normal(stream_key, dims, jnp.float32)
    if cuts:
        values = values * block_scale(stream_key, dims, cuts, -0.22, 0.18)
    return jnp.clip(values, -bound, bound).astype(dtype)


def setup_inputs(seed: int = 0) -> dict:
    key_list = jax.random.split(jax.random.key(seed), 16)
    inputs = scatter_about(key_list[0], (TOKENS, D), 1.0, 6.0, ((0, 32),))
    text_states = scatter_about(key_list[1], (CLIPS, TEXT, D), 1.0, 6.0, ((0, 16),))
    self_query = scatter_about(key_list[2], (D, D), D ** -0.5, 0.15625, ((0, 16), (1, 2)))
    self_key = scatter_about(key_list[3], (D, D), D ** -0.5, 0.15625, ((0, 16), (1, 2)))
    self_value = scatter_about(key_list[4], (D, D), D ** -0.5, 0.15625, ((0, 16), (1, 2)))
    self_output = scatter_about(key_list[5], (D, D), (D // 64) ** -0.5, 1.25, ((0, 2), (1, 16)))
    cross_query = scatter_about(key_list[6], (D, D), D ** -0.5, 0.15625, ((0, 16), (1, 2)))
    cross_key = scatter_about(key_list[7], (D, D), D ** -0.5, 0.15625, ((0, 16), (1, 2)))
    cross_value = scatter_about(key_list[8], (D, D), D ** -0.5, 0.15625, ((0, 16), (1, 2)))
    cross_output = scatter_about(key_list[9], (D, D), (D // 16) ** -0.5, 0.625, ((0, 2), (1, 16)))
    inner_weight = scatter_about(key_list[10], (D, FF), D ** -0.5, 0.15625, ((0, 16), (1, 2)))
    outer_weight = scatter_about(key_list[11], (FF, D), FF ** -0.5, 0.078125, ((0, 2), (1, 16)))
    norm_gains = jnp.clip(1.0 + 0.15 * jax.random.normal(key_list[12], (3, D), jnp.float32), 0.25, 1.75)
    norm_shifts = scatter_about(key_list[13], (3, D), 0.3, 2.0, (), jnp.float32)
    cotangent = scatter_about(key_list[14], (TOKENS, D), 1.0, 6.0, ((0, 32),))
    return dict(inputs=inputs, text_states=text_states, self_query=self_query, self_key=self_key, self_value=self_value, self_output=self_output, cross_query=cross_query, cross_key=cross_key, cross_value=cross_value, cross_output=cross_output, inner_weight=inner_weight, outer_weight=outer_weight, norm_gains=norm_gains, norm_shifts=norm_shifts, cotangent=cotangent)


EPS = 1e-05
MASKED = -1e+30

@jax.custom_vjp
def low(v):
    return lax.optimization_barrier(v.astype(jnp.bfloat16)).astype(jnp.float32)

@jax.custom_vjp
def low_back(v):
    return v

def low_keep(v):
    return (low(v), None)

def low_pass(kept, grad):
    return (grad,)

def back_keep(v):
    return (v, None)

def back_low(kept, grad):
    return (low(grad),)
low.defvjp(low_keep, low_pass)
low_back.defvjp(back_keep, back_low)

def norm_rows(value, gain, shift):
    mean = lax.optimization_barrier(jnp.mean(value, axis=-1, keepdims=True))
    centred = value - mean
    spread = lax.optimization_barrier(jnp.mean(centred * centred, axis=-1, keepdims=True))
    return centred * lax.rsqrt(spread + EPS) * gain + shift

def product(left, right):
    return jnp.dot(left, right, precision=lax.Precision.HIGHEST)

def attend_clip(block, masked):
    query, key, value = block
    scale = 1.0 / math.sqrt(HD)
    rows = query.shape[0]
    cols = key.shape[0]
    query_heads = query.reshape(rows, HEADS, HD)
    key_heads = key.reshape(cols, HEADS, HD)
    value_heads = value.reshape(cols, HEADS, HD)
    scores = jnp.einsum('qhd,khd->hqk', query_heads, key_heads, precision=lax.Precision.HIGHEST) * scale
    scores = low_back(scores)
    if masked:
        places = jnp.arange(rows)
        allowed = places[:, None] >= places[None, :]
        scores = jnp.where(allowed[None], scores, MASKED)
    weights = low(jax.nn.softmax(scores, axis=-1))
    mixed = jnp.einsum('hqk,khd->qhd', weights, value_heads, precision=lax.Precision.HIGHEST)
    return mixed.reshape(rows, HEADS * HD)

def self_clip(block):
    return attend_clip(block, True)

def cross_clip(block):
    return attend_clip(block, False)

def forward(frames, text, s_query, s_key, s_value, s_output, c_query, c_key, c_value, c_output, w_inner, w_outer, gains, shifts):
    clips = frames.shape[0] // LEN
    normed1 = low(norm_rows(frames, gains[0], shifts[0]))
    query1 = low_back(low(product(normed1, s_query)))
    first_key = low_back(low(product(normed1, s_key)))
    value1 = low_back(low(product(normed1, s_value)))
    mixed1 = lax.map(jax.checkpoint(self_clip), (query1.reshape(clips, LEN, D), first_key.reshape(clips, LEN, D), value1.reshape(clips, LEN, D)))
    mixed1 = low_back(low(mixed1.reshape(-1, D)))
    state1 = frames + low_back(product(mixed1, s_output))
    normed2 = low(norm_rows(state1, gains[1], shifts[1]))
    query2 = low_back(low(product(normed2, c_query)))
    text_flat = text.reshape(-1, D)
    key2 = low_back(low(product(text_flat, c_key))).reshape(clips, TEXT, D)
    value2 = low_back(low(product(text_flat, c_value))).reshape(clips, TEXT, D)
    mixed2 = lax.map(jax.checkpoint(cross_clip), (query2.reshape(clips, LEN, D), key2, value2))
    mixed2 = low_back(low(mixed2.reshape(-1, D)))
    state2 = state1 + low_back(product(mixed2, c_output))
    normed3 = low(norm_rows(state2, gains[2], shifts[2]))
    inner = low_back(product(normed3, w_inner))
    active = low(jax.nn.gelu(inner, approximate=False))
    return state2 + low_back(product(active, w_outer))

def reference(inputs, text_states, self_query, self_key, self_value, self_output, cross_query, cross_key, cross_value, cross_output, inner_weight, outer_weight, norm_gains, norm_shifts, cotangent):
    floats = [a.astype(jnp.float32) for a in (inputs, text_states, self_query, self_key, self_value, self_output, cross_query, cross_key, cross_value, cross_output, inner_weight, outer_weight, norm_gains, norm_shifts)]
    result, pullback = jax.vjp(forward, *floats)
    grads = pullback(cotangent.astype(jnp.float32))
    return (result.astype(jnp.bfloat16), grads[0], grads[1], grads[2], grads[3], grads[4], grads[5], grads[6], grads[7], grads[8], grads[9], grads[10], grads[11], grads[12], grads[13])
```

```python
from functools import partial
import math

import jax
import jax.numpy as jnp
from jax import lax
from jax.experimental import pallas as pl
from jax.experimental.pallas import tpu as pltpu
from jax.sharding import PartitionSpec as P

HD = 64
TEXT = 64
LEN = 1024


EPS = 1e-05
MASKED = -1e30


def norm_rows(value, gain, shift):
    mean = jnp.mean(value, axis=-1, keepdims=True)
    centred = value - mean
    spread = jnp.mean(centred * centred, axis=-1, keepdims=True)
    return centred * lax.rsqrt(spread + EPS) * gain + shift


def norm_back(value, gain, shift, incoming):
    ignored, pullback = jax.vjp(norm_rows, value, gain, shift)
    return pullback(incoming)


def gelu_exact(value):
    return jax.nn.gelu(value, approximate=False)


def transposed_times(left, right):
    return lax.dot_general(
        left, right, (((0,), (0,)), ((), ())), preferred_element_type=jnp.float32
    )


def times_t(left, right):
    return lax.dot_general(
        left, right, (((1,), (1,)), ((), ())), preferred_element_type=jnp.float32
    )


def apply_projection(left, right):
    return jnp.dot(left, right, preferred_element_type=jnp.float32).astype(jnp.bfloat16)


def scores_of(query, key, masked):
    scale = 1.0 / math.sqrt(HD)
    scores = jnp.einsum("qhd,khd->hqk", query, key, preferred_element_type=jnp.float32) * scale
    if masked:
        places = jnp.arange(query.shape[0])
        allowed = places[:, None] >= places[None, :]
        scores = jnp.where(allowed[None], scores, MASKED)
    return scores


def attend(block, masked):
    query, key, value = block
    scores = scores_of(query, key, masked)
    highest = jnp.max(scores, axis=-1, keepdims=True)
    total = jnp.sum(jnp.exp(scores - highest), axis=-1, keepdims=True)
    log_total = highest + jnp.log(total)
    weights = jnp.exp(scores - log_total).astype(jnp.bfloat16)
    mixed = jnp.einsum("hqk,khd->qhd", weights, value, preferred_element_type=jnp.float32)
    return (mixed.astype(jnp.bfloat16), log_total)


def attend_back(block, masked):
    query, key, value, log_total, grad_mixed = block
    scale = 1.0 / math.sqrt(HD)
    weights = jnp.exp(scores_of(query, key, masked) - log_total)
    rounded = weights.astype(jnp.bfloat16)
    d_value = jnp.einsum("hqk,qhd->khd", rounded, grad_mixed, preferred_element_type=jnp.float32)
    d_weights = jnp.einsum("qhd,khd->hqk", grad_mixed, value, preferred_element_type=jnp.float32)
    centred = d_weights - jnp.sum(weights * d_weights, axis=-1, keepdims=True)
    d_scores = (weights * centred).astype(jnp.bfloat16)
    d_query = jnp.einsum("hqk,khd->qhd", d_scores, key, preferred_element_type=jnp.float32) * scale
    d_key = jnp.einsum("hqk,qhd->khd", d_scores, query, preferred_element_type=jnp.float32) * scale
    return (d_query.astype(jnp.bfloat16), d_key.astype(jnp.bfloat16), d_value.astype(jnp.bfloat16))


def spread_rows(normed):
    return lax.all_gather(normed, "tensor", axis=0, tiled=True)


def spread_grads(grad):
    return lax.all_gather(grad.astype(jnp.bfloat16), "tensor", axis=0, tiled=True)


def branch_total(mixed, weight):
    return lax.psum_scatter(
        jnp.dot(mixed, weight, preferred_element_type=jnp.float32),
        "tensor",
        scatter_dimension=0,
        tiled=True,
    )


def normalized_total(pairs):
    total = None
    for grad, weight in pairs:
        added = times_t(grad, weight)
        total = added if total is None else total + added
    return lax.psum_scatter(total, "tensor", scatter_dimension=0, tiled=True)


def on_device(
    inputs,
    text_states,
    self_query,
    self_key,
    self_value,
    self_output,
    cross_query,
    cross_key,
    cross_value,
    cross_output,
    inner_weight,
    outer_weight,
    norm_gains,
    norm_shifts,
    cotangent,
):
    (
        gathered_self_query,
        gathered_self_key,
        gathered_self_value,
        full_soutput,
        full_cquery,
        full_ckey,
        full_cvalue,
        full_coutput,
        full_inner,
        full_outer,
    ) = (
        lax.all_gather(self_query, "dp", axis=0, tiled=True),
        lax.all_gather(self_key, "dp", axis=0, tiled=True),
        lax.all_gather(self_value, "dp", axis=0, tiled=True),
        lax.all_gather(self_output, "dp", axis=1, tiled=True),
        lax.all_gather(cross_query, "dp", axis=0, tiled=True),
        lax.all_gather(cross_key, "dp", axis=0, tiled=True),
        lax.all_gather(cross_value, "dp", axis=0, tiled=True),
        lax.all_gather(cross_output, "dp", axis=1, tiled=True),
        lax.all_gather(inner_weight, "dp", axis=0, tiled=True),
        lax.all_gather(outer_weight, "dp", axis=1, tiled=True),
    )
    width = inputs.shape[1]
    clips = text_states.shape[0]
    local_heads = gathered_self_query.shape[1] // HD

    def heads(value, length):
        return value.reshape(clips, length, local_heads, HD)

    def flatten(value):
        return value.reshape(-1, local_heads * HD)

    start = inputs.astype(jnp.float32)
    first_rows = spread_rows(norm_rows(start, norm_gains[0], norm_shifts[0]).astype(jnp.bfloat16))
    query1 = apply_projection(first_rows, gathered_self_query)
    first_key = apply_projection(first_rows, gathered_self_key)
    value1 = apply_projection(first_rows, gathered_self_value)
    mixed1, lse1 = lax.map(
        partial(attend, masked=True),
        (heads(query1, LEN), heads(first_key, LEN), heads(value1, LEN)),
    )
    mixed1 = flatten(mixed1)
    state1 = start + branch_total(mixed1, full_soutput)
    rows2 = spread_rows(norm_rows(state1, norm_gains[1], norm_shifts[1]).astype(jnp.bfloat16))
    query2 = apply_projection(rows2, full_cquery)
    text_flat = text_states.reshape(-1, width)
    key2 = apply_projection(text_flat, full_ckey)
    value2 = apply_projection(text_flat, full_cvalue)
    mixed2, lse2 = lax.map(
        partial(attend, masked=False), (heads(query2, LEN), heads(key2, TEXT), heads(value2, TEXT))
    )
    mixed2 = flatten(mixed2)
    state2 = state1 + branch_total(mixed2, full_coutput)
    rows3 = spread_rows(norm_rows(state2, norm_gains[2], norm_shifts[2]).astype(jnp.bfloat16))
    inner = jnp.dot(rows3, full_inner, preferred_element_type=jnp.float32)
    active_float, gelu_pull = jax.vjp(gelu_exact, inner)
    active = active_float.astype(jnp.bfloat16)
    result = state2 + branch_total(active, full_outer)
    output = result.astype(jnp.bfloat16)
    grad3 = cotangent.astype(jnp.float32)
    grads_outer = spread_grads(grad3)
    d_outer = transposed_times(active, grads_outer)
    d_inner = gelu_pull(times_t(grads_outer, full_outer))[0].astype(jnp.bfloat16)
    d_innerw = transposed_times(rows3, d_inner)
    back3 = normalized_total(((d_inner, full_inner),))
    d_state2, gain_three, shift_three = norm_back(state2, norm_gains[2], norm_shifts[2], back3)
    grad2 = grad3 + d_state2
    grads_cross = spread_grads(grad2)
    d_coutput = transposed_times(mixed2, grads_cross)
    d_mixed2 = times_t(grads_cross, full_coutput).astype(jnp.bfloat16)
    d_query2, d_key2, d_value2 = lax.map(
        partial(attend_back, masked=False),
        (heads(query2, LEN), heads(key2, TEXT), heads(value2, TEXT), lse2, heads(d_mixed2, LEN)),
    )
    d_query2 = flatten(d_query2)
    d_key2 = flatten(d_key2)
    d_value2 = flatten(d_value2)
    d_cquery = transposed_times(rows2, d_query2)
    d_ckey = transposed_times(text_flat, d_key2)
    d_cvalue = transposed_times(text_flat, d_value2)
    text_terms = (times_t(d_key2, full_ckey) + times_t(d_value2, full_cvalue)).reshape(
        clips, TEXT, width
    )
    text_grad = lax.psum_scatter(
        text_terms.astype(jnp.bfloat16), "tensor", scatter_dimension=2, tiled=True
    ).astype(jnp.float32)
    back2 = normalized_total(((d_query2, full_cquery),))
    d_state1, gain_two, shift_two = norm_back(state1, norm_gains[1], norm_shifts[1], back2)
    grad1 = grad2 + d_state1
    grads_self = spread_grads(grad1)
    d_soutput = transposed_times(mixed1, grads_self)
    d_mixed1 = times_t(grads_self, full_soutput).astype(jnp.bfloat16)
    first_query_grad, first_key_grad, first_value_grad = lax.map(
        partial(attend_back, masked=True),
        (heads(query1, LEN), heads(first_key, LEN), heads(value1, LEN), lse1, heads(d_mixed1, LEN)),
    )
    first_query_grad = flatten(first_query_grad)
    first_key_grad = flatten(first_key_grad)
    first_value_grad = flatten(first_value_grad)
    d_squery = transposed_times(first_rows, first_query_grad)
    self_key_partial = transposed_times(first_rows, first_key_grad)
    d_svalue = transposed_times(first_rows, first_value_grad)
    first_backward = normalized_total(
        (
            (first_query_grad, gathered_self_query),
            (first_key_grad, gathered_self_key),
            (first_value_grad, gathered_self_value),
        )
    )
    d_start, gain_one, shift_one = norm_back(start, norm_gains[0], norm_shifts[0], first_backward)
    input_grad = grad1 + d_start
    gains_grad, shifts_grad = lax.psum(
        (
            jnp.stack([gain_one, gain_two, gain_three]),
            jnp.stack([shift_one, shift_two, shift_three]),
        ),
        ("dp", "tensor"),
    )
    summed = (
        lax.psum_scatter(
            d_squery.astype(jnp.bfloat16), "dp", scatter_dimension=0, tiled=True
        ).astype(jnp.float32),
        lax.psum_scatter(
            self_key_partial.astype(jnp.bfloat16), "dp", scatter_dimension=0, tiled=True
        ).astype(jnp.float32),
        lax.psum_scatter(
            d_svalue.astype(jnp.bfloat16), "dp", scatter_dimension=0, tiled=True
        ).astype(jnp.float32),
        lax.psum_scatter(
            d_soutput.astype(jnp.bfloat16), "dp", scatter_dimension=1, tiled=True
        ).astype(jnp.float32),
        lax.psum_scatter(
            d_cquery.astype(jnp.bfloat16), "dp", scatter_dimension=0, tiled=True
        ).astype(jnp.float32),
        lax.psum_scatter(d_ckey.astype(jnp.bfloat16), "dp", scatter_dimension=0, tiled=True).astype(
            jnp.float32
        ),
        lax.psum_scatter(
            d_cvalue.astype(jnp.bfloat16), "dp", scatter_dimension=0, tiled=True
        ).astype(jnp.float32),
        lax.psum_scatter(
            d_coutput.astype(jnp.bfloat16), "dp", scatter_dimension=1, tiled=True
        ).astype(jnp.float32),
        lax.psum_scatter(
            d_innerw.astype(jnp.bfloat16), "dp", scatter_dimension=0, tiled=True
        ).astype(jnp.float32),
        lax.psum_scatter(
            d_outer.astype(jnp.bfloat16), "dp", scatter_dimension=1, tiled=True
        ).astype(jnp.float32),
    )
    return (
        output,
        input_grad,
        text_grad,
        summed[0],
        summed[1],
        summed[2],
        summed[3],
        summed[4],
        summed[5],
        summed[6],
        summed[7],
        summed[8],
        summed[9],
        gains_grad,
        shifts_grad,
    )


BF = jnp.bfloat16
F32 = jnp.float32
NN = (((1,), (0,)), ((), ()))
NT = (((1,), (1,)), ((), ()))
TN = (((0,), (0,)), ((), ()))
QB = 256
PAIR = 128
QUAD = 256


def mm(left, right, dims):
    return lax.dot_general(left, right, dims, preferred_element_type=F32)


def lanes_of(width, head):
    lane = lax.broadcasted_iota(jnp.int32, (1, width), 1)
    return (lane >= head * HD) & (lane < (head + 1) * HD)


def only(value, mask):
    return jnp.where(mask, value, jnp.zeros_like(value))


def pieces_of(block):
    start = block * QB
    found = [(0, start, False)] if block else []
    return found + [(start, start + QB, True)]


def causal():
    key = lax.broadcasted_iota(jnp.int32, (QB, QB), 0)
    place = lax.broadcasted_iota(jnp.int32, (QB, QB), 1)
    return key <= place


def to_places(t, ref, held, half):
    low = pl.multiple_of(t * half, half)
    high = pl.multiple_of((1 - t) * half, half)
    held[0:half, :] = ref[pl.ds(low, half), :]
    held[half : 2 * half, :] = ref[pl.ds(high, half), :]


def row_of(t, start, half):
    side = start // half
    base = (1 - t) * half if side else t * half
    return pl.multiple_of(base + start % half, QB)


def self_kernel(t_ref, q_ref, k_ref, v_ref, o_ref, lse_ref, qs, ks, vs):
    t = t_ref[0]
    length = q_ref.shape[0]
    half = length // 2
    for ref, held in ((q_ref, qs), (k_ref, ks), (v_ref, vs)):
        to_places(t, ref, held, half)
    allowed = causal()
    for block in range(length // QB):
        rows = slice(block * QB, (block + 1) * QB)
        query = qs[rows, :] * BF(0.125)
        mixed = []
        for head in range(2):
            mine = only(query, lanes_of(PAIR, head))
            parts = []
            for a, b, edge in pieces_of(block):
                score = mm(ks[a:b, :], mine, NT)
                parts.append(jnp.where(allowed, score, MASKED) if edge else score)
            top = jnp.max(parts[0], axis=0, keepdims=True)
            for part in parts[1:]:
                top = jnp.maximum(top, jnp.max(part, axis=0, keepdims=True))
            total, out = None, None
            for part, (a, b, edge) in zip(parts, pieces_of(block)):
                power = jnp.exp(part - top)
                added = jnp.sum(power, axis=0, keepdims=True)
                term = mm(vs[a:b, :], power.astype(BF), TN)
                total = added if total is None else total + added
                out = term if out is None else out + term
            lse_ref[0, head : head + 1, rows] = top + jnp.log(total)
            mixed.append(out[head * HD : (head + 1) * HD, :] / total)
        both = jnp.concatenate(mixed, axis=0)
        o_ref[pl.ds(row_of(t, block * QB, half), QB), :] = both.T.astype(BF)


def self_forward(t, qkv):
    length, width = qkv.shape
    pairs = width // (3 * PAIR)
    spec = lambda part: pl.BlockSpec((length, PAIR), lambda j, s: (0, part * pairs + j))
    return pl.pallas_call(
        self_kernel,
        out_shape=(
            jax.ShapeDtypeStruct((length, pairs * PAIR), BF),
            jax.ShapeDtypeStruct((pairs, 8, length), F32),
        ),
        grid_spec=pltpu.PrefetchScalarGridSpec(
            num_scalar_prefetch=1,
            grid=(pairs,),
            in_specs=[spec(0), spec(1), spec(2)],
            out_specs=[
                pl.BlockSpec((length, PAIR), lambda j, s: (0, j)),
                pl.BlockSpec((1, 8, length), lambda j, s: (j, 0, 0)),
            ],
            scratch_shapes=[pltpu.VMEM((length, PAIR), BF)] * 3,
        ),
        name="self_attend",
        cost_estimate=pl.CostEstimate(
            flops=16 * length * length * PAIR * pairs // 3,
            transcendentals=length * length * pairs,
            bytes_accessed=8 * length * PAIR * pairs,
        ),
    )(t, qkv, qkv, qkv)


def self_back_kernel(
    t_ref, q_ref, k_ref, v_ref, o_ref, do_ref, lse_ref, out_ref, qs, ks, vs, os, dos, dk, dv, dkb, dvb
):
    t = t_ref[0]
    length = q_ref.shape[0]
    half = length // 2
    step = pl.program_id(1)

    @pl.when(step == 0)
    def _():
        for ref, held in ((q_ref, qs), (k_ref, ks), (v_ref, vs), (o_ref, os), (do_ref, dos)):
            to_places(t, ref, held, half)
        allowed = causal()
        blocks = length // QB
        for block in reversed(range(blocks)):
            rows = slice(block * QB, (block + 1) * QB)
            query = qs[rows, :] * BF(0.125)
            grad = dos[rows, :]
            product = (grad.astype(F32) * os[rows, :].astype(F32)).T
            mine = [only(query, lanes_of(PAIR, head)) for head in range(2)]
            mine_grad = [only(grad, lanes_of(PAIR, head)) for head in range(2)]
            both_query = jnp.concatenate(mine, axis=0)
            both_grad = jnp.concatenate(mine_grad, axis=0)
            d_query = [None, None]
            for a, b, edge in pieces_of(block):
                weights, d_scores = [], []
                for head in range(2):
                    drop = jnp.sum(product[head * HD : (head + 1) * HD, :], axis=0, keepdims=True)
                    score = mm(ks[a:b, :], mine[head], NT)
                    power = jnp.exp(score - lse_ref[0, head : head + 1, rows])
                    if edge:
                        power = jnp.where(allowed, power, 0.0)
                    d_power = mm(vs[a:b, :], mine_grad[head], NT)
                    d_score = (power * (d_power - drop)).astype(BF)
                    weights.append(power.astype(BF))
                    d_scores.append(d_score)
                    term = mm(ks[a:b, :], d_score, TN)
                    d_query[head] = term if d_query[head] is None else d_query[head] + term
                add_v = mm(jnp.concatenate(weights, axis=1), both_grad, NN)
                add_k = mm(jnp.concatenate(d_scores, axis=1), both_query, NN)
                if block == blocks - 1:
                    dv[a:b, :] = add_v
                    dk[a:b, :] = add_k
                else:
                    dv[a:b, :] += add_v
                    dk[a:b, :] += add_k
            both = jnp.concatenate([d_query[0][:HD, :], d_query[1][HD:, :]], axis=0) * 0.125
            out_ref[pl.ds(row_of(t, block * QB, half), QB), :] = both.T.astype(BF)
        for block in range(blocks):
            rows = slice(block * QB, (block + 1) * QB)
            place = row_of(t, block * QB, half)
            dkb[pl.ds(place, QB), :] = dk[rows, :].astype(BF)
            dvb[pl.ds(place, QB), :] = dv[rows, :].astype(BF)

    @pl.when(step == 1)
    def _():
        out_ref[...] = dkb[...]

    @pl.when(step == 2)
    def _():
        out_ref[...] = dvb[...]


def self_backward(t, qkv, mixed, d_mixed, lse):
    length, width = qkv.shape
    pairs = width // (3 * PAIR)
    spec = lambda part: pl.BlockSpec((length, PAIR), lambda j, s, r: (0, part * pairs + j))
    return pl.pallas_call(
        self_back_kernel,
        out_shape=jax.ShapeDtypeStruct((length, width), BF),
        grid_spec=pltpu.PrefetchScalarGridSpec(
            num_scalar_prefetch=1,
            grid=(pairs, 3),
            in_specs=[
                spec(0),
                spec(1),
                spec(2),
                pl.BlockSpec((length, PAIR), lambda j, s, r: (0, j)),
                pl.BlockSpec((length, PAIR), lambda j, s, r: (0, j)),
                pl.BlockSpec((1, 8, length), lambda j, s, r: (j, 0, 0)),
            ],
            out_specs=pl.BlockSpec((length, PAIR), lambda j, s, r: (0, s * pairs + j)),
            scratch_shapes=[pltpu.VMEM((length, PAIR), BF)] * 5
            + [pltpu.VMEM((length, PAIR), F32)] * 2
            + [pltpu.VMEM((length, PAIR), BF)] * 2,
        ),
        name="self_attend_back",
        cost_estimate=pl.CostEstimate(
            flops=40 * length * length * PAIR * pairs // 3,
            transcendentals=length * length * pairs,
            bytes_accessed=16 * length * PAIR * pairs,
        ),
    )(t, qkv, qkv, qkv, mixed, d_mixed, lse)


def spread_heads(value):
    count = QUAD // HD
    return jnp.concatenate([only(value, lanes_of(QUAD, head)) for head in range(count)], axis=0)


def cross_kernel(q_ref, k_ref, v_ref, o_ref, lse_ref):
    keys = k_ref.shape[0]
    scores = mm(spread_heads(k_ref[...] * BF(0.125)), q_ref[...], NT)
    powers, totals = [], []
    for head in range(QUAD // HD):
        score = scores[head * keys : (head + 1) * keys, :]
        top = jnp.max(score, axis=0, keepdims=True)
        power = jnp.exp(score - top)
        total = jnp.sum(power, axis=0, keepdims=True)
        lse_ref[0, head : head + 1, :] = top + jnp.log(total)
        powers.append(power.astype(BF))
        totals.append(total)
    mixed = mm(spread_heads(v_ref[...]), jnp.concatenate(powers, axis=0), TN)
    scaled = [
        mixed[head * HD : (head + 1) * HD, :] / totals[head] for head in range(QUAD // HD)
    ]
    o_ref[...] = jnp.concatenate(scaled, axis=0).T.astype(BF)


def cross_specs(rows, keys, quads):
    return [
        pl.BlockSpec((rows, QUAD), lambda j: (0, j)),
        pl.BlockSpec((keys, QUAD), lambda j: (0, j)),
        pl.BlockSpec((keys, QUAD), lambda j: (0, j)),
    ]


def cross_forward(query, key, value):
    rows, width = query.shape
    keys = key.shape[0]
    quads = width // QUAD
    return pl.pallas_call(
        cross_kernel,
        grid=(quads,),
        out_shape=(
            jax.ShapeDtypeStruct((rows, width), BF),
            jax.ShapeDtypeStruct((quads, 8, rows), F32),
        ),
        in_specs=cross_specs(rows, keys, quads),
        out_specs=[
            pl.BlockSpec((rows, QUAD), lambda j: (0, j)),
            pl.BlockSpec((1, 8, rows), lambda j: (j, 0, 0)),
        ],
        name="cross_attend",
        cost_estimate=pl.CostEstimate(
            flops=4 * rows * QUAD * width, transcendentals=rows * width, bytes_accessed=4 * rows * width
        ),
    )(query, key, value)


def cross_back_kernel(q_ref, k_ref, v_ref, o_ref, do_ref, lse_ref, dq_ref, dk_ref, dv_ref):
    keys = k_ref.shape[0]
    count = QUAD // HD
    query, grad = q_ref[...], do_ref[...]
    key = spread_heads(k_ref[...] * BF(0.125))
    scores = mm(key, query, NT)
    d_powers = mm(spread_heads(v_ref[...]), grad, NT)
    product = (grad.astype(F32) * o_ref[...].astype(F32)).T
    weights, d_scores = [], []
    for head in range(count):
        group = slice(head * keys, (head + 1) * keys)
        drop = jnp.sum(product[head * HD : (head + 1) * HD, :], axis=0, keepdims=True)
        power = jnp.exp(scores[group, :] - lse_ref[0, head : head + 1, :])
        weights.append(power.astype(BF))
        d_scores.append((power * (d_powers[group, :] - drop)).astype(BF))
    weights = jnp.concatenate(weights, axis=0)
    d_scores = jnp.concatenate(d_scores, axis=0)
    dq_ref[...] = mm(key, d_scores, TN).T.astype(BF)
    d_key = mm(d_scores, query, NN)
    d_value = mm(weights, grad, NN)
    for ref, found, scale in ((dk_ref, d_key, 0.125), (dv_ref, d_value, 1.0)):
        total = None
        for head in range(count):
            term = only(found[head * keys : (head + 1) * keys, :], lanes_of(QUAD, head))
            total = term if total is None else total + term
        ref[...] = total * scale


def cross_backward(query, key, value, mixed, d_mixed, lse):
    rows, width = query.shape
    keys = key.shape[0]
    quads = width // QUAD
    wide = pl.BlockSpec((rows, QUAD), lambda j: (0, j))
    return pl.pallas_call(
        cross_back_kernel,
        grid=(quads,),
        out_shape=(
            jax.ShapeDtypeStruct((rows, width), BF),
            jax.ShapeDtypeStruct((keys, width), F32),
            jax.ShapeDtypeStruct((keys, width), F32),
        ),
        in_specs=cross_specs(rows, keys, quads)
        + [wide, wide, pl.BlockSpec((1, 8, rows), lambda j: (j, 0, 0))],
        out_specs=[
            wide,
            pl.BlockSpec((keys, QUAD), lambda j: (0, j)),
            pl.BlockSpec((keys, QUAD), lambda j: (0, j)),
        ],
        name="cross_attend_back",
        cost_estimate=pl.CostEstimate(
            flops=10 * rows * QUAD * width, transcendentals=rows * width, bytes_accessed=8 * rows * width
        ),
    )(query, key, value, mixed, d_mixed, lse)


FF_STEP = 1024
FF_PART = 256


def ffn_kernel(n_ref, g_ref, wi_ref, wo_ref, *refs):
    act_ref, din_ref = refs[-2:]
    for part in range(wi_ref.shape[1] // FF_PART):
        cols = slice(part * FF_PART, (part + 1) * FF_PART)
        inner = mm(n_ref[...], wi_ref[:, cols], NN)
        d_act = mm(g_ref[...], wo_ref[:, cols], NN)
        phi = 0.5 + 0.5 * lax.erf(inner * (1.0 / math.sqrt(2.0)))
        bell = jnp.exp(inner * inner * -0.5) * (1.0 / math.sqrt(2.0 * math.pi))
        act_ref[:, cols] = (inner * phi).astype(BF)
        din_ref[:, cols] = (d_act * (phi + inner * bell)).astype(BF)


def ffn_middle(normed, grads, weights, block, blocks, kept=()):
    rows, width = normed.shape
    hidden = weights.shape[1] // 2
    steps = hidden // FF_STEP
    out_shape = jax.ShapeDtypeStruct((rows * blocks, hidden), BF)
    whole = pl.BlockSpec((rows, width), lambda j: (0, 0))
    out_spec = pl.BlockSpec((rows, FF_STEP), lambda j: (block, j))
    return pl.pallas_call(
        ffn_kernel,
        grid=(steps,),
        out_shape=(out_shape, out_shape),
        in_specs=[
            whole,
            whole,
            pl.BlockSpec((width, FF_STEP), lambda j: (0, j)),
            pl.BlockSpec((width, FF_STEP), lambda j: (0, steps + j)),
        ]
        + [pl.BlockSpec(memory_space=pl.ANY)] * len(kept),
        out_specs=[out_spec, out_spec],
        input_output_aliases={4 + i: i for i in range(len(kept))},
        name="ffn_middle",
        cost_estimate=pl.CostEstimate(
            flops=4 * rows * width * hidden,
            transcendentals=2 * rows * hidden,
            bytes_accessed=4 * width * hidden + 4 * rows * hidden,
        ),
    )(normed, grads, weights, weights, *kept)


def stats_of(value):
    mean = jnp.mean(value, axis=-1, keepdims=True)
    centred = value - mean
    spread = jnp.mean(centred * centred, axis=-1, keepdims=True)
    return centred, lax.rsqrt(spread + EPS)


def norm_grad(value, gain, incoming):
    centred, scale = stats_of(value)
    hat = centred * scale
    scaled = incoming * gain
    mean = jnp.mean(scaled, axis=-1, keepdims=True)
    along = jnp.mean(scaled * hat, axis=-1, keepdims=True)
    return (
        scale * (scaled - mean - hat * along),
        jnp.sum(incoming * hat, axis=0),
        jnp.sum(incoming, axis=0),
    )


def on_pair(
    inputs,
    text_states,
    self_query,
    self_key,
    self_value,
    self_output,
    cross_query,
    cross_key,
    cross_value,
    cross_output,
    inner_weight,
    outer_weight,
    norm_gains,
    norm_shifts,
    cotangent,
    *,
    groups,
):
    rows, width = inputs.shape
    half = width // 2
    hidden = inner_weight.shape[1]
    shard = self_query.shape[0]
    tensor = lax.axis_index("tensor")
    place = lax.axis_index("dp")
    core, column = place % 2, (place // 2) % 2
    core_swap = [(i, i ^ 1) for i in range(groups)]
    column_swap = [(i, i ^ 2) for i in range(groups)]
    lines = [[i + 4 * j for j in range(groups // 4)] for i in range(4)]
    t_ref = tensor.astype(jnp.int32).reshape(1)

    def peer(value):
        return lax.ppermute(value, "tensor", [(0, 1), (1, 0)])

    def gather(parts):
        return lax.all_gather(jnp.concatenate(parts, axis=1), "dp", axis=0, tiled=True)

    def halved(value, bit, swap):
        send = lax.dynamic_index_in_dim(value, 1 - bit, 1, False)
        keep = lax.dynamic_index_in_dim(value, bit, 1, False)
        got = lax.ppermute(send, "dp", swap)
        return (keep.astype(F32) + got.astype(F32)).astype(BF)

    def core_sum(grad):
        cut = grad.reshape(groups // 2, 2, shard, grad.shape[1])
        return halved(cut, core, core_swap)

    def column_sum(grad):
        cut = grad.reshape(groups // 4, 2, shard, grad.shape[-1])
        return halved(cut, column, column_swap)

    def line_sum(parts):
        whole = jnp.concatenate(parts, axis=-1) if len(parts) > 1 else parts[0]
        whole = whole.reshape(-1, whole.shape[-1])
        return lax.psum_scatter(
            whole, "dp", scatter_dimension=0, tiled=True, axis_index_groups=lines
        ).astype(F32)

    def pair_sum(grad):
        got = peer(grad[..., half:])
        return (grad[..., :half].astype(F32) + got.astype(F32)).astype(BF)

    inputs_peer = peer(inputs)
    cross_two = jnp.concatenate([cross_query, cross_output.T], axis=1)
    cross_peer = peer(cross_two)
    grads_peer = peer(cotangent)

    first = gather([self_query, self_key, self_value, self_output.T, cross_key, cross_value])
    second = gather(
        [cross_query, cross_peer[:, :half], cross_two[:, half:], cross_peer[:, half:]]
    )
    third = gather([inner_weight, outer_weight.T])
    w_qkv = first[:, : 3 * half]
    w_self_out = first[:, 3 * half : 4 * half]
    w_text = first[:, 4 * half :]
    w_cross_query = second[:, :width]
    w_cross_out = second[:, width:]
    w_inner = third[:, :hidden]
    w_outer = third[:, hidden:]

    start = jnp.concatenate([inputs, inputs_peer], axis=0).astype(F32)
    normed1 = norm_rows(start, norm_gains[0], norm_shifts[0]).astype(BF)
    qkv = mm(normed1, w_qkv, NN).astype(BF)
    text = text_states.reshape(-1, width)
    text_own = mm(text, w_text, NN).astype(BF)
    text_peer = peer(text_own)
    key2 = jnp.concatenate([text_own[:, :half], text_peer[:, :half]], axis=1)
    value2 = jnp.concatenate([text_own[:, half:], text_peer[:, half:]], axis=1)
    mixed1, lse1 = self_forward(t_ref, qkv)
    away = peer(mm(mixed1[rows:], w_self_out, NT).astype(BF))
    home = mm(mixed1[:rows], w_self_out, NT)
    state1 = inputs.astype(F32) + home + away.astype(F32)

    normed2 = norm_rows(state1, norm_gains[1], norm_shifts[1]).astype(BF)
    query2 = mm(normed2, w_cross_query, NN).astype(BF)
    mixed2, lse2 = cross_forward(query2, key2, value2)
    state2 = state1 + mm(mixed2, w_cross_out, NT)

    normed3 = norm_rows(state2, norm_gains[2], norm_shifts[2]).astype(BF)
    normed3_peer = peer(normed3)
    active, d_inner = ffn_middle(normed3, cotangent, third, 0, 2)
    active, d_inner = ffn_middle(normed3_peer, grads_peer, third, 1, 2, (active, d_inner))
    back3_away = peer(mm(d_inner[rows:], w_inner, NT).astype(BF))
    grads3 = jnp.concatenate([cotangent, grads_peer], axis=0)
    d_outer = column_sum(core_sum(mm(grads3, active, TN).astype(BF)))
    outer_sum = line_sum([d_outer])
    rows3 = jnp.concatenate([normed3, normed3_peer], axis=0)
    d_innerw = column_sum(core_sum(mm(rows3, d_inner, TN).astype(BF)))
    inner_sum = line_sum([d_innerw])
    out_away = peer(mm(active[rows:], w_outer, NT).astype(BF))
    output = (state2 + mm(active[:rows], w_outer, NT) + out_away.astype(F32)).astype(BF)

    back3 = mm(d_inner[:rows], w_inner, NT) + back3_away.astype(F32)
    d_state2, gain3, shift3 = norm_grad(state2, norm_gains[2], back3)
    grad2 = cotangent.astype(F32) + d_state2
    g2 = grad2.astype(BF)
    d_mixed2 = mm(g2, w_cross_out, NN).astype(BF)
    d_query2, d_key2, d_value2 = cross_backward(query2, key2, value2, mixed2, d_mixed2, lse2)
    back2 = mm(d_query2, w_cross_query, NT)
    d_state1, gain2, shift2 = norm_grad(state1, norm_gains[1], back2)
    grad1 = grad2 + d_state1
    g1 = grad1.astype(BF)
    g1_peer = peer(g1)

    d_text_send = jnp.concatenate([d_key2[:, half:], d_value2[:, half:]], axis=1)
    d_text_keep = jnp.concatenate([d_key2[:, :half], d_value2[:, :half]], axis=1)
    d_text = (d_text_keep + peer(d_text_send.astype(BF)).astype(F32)).astype(BF)
    d_coutput = pair_sum(core_sum(mm(g2, mixed2, TN).astype(BF)))
    d_cquery = pair_sum(core_sum(mm(normed2, d_query2, TN).astype(BF)))
    d_ckv = core_sum(mm(text, d_text, TN).astype(BF))
    cross_sum = line_sum([column_sum(v) for v in (d_coutput, d_cquery, d_ckv)])
    text_terms = mm(d_text, w_text, NT).astype(BF)
    text_keep = lax.dynamic_slice_in_dim(text_terms, tensor * half, half, 1)
    text_send = lax.dynamic_slice_in_dim(text_terms, (1 - tensor) * half, half, 1)
    text_grad = (text_keep.astype(F32) + peer(text_send).astype(F32)).reshape(1, -1, half)

    grads1 = jnp.concatenate([g1, g1_peer], axis=0)
    d_mixed1 = mm(grads1, w_self_out, NN).astype(BF)
    d_soutput = column_sum(core_sum(mm(grads1, mixed1, TN).astype(BF)))
    so_sum = line_sum([d_soutput])
    d_qkv = self_backward(t_ref, qkv, mixed1, d_mixed1, lse1)
    qkv_sum = line_sum([column_sum(core_sum(mm(normed1, d_qkv, TN).astype(BF)))])
    back1_away = peer(mm(d_qkv[rows:], w_qkv, NT).astype(BF))
    back1 = mm(d_qkv[:rows], w_qkv, NT) + back1_away.astype(F32)
    d_start, gain1, shift1 = norm_grad(inputs.astype(F32), norm_gains[0], back1)
    input_grad = grad1 + d_start

    small = jnp.stack([gain1, gain2, gain3, shift1, shift2, shift3])
    small = small + peer(small)
    bit = 1
    while bit < groups:
        small = small + lax.ppermute(small, "dp", [(i, i ^ bit) for i in range(groups)])
        bit *= 2
    return (
        output,
        input_grad,
        text_grad,
        qkv_sum[:, :half],
        qkv_sum[:, half : 2 * half],
        qkv_sum[:, 2 * half :],
        so_sum.T,
        cross_sum[:, half : 2 * half],
        cross_sum[:, 2 * half : 3 * half],
        cross_sum[:, 3 * half :],
        cross_sum[:, :half].T,
        inner_sum,
        outer_sum.T,
        small[:3],
        small[3:],
    )


def pairs_up(mesh, inputs, text_states, inner_weight):
    groups, sides = mesh.shape["dp"], mesh.shape["tensor"]
    width = inputs.shape[1]
    return (
        sides == 2
        and groups >= 4
        and groups & (groups - 1) == 0
        and text_states.shape[0] == groups
        and text_states.shape[1] == TEXT
        and inputs.shape[0] == groups * LEN
        and width % (2 * QUAD) == 0
        and width % (32 * groups) in (0, 16 * groups)
        and inner_weight.shape[1] % (2 * FF_STEP) == 0
    )


def solution(mesh):
    in_specs = (
        P(("dp", "tensor"), None),
        P("dp", None, None),
        P("dp", "tensor"),
        P("dp", "tensor"),
        P("dp", "tensor"),
        P("tensor", "dp"),
        P("dp", "tensor"),
        P("dp", "tensor"),
        P("dp", "tensor"),
        P("tensor", "dp"),
        P("dp", "tensor"),
        P("tensor", "dp"),
        P(),
        P(),
        P(("dp", "tensor"), None),
    )
    out_specs = (
        P(("dp", "tensor"), None),
        P(("dp", "tensor"), None),
        P("dp", None, "tensor"),
        P("dp", "tensor"),
        P("dp", "tensor"),
        P("dp", "tensor"),
        P("tensor", "dp"),
        P("dp", "tensor"),
        P("dp", "tensor"),
        P("dp", "tensor"),
        P("tensor", "dp"),
        P("dp", "tensor"),
        P("tensor", "dp"),
        P(),
        P(),
    )

    def layer(*args):
        body = on_device
        if pairs_up(mesh, args[0], args[1], args[10]):
            body = partial(on_pair, groups=mesh.shape["dp"])
        return jax.shard_map(
            body, mesh=mesh, in_specs=in_specs, out_specs=out_specs, check_vma=False
        )(*args)

    return layer
```

```python
from functools import partial
import math

import jax
import jax.numpy as jnp
from jax import lax
from jax.experimental import pallas as pl
from jax.experimental.pallas import tpu as pltpu
from jax.sharding import PartitionSpec as P

HD = 64
TEXT = 64
LEN = 1024


EPS = 1e-05
MASKED = -1e30


def norm_rows(value, gain, shift):
    mean = jnp.mean(value, axis=-1, keepdims=True)
    centred = value - mean
    spread = jnp.mean(centred * centred, axis=-1, keepdims=True)
    return centred * lax.rsqrt(spread + EPS) * gain + shift


def norm_back(value, gain, shift, incoming):
    ignored, pullback = jax.vjp(norm_rows, value, gain, shift)
    return pullback(incoming)


def gelu_exact(value):
    return jax.nn.gelu(value, approximate=False)


def transposed_times(left, right):
    return lax.dot_general(
        left, right, (((0,), (0,)), ((), ())), preferred_element_type=jnp.float32
    )


def times_t(left, right):
    return lax.dot_general(
        left, right, (((1,), (1,)), ((), ())), preferred_element_type=jnp.float32
    )


def apply_projection(left, right):
    return jnp.dot(left, right, preferred_element_type=jnp.float32).astype(jnp.bfloat16)


def scores_of(query, key, masked):
    scale = 1.0 / math.sqrt(HD)
    scores = jnp.einsum("qhd,khd->hqk", query, key, preferred_element_type=jnp.float32) * scale
    if masked:
        places = jnp.arange(query.shape[0])
        allowed = places[:, None] >= places[None, :]
        scores = jnp.where(allowed[None], scores, MASKED)
    return scores


def attend(block, masked):
    query, key, value = block
    scores = scores_of(query, key, masked)
    highest = jnp.max(scores, axis=-1, keepdims=True)
    total = jnp.sum(jnp.exp(scores - highest), axis=-1, keepdims=True)
    log_total = highest + jnp.log(total)
    weights = jnp.exp(scores - log_total).astype(jnp.bfloat16)
    mixed = jnp.einsum("hqk,khd->qhd", weights, value, preferred_element_type=jnp.float32)
    return (mixed.astype(jnp.bfloat16), log_total)


def attend_back(block, masked):
    query, key, value, log_total, grad_mixed = block
    scale = 1.0 / math.sqrt(HD)
    weights = jnp.exp(scores_of(query, key, masked) - log_total)
    rounded = weights.astype(jnp.bfloat16)
    d_value = jnp.einsum("hqk,qhd->khd", rounded, grad_mixed, preferred_element_type=jnp.float32)
    d_weights = jnp.einsum("qhd,khd->hqk", grad_mixed, value, preferred_element_type=jnp.float32)
    centred = d_weights - jnp.sum(weights * d_weights, axis=-1, keepdims=True)
    d_scores = (weights * centred).astype(jnp.bfloat16)
    d_query = jnp.einsum("hqk,khd->qhd", d_scores, key, preferred_element_type=jnp.float32) * scale
    d_key = jnp.einsum("hqk,qhd->khd", d_scores, query, preferred_element_type=jnp.float32) * scale
    return (d_query.astype(jnp.bfloat16), d_key.astype(jnp.bfloat16), d_value.astype(jnp.bfloat16))


def spread_rows(normed):
    return lax.all_gather(normed, "tensor", axis=0, tiled=True)


def spread_grads(grad):
    return lax.all_gather(grad.astype(jnp.bfloat16), "tensor", axis=0, tiled=True)


def branch_total(mixed, weight):
    return lax.psum_scatter(
        jnp.dot(mixed, weight, preferred_element_type=jnp.float32),
        "tensor",
        scatter_dimension=0,
        tiled=True,
    )


def normalized_total(pairs):
    total = None
    for grad, weight in pairs:
        added = times_t(grad, weight)
        total = added if total is None else total + added
    return lax.psum_scatter(total, "tensor", scatter_dimension=0, tiled=True)


def on_device(
    inputs,
    text_states,
    self_query,
    self_key,
    self_value,
    self_output,
    cross_query,
    cross_key,
    cross_value,
    cross_output,
    inner_weight,
    outer_weight,
    norm_gains,
    norm_shifts,
    cotangent,
):
    (
        gathered_self_query,
        gathered_self_key,
        gathered_self_value,
        full_soutput,
        full_cquery,
        full_ckey,
        full_cvalue,
        full_coutput,
        full_inner,
        full_outer,
    ) = (
        lax.all_gather(self_query, "dp", axis=0, tiled=True),
        lax.all_gather(self_key, "dp", axis=0, tiled=True),
        lax.all_gather(self_value, "dp", axis=0, tiled=True),
        lax.all_gather(self_output, "dp", axis=1, tiled=True),
        lax.all_gather(cross_query, "dp", axis=0, tiled=True),
        lax.all_gather(cross_key, "dp", axis=0, tiled=True),
        lax.all_gather(cross_value, "dp", axis=0, tiled=True),
        lax.all_gather(cross_output, "dp", axis=1, tiled=True),
        lax.all_gather(inner_weight, "dp", axis=0, tiled=True),
        lax.all_gather(outer_weight, "dp", axis=1, tiled=True),
    )
    width = inputs.shape[1]
    clips = text_states.shape[0]
    local_heads = gathered_self_query.shape[1] // HD

    def heads(value, length):
        return value.reshape(clips, length, local_heads, HD)

    def flatten(value):
        return value.reshape(-1, local_heads * HD)

    start = inputs.astype(jnp.float32)
    first_rows = spread_rows(norm_rows(start, norm_gains[0], norm_shifts[0]).astype(jnp.bfloat16))
    query1 = apply_projection(first_rows, gathered_self_query)
    first_key = apply_projection(first_rows, gathered_self_key)
    value1 = apply_projection(first_rows, gathered_self_value)
    mixed1, lse1 = lax.map(
        partial(attend, masked=True),
        (heads(query1, LEN), heads(first_key, LEN), heads(value1, LEN)),
    )
    mixed1 = flatten(mixed1)
    state1 = start + branch_total(mixed1, full_soutput)
    rows2 = spread_rows(norm_rows(state1, norm_gains[1], norm_shifts[1]).astype(jnp.bfloat16))
    query2 = apply_projection(rows2, full_cquery)
    text_flat = text_states.reshape(-1, width)
    key2 = apply_projection(text_flat, full_ckey)
    value2 = apply_projection(text_flat, full_cvalue)
    mixed2, lse2 = lax.map(
        partial(attend, masked=False), (heads(query2, LEN), heads(key2, TEXT), heads(value2, TEXT))
    )
    mixed2 = flatten(mixed2)
    state2 = state1 + branch_total(mixed2, full_coutput)
    rows3 = spread_rows(norm_rows(state2, norm_gains[2], norm_shifts[2]).astype(jnp.bfloat16))
    inner = jnp.dot(rows3, full_inner, preferred_element_type=jnp.float32)
    active_float, gelu_pull = jax.vjp(gelu_exact, inner)
    active = active_float.astype(jnp.bfloat16)
    result = state2 + branch_total(active, full_outer)
    output = result.astype(jnp.bfloat16)
    grad3 = cotangent.astype(jnp.float32)
    grads_outer = spread_grads(grad3)
    d_outer = transposed_times(active, grads_outer)
    d_inner = gelu_pull(times_t(grads_outer, full_outer))[0].astype(jnp.bfloat16)
    d_innerw = transposed_times(rows3, d_inner)
    back3 = normalized_total(((d_inner, full_inner),))
    d_state2, gain_three, shift_three = norm_back(state2, norm_gains[2], norm_shifts[2], back3)
    grad2 = grad3 + d_state2
    grads_cross = spread_grads(grad2)
    d_coutput = transposed_times(mixed2, grads_cross)
    d_mixed2 = times_t(grads_cross, full_coutput).astype(jnp.bfloat16)
    d_query2, d_key2, d_value2 = lax.map(
        partial(attend_back, masked=False),
        (heads(query2, LEN), heads(key2, TEXT), heads(value2, TEXT), lse2, heads(d_mixed2, LEN)),
    )
    d_query2 = flatten(d_query2)
    d_key2 = flatten(d_key2)
    d_value2 = flatten(d_value2)
    d_cquery = transposed_times(rows2, d_query2)
    d_ckey = transposed_times(text_flat, d_key2)
    d_cvalue = transposed_times(text_flat, d_value2)
    text_terms = (times_t(d_key2, full_ckey) + times_t(d_value2, full_cvalue)).reshape(
        clips, TEXT, width
    )
    text_grad = lax.psum_scatter(
        text_terms.astype(jnp.bfloat16), "tensor", scatter_dimension=2, tiled=True
    ).astype(jnp.float32)
    back2 = normalized_total(((d_query2, full_cquery),))
    d_state1, gain_two, shift_two = norm_back(state1, norm_gains[1], norm_shifts[1], back2)
    grad1 = grad2 + d_state1
    grads_self = spread_grads(grad1)
    d_soutput = transposed_times(mixed1, grads_self)
    d_mixed1 = times_t(grads_self, full_soutput).astype(jnp.bfloat16)
    first_query_grad, first_key_grad, first_value_grad = lax.map(
        partial(attend_back, masked=True),
        (heads(query1, LEN), heads(first_key, LEN), heads(value1, LEN), lse1, heads(d_mixed1, LEN)),
    )
    first_query_grad = flatten(first_query_grad)
    first_key_grad = flatten(first_key_grad)
    first_value_grad = flatten(first_value_grad)
    d_squery = transposed_times(first_rows, first_query_grad)
    self_key_partial = transposed_times(first_rows, first_key_grad)
    d_svalue = transposed_times(first_rows, first_value_grad)
    first_backward = normalized_total(
        (
            (first_query_grad, gathered_self_query),
            (first_key_grad, gathered_self_key),
            (first_value_grad, gathered_self_value),
        )
    )
    d_start, gain_one, shift_one = norm_back(start, norm_gains[0], norm_shifts[0], first_backward)
    input_grad = grad1 + d_start
    gains_grad, shifts_grad = lax.psum(
        (
            jnp.stack([gain_one, gain_two, gain_three]),
            jnp.stack([shift_one, shift_two, shift_three]),
        ),
        ("dp", "tensor"),
    )
    summed = (
        lax.psum_scatter(
            d_squery.astype(jnp.bfloat16), "dp", scatter_dimension=0, tiled=True
        ).astype(jnp.float32),
        lax.psum_scatter(
            self_key_partial.astype(jnp.bfloat16), "dp", scatter_dimension=0, tiled=True
        ).astype(jnp.float32),
        lax.psum_scatter(
            d_svalue.astype(jnp.bfloat16), "dp", scatter_dimension=0, tiled=True
        ).astype(jnp.float32),
        lax.psum_scatter(
            d_soutput.astype(jnp.bfloat16), "dp", scatter_dimension=1, tiled=True
        ).astype(jnp.float32),
        lax.psum_scatter(
            d_cquery.astype(jnp.bfloat16), "dp", scatter_dimension=0, tiled=True
        ).astype(jnp.float32),
        lax.psum_scatter(d_ckey.astype(jnp.bfloat16), "dp", scatter_dimension=0, tiled=True).astype(
            jnp.float32
        ),
        lax.psum_scatter(
            d_cvalue.astype(jnp.bfloat16), "dp", scatter_dimension=0, tiled=True
        ).astype(jnp.float32),
        lax.psum_scatter(
            d_coutput.astype(jnp.bfloat16), "dp", scatter_dimension=1, tiled=True
        ).astype(jnp.float32),
        lax.psum_scatter(
            d_innerw.astype(jnp.bfloat16), "dp", scatter_dimension=0, tiled=True
        ).astype(jnp.float32),
        lax.psum_scatter(
            d_outer.astype(jnp.bfloat16), "dp", scatter_dimension=1, tiled=True
        ).astype(jnp.float32),
    )
    return (
        output,
        input_grad,
        text_grad,
        summed[0],
        summed[1],
        summed[2],
        summed[3],
        summed[4],
        summed[5],
        summed[6],
        summed[7],
        summed[8],
        summed[9],
        gains_grad,
        shifts_grad,
    )


BF = jnp.bfloat16
F32 = jnp.float32
NN = (((1,), (0,)), ((), ()))
NT = (((1,), (1,)), ((), ()))
TN = (((0,), (0,)), ((), ()))
QB = 256
PAIR = 128
QUAD = 256
CUTS = 2


def after(value, *ready):
    return lax.optimization_barrier((value,) + ready)[0]


def mm(left, right, dims):
    return lax.dot_general(left, right, dims, preferred_element_type=F32)


LIGHT = pl.CostEstimate(flops=1024, transcendentals=0, bytes_accessed=1024)
MIDDLE = pl.CostEstimate(flops=20_000_000_000, transcendentals=0, bytes_accessed=1024)
HEAVY = pl.CostEstimate(flops=10**15, transcendentals=0, bytes_accessed=1024)


def weight_kernel(side_ref, left_ref, right_ref, send_ref, keep_ref, *, shard):
    total = mm(left_ref[...], right_ref[...], TN).astype(BF)
    side = side_ref[0]
    for parity in range(2):
        even, odd = (keep_ref, send_ref) if parity == 0 else (send_ref, keep_ref)

        @pl.when(side == parity)
        def _():
            for at in range(total.shape[0] // shard):
                rows = total[at * shard : (at + 1) * shard, :]
                (odd if at % 2 else even)[at // 2] = rows


def weight_halves(side, left, right, shard, first=0, size=None):
    depth, width = left.shape
    size = size or right.shape[1]
    tile = next(t for t in (768, 1152, 512, 384, 256, 128) if size % t == 0 and first % t == 0)
    count = width // shard // 2
    shape = jax.ShapeDtypeStruct((count, shard, size), BF)
    out = pl.BlockSpec((count, shard, tile), lambda j, s: (0, 0, j))
    return pl.pallas_call(
        partial(weight_kernel, shard=shard),
        out_shape=(shape, shape),
        grid_spec=pltpu.PrefetchScalarGridSpec(
            num_scalar_prefetch=1,
            grid=(size // tile,),
            in_specs=[
                pl.BlockSpec((depth, width), lambda j, s: (0, 0)),
                pl.BlockSpec((depth, tile), lambda j, s: (0, first // tile + j)),
            ],
            out_specs=[out, out],
        ),
        name="weight_halves",
        cost_estimate=LIGHT,
    )(side, left, right)


def added(refs, at=slice(None)):
    total = refs[0][at].astype(F32)
    for ref in refs[1:]:
        total = total + ref[at].astype(F32)
    return total.astype(BF)


def fold_kernel(side_ref, *refs):
    side = side_ref[0]
    refs[-2][...] = added(refs[:-2], pl.ds(1 - side, 1))
    refs[-1][...] = added(refs[:-2], pl.ds(side, 1))


def fold(side, *terms):
    count, shard, size = terms[0].shape[0] // 2, terms[0].shape[1], terms[0].shape[2]
    shape = jax.ShapeDtypeStruct((count, shard, size), BF)
    whole = pl.BlockSpec((2, shard, size), lambda j, s: (j, 0, 0))
    part = pl.BlockSpec((1, shard, size), lambda j, s: (j, 0, 0))
    return pl.pallas_call(
        fold_kernel,
        out_shape=(shape, shape),
        grid_spec=pltpu.PrefetchScalarGridSpec(
            num_scalar_prefetch=1,
            grid=(count,),
            in_specs=[whole] * len(terms),
            out_specs=[part, part],
        ),
        name="fold",
        cost_estimate=LIGHT,
    )(side, *terms)


def totals_kernel(*refs, counts):
    out_ref = refs[-1]
    first, at = 0, 0
    for count in counts:
        size = refs[at].shape[2]
        out_ref[:, :, first : first + size] = added(refs[at : at + count])
        first, at = first + size, at + count


def totals(groups):
    count, shard = groups[0][0].shape[:2]
    sizes = [terms[0].shape[2] for terms in groups]
    spec = lambda size: pl.BlockSpec((2, shard, size), lambda j: (j, 0, 0))
    return pl.pallas_call(
        partial(totals_kernel, counts=[len(terms) for terms in groups]),
        grid=(count // 2,),
        out_shape=jax.ShapeDtypeStruct((count, shard, sum(sizes)), BF),
        in_specs=[spec(size) for size, terms in zip(sizes, groups) for _ in terms],
        out_specs=spec(sum(sizes)),
        name="totals",
        cost_estimate=LIGHT,
    )(*[v for terms in groups for v in terms])


def norm_sums_kernel(value_ref, *refs):
    sums_ref = refs[-1]
    incoming = refs[0][...]
    for ref in refs[1:-1]:
        incoming = incoming + ref[...]
    centred, scale = stats_of(value_ref[...].astype(F32))

    @pl.when(pl.program_id(0) == 0)
    def _():
        sums_ref[...] = jnp.zeros_like(sums_ref)

    sums_ref[0:1, :] += jnp.sum(incoming * (centred * scale), axis=0, keepdims=True)
    sums_ref[1:2, :] += jnp.sum(incoming, axis=0, keepdims=True)


def norm_sums(value, incoming):
    rows, width = value.shape
    tile = 128
    spec = pl.BlockSpec((tile, width), lambda j: (j, 0))
    return pl.pallas_call(
        norm_sums_kernel,
        grid=(rows // tile,),
        out_shape=jax.ShapeDtypeStruct((8, width), F32),
        in_specs=[spec] * (1 + len(incoming)),
        out_specs=pl.BlockSpec((8, width), lambda j: (0, 0)),
        name="norm_sums",
        cost_estimate=LIGHT,
    )(value, *incoming)


def norm_back_kernel(value_ref, gain_ref, base_ref, *refs, parts):
    grad_ref, low_ref, sums_ref = refs[parts:]
    incoming = refs[0][...].astype(F32)
    for ref in refs[1:parts]:
        incoming = incoming + ref[...].astype(F32)
    centred, scale = stats_of(value_ref[...].astype(F32))
    hat = centred * scale
    scaled = incoming * gain_ref[...]
    mean = jnp.mean(scaled, axis=-1, keepdims=True)
    along = jnp.mean(scaled * hat, axis=-1, keepdims=True)
    grad = base_ref[...].astype(F32) + scale * (scaled - mean - hat * along)
    grad_ref[...] = grad
    low_ref[...] = grad.astype(BF)

    @pl.when(pl.program_id(0) == 0)
    def _():
        sums_ref[...] = jnp.zeros_like(sums_ref)

    sums_ref[0:1, :] += jnp.sum(incoming * hat, axis=0, keepdims=True)
    sums_ref[1:2, :] += jnp.sum(incoming, axis=0, keepdims=True)


def norm_back_rows(value, gain, base, incoming, cost=LIGHT):
    rows, width = value.shape
    tile = 128
    spec = pl.BlockSpec((tile, width), lambda j: (j, 0))
    return pl.pallas_call(
        partial(norm_back_kernel, parts=len(incoming)),
        grid=(rows // tile,),
        out_shape=(
            jax.ShapeDtypeStruct((rows, width), F32),
            jax.ShapeDtypeStruct((rows, width), BF),
            jax.ShapeDtypeStruct((8, width), F32),
        ),
        in_specs=[spec, pl.BlockSpec((1, width), lambda j: (0, 0)), spec] + [spec] * len(incoming),
        out_specs=[spec, spec, pl.BlockSpec((8, width), lambda j: (0, 0))],
        name="norm_back",
        cost_estimate=cost,
    )(value, gain.reshape(1, width), base, *incoming)


def product_kernel(left_ref, right_ref, out_ref, *, dims):
    out_ref[...] = mm(left_ref[...], right_ref[...], dims).astype(out_ref.dtype)


def product(left, right, dims, dtype, row=0, rows=None, first=0, size=None, cost=LIGHT):
    rows = rows or left.shape[0]
    depth = left.shape[1]
    if dims is NN:
        size = size or right.shape[1]
        tile = next(t for t in (768, 512, 384, 256) if size % t == 0 and first % t == 0)
        right_spec = pl.BlockSpec((depth, tile), lambda j: (0, first // tile + j))
    else:
        size = right.shape[0]
        tile = 512
        right_spec = pl.BlockSpec((tile, depth), lambda j: (j, first // depth))
    return pl.pallas_call(
        partial(product_kernel, dims=dims),
        grid=(size // tile,),
        out_shape=jax.ShapeDtypeStruct((rows, size), dtype),
        in_specs=[pl.BlockSpec((rows, depth), lambda j: (row, 0)), right_spec],
        out_specs=pl.BlockSpec((rows, tile), lambda j: (0, j)),
        name="product",
        cost_estimate=cost,
    )(left, right)


def lanes_of(width, head):
    lane = lax.broadcasted_iota(jnp.int32, (1, width), 1)
    return (lane >= head * HD) & (lane < (head + 1) * HD)


def only(value, mask):
    return jnp.where(mask, value, jnp.zeros_like(value))


def pieces_of(block):
    start = block * QB
    found = [(0, start, False)] if block else []
    return found + [(start, start + QB, True)]


def causal():
    key = lax.broadcasted_iota(jnp.int32, (QB, QB), 0)
    place = lax.broadcasted_iota(jnp.int32, (QB, QB), 1)
    return key <= place


def to_places(t, ref, held, half):
    low = pl.multiple_of(t * half, half)
    high = pl.multiple_of((1 - t) * half, half)
    held[0:half, :] = ref[pl.ds(low, half), :]
    held[half : 2 * half, :] = ref[pl.ds(high, half), :]


def row_of(t, start, half):
    side = start // half
    base = (1 - t) * half if side else t * half
    return pl.multiple_of(base + start % half, QB)


def self_kernel(t_ref, q_ref, k_ref, v_ref, o_ref, lse_ref, qs, ks, vs):
    t = t_ref[0]
    length = q_ref.shape[0]
    half = length // 2
    for ref, held in ((q_ref, qs), (k_ref, ks), (v_ref, vs)):
        to_places(t, ref, held, half)
    allowed = causal()
    for block in range(length // QB):
        rows = slice(block * QB, (block + 1) * QB)
        query = qs[rows, :] * BF(0.125)
        mixed = []
        for head in range(2):
            mine = only(query, lanes_of(PAIR, head))
            parts = []
            for a, b, edge in pieces_of(block):
                score = mm(ks[a:b, :], mine, NT)
                parts.append(jnp.where(allowed, score, MASKED) if edge else score)
            top = jnp.max(parts[0], axis=0, keepdims=True)
            for part in parts[1:]:
                top = jnp.maximum(top, jnp.max(part, axis=0, keepdims=True))
            total, out = None, None
            for part, (a, b, edge) in zip(parts, pieces_of(block)):
                power = jnp.exp(part - top)
                added = jnp.sum(power, axis=0, keepdims=True)
                term = mm(vs[a:b, :], power.astype(BF), TN)
                total = added if total is None else total + added
                out = term if out is None else out + term
            lse_ref[0, head : head + 1, rows] = top + jnp.log(total)
            mixed.append(out[head * HD : (head + 1) * HD, :] / total)
        both = jnp.concatenate(mixed, axis=0)
        o_ref[pl.ds(row_of(t, block * QB, half), QB), :] = both.T.astype(BF)


def self_forward(t, qkv):
    length, width = qkv.shape
    pairs = width // (3 * PAIR)
    cut = pairs // CUTS
    spec = lambda part: pl.BlockSpec(
        (length, PAIR), lambda j, r: (0, (3 * (j // cut) + part) * cut + j % cut)
    )
    return pl.pallas_call(
        self_kernel,
        out_shape=(
            jax.ShapeDtypeStruct((length, pairs * PAIR), BF),
            jax.ShapeDtypeStruct((pairs, 8, length), F32),
        ),
        grid_spec=pltpu.PrefetchScalarGridSpec(
            num_scalar_prefetch=1,
            grid=(pairs,),
            in_specs=[spec(0), spec(1), spec(2)],
            out_specs=[
                pl.BlockSpec((length, PAIR), lambda j, s: (0, j)),
                pl.BlockSpec((1, 8, length), lambda j, s: (j, 0, 0)),
            ],
            scratch_shapes=[pltpu.VMEM((length, PAIR), BF)] * 3,
        ),
        name="self_attend",
        cost_estimate=LIGHT,
    )(t, qkv, qkv, qkv)


def self_back_kernel(
    t_ref, q_ref, k_ref, v_ref, o_ref, do_ref, lse_ref, out_ref, qs, ks, vs, os, dos, dk, dv, dkb, dvb
):
    t = t_ref[0]
    length = q_ref.shape[0]
    half = length // 2
    step = pl.program_id(1)

    @pl.when(step == 0)
    def _():
        for ref, held in ((q_ref, qs), (k_ref, ks), (v_ref, vs), (o_ref, os), (do_ref, dos)):
            to_places(t, ref, held, half)
        allowed = causal()
        blocks = length // QB
        for block in reversed(range(blocks)):
            rows = slice(block * QB, (block + 1) * QB)
            query = qs[rows, :] * BF(0.125)
            grad = dos[rows, :]
            product = (grad.astype(F32) * os[rows, :].astype(F32)).T
            mine = [only(query, lanes_of(PAIR, head)) for head in range(2)]
            mine_grad = [only(grad, lanes_of(PAIR, head)) for head in range(2)]
            both_query = jnp.concatenate(mine, axis=0)
            both_grad = jnp.concatenate(mine_grad, axis=0)
            d_query = [None, None]
            for a, b, edge in pieces_of(block):
                weights, d_scores = [], []
                for head in range(2):
                    drop = jnp.sum(product[head * HD : (head + 1) * HD, :], axis=0, keepdims=True)
                    score = mm(ks[a:b, :], mine[head], NT)
                    power = jnp.exp(score - lse_ref[0, head : head + 1, rows])
                    if edge:
                        power = jnp.where(allowed, power, 0.0)
                    d_power = mm(vs[a:b, :], mine_grad[head], NT)
                    d_score = (power * (d_power - drop)).astype(BF)
                    weights.append(power.astype(BF))
                    d_scores.append(d_score)
                    term = mm(ks[a:b, :], d_score, TN)
                    d_query[head] = term if d_query[head] is None else d_query[head] + term
                add_v = mm(jnp.concatenate(weights, axis=1), both_grad, NN)
                add_k = mm(jnp.concatenate(d_scores, axis=1), both_query, NN)
                if block == blocks - 1:
                    dv[a:b, :] = add_v
                    dk[a:b, :] = add_k
                else:
                    dv[a:b, :] += add_v
                    dk[a:b, :] += add_k
            both = jnp.concatenate([d_query[0][:HD, :], d_query[1][HD:, :]], axis=0) * 0.125
            out_ref[pl.ds(row_of(t, block * QB, half), QB), :] = both.T.astype(BF)
        for block in range(blocks):
            rows = slice(block * QB, (block + 1) * QB)
            place = row_of(t, block * QB, half)
            dkb[pl.ds(place, QB), :] = dk[rows, :].astype(BF)
            dvb[pl.ds(place, QB), :] = dv[rows, :].astype(BF)

    @pl.when(step == 1)
    def _():
        out_ref[...] = dkb[...]

    @pl.when(step == 2)
    def _():
        out_ref[...] = dvb[...]


def self_backward(t, qkv, mixed, d_mixed, lse, part):
    length, width = qkv.shape[0], qkv.shape[1] // CUTS
    pairs = width // (3 * PAIR)
    first = part * pairs
    spec = lambda kind: pl.BlockSpec(
        (length, PAIR), lambda j, s, r: (0, 3 * first + kind * pairs + j)
    )
    return pl.pallas_call(
        self_back_kernel,
        out_shape=jax.ShapeDtypeStruct((length, width), BF),
        grid_spec=pltpu.PrefetchScalarGridSpec(
            num_scalar_prefetch=1,
            grid=(pairs, 3),
            in_specs=[
                spec(0),
                spec(1),
                spec(2),
                pl.BlockSpec((length, PAIR), lambda j, s, r: (0, first + j)),
                pl.BlockSpec((length, PAIR), lambda j, s, r: (0, first + j)),
                pl.BlockSpec((1, 8, length), lambda j, s, r: (first + j, 0, 0)),
            ],
            out_specs=pl.BlockSpec((length, PAIR), lambda j, s, r: (0, s * pairs + j)),
            scratch_shapes=[pltpu.VMEM((length, PAIR), BF)] * 5
            + [pltpu.VMEM((length, PAIR), F32)] * 2
            + [pltpu.VMEM((length, PAIR), BF)] * 2,
        ),
        name="self_attend_back",
        cost_estimate=MIDDLE,
    )(t, qkv, qkv, qkv, mixed, d_mixed, lse)


def spread_heads(value):
    count = QUAD // HD
    return jnp.concatenate([only(value, lanes_of(QUAD, head)) for head in range(count)], axis=0)


def cross_kernel(q_ref, k_ref, v_ref, o_ref, lse_ref):
    keys = k_ref.shape[0]
    scores = mm(spread_heads(k_ref[...] * BF(0.125)), q_ref[...], NT)
    powers, totals = [], []
    for head in range(QUAD // HD):
        score = scores[head * keys : (head + 1) * keys, :]
        top = jnp.max(score, axis=0, keepdims=True)
        power = jnp.exp(score - top)
        total = jnp.sum(power, axis=0, keepdims=True)
        lse_ref[0, head : head + 1, :] = top + jnp.log(total)
        powers.append(power.astype(BF))
        totals.append(total)
    mixed = mm(spread_heads(v_ref[...]), jnp.concatenate(powers, axis=0), TN)
    scaled = [
        mixed[head * HD : (head + 1) * HD, :] / totals[head] for head in range(QUAD // HD)
    ]
    o_ref[...] = jnp.concatenate(scaled, axis=0).T.astype(BF)


def cross_specs(rows, keys, quads):
    return [
        pl.BlockSpec((rows, QUAD), lambda j: (0, j)),
        pl.BlockSpec((keys, QUAD), lambda j: (0, j)),
        pl.BlockSpec((keys, QUAD), lambda j: (0, j)),
    ]


def cross_forward(query, key, value):
    rows, width = query.shape
    keys = key.shape[0]
    quads = width // QUAD
    return pl.pallas_call(
        cross_kernel,
        grid=(quads,),
        out_shape=(
            jax.ShapeDtypeStruct((rows, width), BF),
            jax.ShapeDtypeStruct((quads, 8, rows), F32),
        ),
        in_specs=cross_specs(rows, keys, quads),
        out_specs=[
            pl.BlockSpec((rows, QUAD), lambda j: (0, j)),
            pl.BlockSpec((1, 8, rows), lambda j: (j, 0, 0)),
        ],
        name="cross_attend",
        cost_estimate=LIGHT,
    )(query, key, value)


def cross_back_kernel(q_ref, k_ref, v_ref, o_ref, do_ref, lse_ref, dq_ref, dk_ref, dv_ref):
    keys = k_ref.shape[0]
    count = QUAD // HD
    query, grad = q_ref[...], do_ref[...]
    key = spread_heads(k_ref[...] * BF(0.125))
    scores = mm(key, query, NT)
    d_powers = mm(spread_heads(v_ref[...]), grad, NT)
    product = (grad.astype(F32) * o_ref[...].astype(F32)).T
    weights, d_scores = [], []
    for head in range(count):
        group = slice(head * keys, (head + 1) * keys)
        drop = jnp.sum(product[head * HD : (head + 1) * HD, :], axis=0, keepdims=True)
        power = jnp.exp(scores[group, :] - lse_ref[0, head : head + 1, :])
        weights.append(power.astype(BF))
        d_scores.append((power * (d_powers[group, :] - drop)).astype(BF))
    weights = jnp.concatenate(weights, axis=0)
    d_scores = jnp.concatenate(d_scores, axis=0)
    dq_ref[...] = mm(key, d_scores, TN).T.astype(BF)
    d_key = mm(d_scores, query, NN)
    d_value = mm(weights, grad, NN)
    for ref, found, scale in ((dk_ref, d_key, 0.125), (dv_ref, d_value, 1.0)):
        total = None
        for head in range(count):
            term = only(found[head * keys : (head + 1) * keys, :], lanes_of(QUAD, head))
            total = term if total is None else total + term
        ref[...] = total * scale


def cross_backward(query, key, value, mixed, d_mixed, lse):
    rows, width = query.shape
    keys = key.shape[0]
    quads = width // QUAD
    wide = pl.BlockSpec((rows, QUAD), lambda j: (0, j))
    return pl.pallas_call(
        cross_back_kernel,
        grid=(quads,),
        out_shape=(
            jax.ShapeDtypeStruct((rows, width), BF),
            jax.ShapeDtypeStruct((keys, width), F32),
            jax.ShapeDtypeStruct((keys, width), F32),
        ),
        in_specs=cross_specs(rows, keys, quads)
        + [wide, wide, pl.BlockSpec((1, 8, rows), lambda j: (j, 0, 0))],
        out_specs=[
            wide,
            pl.BlockSpec((keys, QUAD), lambda j: (0, j)),
            pl.BlockSpec((keys, QUAD), lambda j: (0, j)),
        ],
        name="cross_attend_back",
        cost_estimate=LIGHT,
    )(query, key, value, mixed, d_mixed, lse)


FF_STEP = 1024
FF_PART = 256


def ffn_kernel(n_ref, g_ref, wi_ref, wo_ref, *refs):
    act_ref, din_ref = refs[-2:]
    for part in range(wi_ref.shape[1] // FF_PART):
        cols = slice(part * FF_PART, (part + 1) * FF_PART)
        inner = mm(n_ref[...], wi_ref[:, cols], NN)
        d_act = mm(g_ref[...], wo_ref[:, cols], NN)
        phi = 0.5 + 0.5 * lax.erf(inner * (1.0 / math.sqrt(2.0)))
        bell = jnp.exp(inner * inner * -0.5) * (1.0 / math.sqrt(2.0 * math.pi))
        act_ref[:, cols] = (inner * phi).astype(BF)
        din_ref[:, cols] = (d_act * (phi + inner * bell)).astype(BF)


def ffn_middle(normed, grads, weights, block, blocks, kept=()):
    rows, width = normed.shape
    hidden = weights.shape[1] // 2
    steps = hidden // FF_STEP
    out_shape = jax.ShapeDtypeStruct((rows * blocks, hidden), BF)
    whole = pl.BlockSpec((rows, width), lambda j: (0, 0))
    out_spec = pl.BlockSpec((rows, FF_STEP), lambda j: (block, j))
    return pl.pallas_call(
        ffn_kernel,
        grid=(steps,),
        out_shape=(out_shape, out_shape),
        in_specs=[
            whole,
            whole,
            pl.BlockSpec((width, FF_STEP), lambda j: (0, j)),
            pl.BlockSpec((width, FF_STEP), lambda j: (0, steps + j)),
        ]
        + [pl.BlockSpec(memory_space=pl.ANY)] * len(kept),
        out_specs=[out_spec, out_spec],
        input_output_aliases={4 + i: i for i in range(len(kept))},
        name="ffn_middle",
        cost_estimate=LIGHT,
    )(normed, grads, weights, weights, *kept)


def stats_of(value):
    mean = jnp.mean(value, axis=-1, keepdims=True)
    centred = value - mean
    spread = jnp.mean(centred * centred, axis=-1, keepdims=True)
    return centred, lax.rsqrt(spread + EPS)


def norm_grad(value, gain, incoming):
    centred, scale = stats_of(value)
    hat = centred * scale
    scaled = incoming * gain
    mean = jnp.mean(scaled, axis=-1, keepdims=True)
    along = jnp.mean(scaled * hat, axis=-1, keepdims=True)
    return (
        scale * (scaled - mean - hat * along),
        jnp.sum(incoming * hat, axis=0),
        jnp.sum(incoming, axis=0),
    )


def on_pair(
    inputs,
    text_states,
    self_query,
    self_key,
    self_value,
    self_output,
    cross_query,
    cross_key,
    cross_value,
    cross_output,
    inner_weight,
    outer_weight,
    norm_gains,
    norm_shifts,
    cotangent,
    *,
    groups,
):
    rows, width = inputs.shape
    half = width // 2
    hidden = inner_weight.shape[1]
    shard = self_query.shape[0]
    tensor = lax.axis_index("tensor").astype(jnp.uint32)
    place = lax.axis_index("dp").astype(jnp.uint32)
    one = jnp.uint32(1)
    bits = [(place >> i) & one for i in range((groups - 1).bit_length())]
    mine, theirs = tensor * jnp.uint32(half), (tensor ^ one) * jnp.uint32(half)
    zero = jnp.uint32(0)
    lines = [[i + 4 * j for j in range(groups // 4)] for i in range(4)]
    t_ref = tensor.astype(jnp.int32).reshape(1)

    def peer(value):
        return lax.ppermute(value, "tensor", [(0, 1), (1, 0)])

    def gather(parts):
        return lax.all_gather(jnp.concatenate(parts, axis=1), "dp", axis=0, tiled=True)

    swaps = [[(i, i ^ (1 << level)) for i in range(groups)] for level in range(len(bits))]

    def swap(send, level):
        return lax.ppermute(send, "dp", swaps[level])

    def line_sum(whole):
        whole = whole.reshape(-1, whole.shape[-1])
        return lax.psum_scatter(
            whole, "dp", scatter_dimension=0, tiled=True, axis_index_groups=lines
        )

    def line_step(send, keep, ready):
        return fold(side_refs[3], after(keep, ready), swap(send, 2))

    def line_end(send, keep):
        for level in range(3, len(bits)):
            got = swap(send, level)
            if level + 1 < len(bits):
                send, keep = fold(side_refs[level + 1], keep, got)
        return (keep.astype(F32) + got.astype(F32)).reshape(shard, -1)

    part = half // CUTS
    pieces = [slice(i * part, (i + 1) * part) for i in range(CUTS)]
    side_refs = [bit.astype(jnp.int32).reshape(1) for bit in bits]
    start_x, side_refs, mine, theirs, t_ref = lax.optimization_barrier(
        (inputs, side_refs, mine, theirs, t_ref)
    )
    cross_two = jnp.concatenate([cross_query, cross_output.T], axis=1)
    cross_peer = peer(cross_two)
    first = gather(
        [v[:, p] for p in pieces for v in (self_query, self_key, self_value)]
        + [self_output.T, cross_key, cross_value]
        + [cross_query, cross_peer[:, :half], cross_two[:, half:], cross_peer[:, half:]]
    )
    second = gather([inner_weight, outer_weight.T])
    inputs_peer = peer(after(start_x, cross_peer))
    grads_peer = peer(after(cotangent, inputs_peer))
    w_qkv = first[:, : 3 * half]
    w_self_out = first[:, 3 * half : 4 * half]
    w_text = first[:, 4 * half : 6 * half]
    w_cross_query = first[:, 6 * half : 8 * half]
    w_cross_out = first[:, 8 * half :]
    w_inner = second[:, :hidden]
    w_outer = second[:, hidden:]

    start = jnp.concatenate([inputs, inputs_peer], axis=0).astype(F32)
    normed1 = norm_rows(start, norm_gains[0], norm_shifts[0]).astype(BF)
    text = text_states.reshape(-1, width)
    text_own = mm(text, w_text, NN).astype(BF)
    grads3 = jnp.concatenate([cotangent, grads_peer], axis=0)
    normed1 = after(normed1, grads3, text_own)
    qkv = mm(normed1, w_qkv, NN).astype(BF)
    text_peer = peer(text_own)
    mixed1, lse1 = self_forward(t_ref, qkv)
    away = peer(mm(mixed1[rows:], w_self_out, NT).astype(BF))
    home = mm(mixed1[:rows], w_self_out, NT)
    key2 = jnp.concatenate([text_own[:, :half], text_peer[:, :half]], axis=1)
    value2 = jnp.concatenate([text_own[:, half:], text_peer[:, half:]], axis=1)
    state1 = inputs.astype(F32) + home + away.astype(F32)

    normed2 = norm_rows(state1, norm_gains[1], norm_shifts[1]).astype(BF)
    query2 = mm(normed2, w_cross_query, NN).astype(BF)
    mixed2, lse2 = cross_forward(query2, key2, value2)
    state2 = state1 + mm(mixed2, w_cross_out, NT)

    normed3 = norm_rows(state2, norm_gains[2], norm_shifts[2]).astype(BF)
    normed3_peer = peer(normed3)
    active, d_inner = ffn_middle(normed3, cotangent, second, 0, 2)
    back3_home = product(d_inner, second, NT, F32, row=0, rows=rows)
    out_home = product(active, second, NT, F32, row=0, rows=rows, first=hidden)
    normed3_peer = after(normed3_peer, back3_home, out_home)
    active, d_inner = ffn_middle(normed3_peer, grads_peer, second, 1, 2, (active, d_inner))
    back3_part = product(d_inner, second, NT, BF, row=1, rows=rows)
    back3_away = peer(back3_part)
    d_outer = mm(after(grads3, back3_part), active, TN).astype(BF)
    outer_sum = lax.psum_scatter(d_outer, "dp", scatter_dimension=0, tiled=True)
    rows3 = jnp.concatenate([normed3, after(normed3_peer, d_outer)], axis=0)
    last = rows3

    def weight_core(left, right, first=0, size=None):
        nonlocal last
        send, keep = weight_halves(side_refs[0], after(left, last), right, shard, first, size)
        last = send
        return send, keep

    inner = weight_core(rows3, d_inner)
    inner_got = swap(inner[0], 0)

    back3_away = after(back3_away, last)
    grad2, g2, sums3 = norm_back_rows(
        state2, norm_gains[2], cotangent, [back3_home, back3_away], HEAVY
    )
    d_mixed2 = product(g2, first, NN, BF, first=8 * half, size=width)
    inner = fold(side_refs[1], after(inner[1], d_mixed2), inner_got)
    inner_got = swap(inner[0], 1)
    d_mixed2 = after(d_mixed2, inner[0])
    d_query2, d_key2, d_value2 = cross_backward(query2, key2, value2, mixed2, d_mixed2, lse2)
    d_text_send = jnp.concatenate([d_key2[:, half:], d_value2[:, half:]], axis=1).astype(BF)
    d_text_keep = jnp.concatenate([d_key2[:, :half], d_value2[:, :half]], axis=1)
    d_text_peer = peer(d_text_send)
    back2 = product(after(d_query2, d_text_send), first, NT, F32, first=6 * half)
    grad1, g1, sums2 = norm_back_rows(state1, norm_gains[1], grad2, [back2])
    g1_peer = peer(g1)

    out_part = product(after(active, g1), second, NT, BF, row=1, rows=rows, first=hidden)
    last = out_part

    def two(left, right):
        found = [weight_core(left, right, i * half, half) for i in range(2)]
        return [(keep, swap(send, 0)) for send, keep in found]

    co_own, co_away = two(g2, mixed2)
    cq_own, cq_away = two(normed2, d_query2)
    d_text = (d_text_keep + after(d_text_peer, last).astype(F32)).astype(BF)
    kv = two(text, d_text)
    text_terms = mm(after(d_text, last), w_text, NT).astype(BF)
    text_keep, text_send = (
        lax.dynamic_slice(
            text_terms, (zero, at), (text_terms.shape[0], half), allow_negative_indices=False
        )
        for at in (mine, theirs)
    )

    grads1 = jnp.concatenate([g1, after(g1_peer, text_send, last)], axis=0)
    d_mixed1 = product(grads1, first, NN, BF, first=3 * half, size=half)
    co_send = totals([(after(co_away[0], d_mixed1), co_away[1])])
    co_got = peer(co_send)
    cq_send = totals([(after(cq_away[0], co_send), cq_away[1])])
    cq_got = peer(cq_send)
    kv = [fold(side_refs[1], after(keep, cq_send), got) for keep, got in kv]
    kv = [(keep, swap(send, 1)) for send, keep in kv]
    inner = fold(side_refs[2], after(inner[1], cq_send), inner_got)
    found0 = self_backward(
        t_ref, qkv, mixed1, after(d_mixed1, kv[0][0], kv[1][0], inner[0], outer_sum), lse1, 0
    )
    text_got = peer(after(text_send, found0))
    out_away = peer(after(out_part, found0))
    last = found0
    qkv0 = weight_core(normed1, found0)
    qkv0_got = swap(qkv0[0], 0)
    so = weight_core(grads1, mixed1)
    so_got = swap(so[0], 0)
    kv_whole = totals([(after(kv[0][0], last), kv[0][1]), kv[1]])
    co = fold(side_refs[1], after(co_own[0], kv_whole), co_own[1], co_got)
    co_got = swap(co[0], 1)
    cq = fold(side_refs[1], after(cq_own[0], co[0]), cq_own[1], cq_got)
    cq_got = swap(cq[0], 1)
    inner = line_step(*inner, cq[0])
    away0 = product(after(found0, inner[0]), first, NT, F32, row=1, rows=rows, cost=HEAVY)
    qkv0 = fold(side_refs[1], after(qkv0[1], away0), qkv0_got)
    qkv0_got = swap(qkv0[0], 1)
    so = fold(side_refs[1], after(so[1], qkv0[0]), so_got)
    so_got = swap(so[0], 1)
    found1 = self_backward(t_ref, qkv, mixed1, after(d_mixed1, so[0]), lse1, 1)
    last = found1
    qkv1 = weight_core(normed1, found1)
    qkv1_got = swap(qkv1[0], 0)
    whole = totals([(after(co[1], qkv1[0]), co_got), (kv_whole,)])
    sum_a = line_sum(whole)
    qkv0 = fold(side_refs[2], after(qkv0[1], whole), qkv0_got)
    away1 = product(
        after(found1, qkv0[0]),
        first,
        NT,
        F32,
        row=1,
        rows=rows,
        first=3 * part,
        cost=HEAVY,
    )
    back1_part = (away0 + away1).astype(BF)
    back1_away = peer(back1_part)
    qkv1 = fold(side_refs[1], after(qkv1[1], back1_part), qkv1_got)
    qkv1_got = swap(qkv1[0], 1)
    cq = fold(side_refs[2], after(cq[1], qkv1[0]), cq_got)
    so = fold(side_refs[2], after(so[1], cq[0]), so_got)
    home0 = product(after(found0, so[0]), first, NT, F32, row=0, rows=rows)
    qkv0 = line_step(*qkv0, home0)
    home1 = product(after(found1, qkv0[0]), first, NT, F32, row=0, rows=rows, first=3 * part)
    qkv1 = fold(side_refs[2], after(qkv1[1], home1), qkv1_got)
    sums0 = norm_sums(after(inputs_peer, qkv1[0]), [away0, away1])
    cq = line_step(*cq, sums0)
    so = line_step(*so, cq[0])
    sums1 = sums0 + norm_sums(after(inputs, so[0], sum_a), [home0, home1])
    qkv1 = line_step(*qkv1, sums1)
    input_grad, _, _ = norm_back_rows(
        inputs, norm_gains[0], grad1, [home0, home1, after(back1_away, qkv1[0])]
    )
    inner_sum = line_end(inner[0], after(inner[1], home0))
    qkv0_sum, cq_sum, so_sum, qkv1_sum = (line_end(*v) for v in (qkv0, cq, so, qkv1))
    output = (state2 + out_home + after(out_away, last).astype(F32)).astype(BF)
    text_grad = text_keep.astype(F32) + after(text_got, last).astype(F32)
    text_grad = text_grad.reshape(1, -1, half)
    qkv_sums = [qkv0_sum, qkv1_sum]

    small = jnp.stack([v[i] for i in range(2) for v in (sums1, sums2, sums3)])
    small = after(small, back1_away)
    small = small + peer(small)
    bit = 1
    while bit < groups:
        small = small + lax.ppermute(small, "dp", [(i, i ^ bit) for i in range(groups)])
        bit *= 2

    def joined(kind):
        return jnp.concatenate([v[:, kind * part : (kind + 1) * part] for v in qkv_sums], axis=1)

    return (
        output,
        input_grad,
        text_grad,
        joined(0),
        joined(1),
        joined(2),
        so_sum.T,
        cq_sum,
        sum_a[:, half : 2 * half].astype(F32),
        sum_a[:, 2 * half :].astype(F32),
        sum_a[:, :half].astype(F32).T,
        inner_sum.astype(F32),
        outer_sum.astype(F32).T,
        small[:3],
        small[3:],
    )


def pairs_up(mesh, inputs, text_states, inner_weight):
    groups, sides = mesh.shape["dp"], mesh.shape["tensor"]
    width = inputs.shape[1]
    return (
        sides == 2
        and groups >= 16
        and groups & (groups - 1) == 0
        and text_states.shape[0] == groups
        and text_states.shape[1] == TEXT
        and inputs.shape[0] == groups * LEN
        and width % (2 * QUAD) == 0
        and width % (2 * CUTS * PAIR) == 0
        and width % (32 * groups) in (0, 16 * groups)
        and inner_weight.shape[1] % (2 * FF_STEP) == 0
    )


def solution(mesh):
    in_specs = (
        P(("dp", "tensor"), None),
        P("dp", None, None),
        P("dp", "tensor"),
        P("dp", "tensor"),
        P("dp", "tensor"),
        P("tensor", "dp"),
        P("dp", "tensor"),
        P("dp", "tensor"),
        P("dp", "tensor"),
        P("tensor", "dp"),
        P("dp", "tensor"),
        P("tensor", "dp"),
        P(),
        P(),
        P(("dp", "tensor"), None),
    )
    out_specs = (
        P(("dp", "tensor"), None),
        P(("dp", "tensor"), None),
        P("dp", None, "tensor"),
        P("dp", "tensor"),
        P("dp", "tensor"),
        P("dp", "tensor"),
        P("tensor", "dp"),
        P("dp", "tensor"),
        P("dp", "tensor"),
        P("dp", "tensor"),
        P("tensor", "dp"),
        P("dp", "tensor"),
        P("tensor", "dp"),
        P(),
        P(),
    )

    def layer(*args):
        body = on_device
        if pairs_up(mesh, args[0], args[1], args[10]):
            body = partial(on_pair, groups=mesh.shape["dp"])
        return jax.shard_map(
            body, mesh=mesh, in_specs=in_specs, out_specs=out_specs, check_vma=False
        )(*args)

    return layer
```

```python
from functools import partial
import math

import jax
import jax.numpy as jnp
from jax import lax
from jax.experimental import pallas as pl
from jax.experimental.pallas import tpu as pltpu
from jax.sharding import PartitionSpec as P

HD = 64
TEXT = 64
LEN = 1024


EPS = 1e-05
MASKED = -1e30


def norm_rows(value, gain, shift):
    mean = jnp.mean(value, axis=-1, keepdims=True)
    centred = value - mean
    spread = jnp.mean(centred * centred, axis=-1, keepdims=True)
    return centred * lax.rsqrt(spread + EPS) * gain + shift


def norm_back(value, gain, shift, incoming):
    ignored, pullback = jax.vjp(norm_rows, value, gain, shift)
    return pullback(incoming)


def gelu_exact(value):
    return jax.nn.gelu(value, approximate=False)


def transposed_times(left, right):
    return lax.dot_general(
        left, right, (((0,), (0,)), ((), ())), preferred_element_type=jnp.float32
    )


def times_t(left, right):
    return lax.dot_general(
        left, right, (((1,), (1,)), ((), ())), preferred_element_type=jnp.float32
    )


def apply_projection(left, right):
    return jnp.dot(left, right, preferred_element_type=jnp.float32).astype(jnp.bfloat16)


def scores_of(query, key, masked):
    scale = 1.0 / math.sqrt(HD)
    scores = jnp.einsum("qhd,khd->hqk", query, key, preferred_element_type=jnp.float32) * scale
    if masked:
        places = jnp.arange(query.shape[0])
        allowed = places[:, None] >= places[None, :]
        scores = jnp.where(allowed[None], scores, MASKED)
    return scores


def attend(block, masked):
    query, key, value = block
    scores = scores_of(query, key, masked)
    highest = jnp.max(scores, axis=-1, keepdims=True)
    total = jnp.sum(jnp.exp(scores - highest), axis=-1, keepdims=True)
    log_total = highest + jnp.log(total)
    weights = jnp.exp(scores - log_total).astype(jnp.bfloat16)
    mixed = jnp.einsum("hqk,khd->qhd", weights, value, preferred_element_type=jnp.float32)
    return (mixed.astype(jnp.bfloat16), log_total)


def attend_back(block, masked):
    query, key, value, log_total, grad_mixed = block
    scale = 1.0 / math.sqrt(HD)
    weights = jnp.exp(scores_of(query, key, masked) - log_total)
    rounded = weights.astype(jnp.bfloat16)
    d_value = jnp.einsum("hqk,qhd->khd", rounded, grad_mixed, preferred_element_type=jnp.float32)
    d_weights = jnp.einsum("qhd,khd->hqk", grad_mixed, value, preferred_element_type=jnp.float32)
    centred = d_weights - jnp.sum(weights * d_weights, axis=-1, keepdims=True)
    d_scores = (weights * centred).astype(jnp.bfloat16)
    d_query = jnp.einsum("hqk,khd->qhd", d_scores, key, preferred_element_type=jnp.float32) * scale
    d_key = jnp.einsum("hqk,qhd->khd", d_scores, query, preferred_element_type=jnp.float32) * scale
    return (d_query.astype(jnp.bfloat16), d_key.astype(jnp.bfloat16), d_value.astype(jnp.bfloat16))


def spread_rows(normed):
    return lax.all_gather(normed, "tensor", axis=0, tiled=True)


def spread_grads(grad):
    return lax.all_gather(grad.astype(jnp.bfloat16), "tensor", axis=0, tiled=True)


def branch_total(mixed, weight):
    return lax.psum_scatter(
        jnp.dot(mixed, weight, preferred_element_type=jnp.float32),
        "tensor",
        scatter_dimension=0,
        tiled=True,
    )


def normalized_total(pairs):
    total = None
    for grad, weight in pairs:
        added = times_t(grad, weight)
        total = added if total is None else total + added
    return lax.psum_scatter(total, "tensor", scatter_dimension=0, tiled=True)


def on_device(
    inputs,
    text_states,
    self_query,
    self_key,
    self_value,
    self_output,
    cross_query,
    cross_key,
    cross_value,
    cross_output,
    inner_weight,
    outer_weight,
    norm_gains,
    norm_shifts,
    cotangent,
):
    (
        gathered_self_query,
        gathered_self_key,
        gathered_self_value,
        full_soutput,
        full_cquery,
        full_ckey,
        full_cvalue,
        full_coutput,
        full_inner,
        full_outer,
    ) = (
        lax.all_gather(self_query, "dp", axis=0, tiled=True),
        lax.all_gather(self_key, "dp", axis=0, tiled=True),
        lax.all_gather(self_value, "dp", axis=0, tiled=True),
        lax.all_gather(self_output, "dp", axis=1, tiled=True),
        lax.all_gather(cross_query, "dp", axis=0, tiled=True),
        lax.all_gather(cross_key, "dp", axis=0, tiled=True),
        lax.all_gather(cross_value, "dp", axis=0, tiled=True),
        lax.all_gather(cross_output, "dp", axis=1, tiled=True),
        lax.all_gather(inner_weight, "dp", axis=0, tiled=True),
        lax.all_gather(outer_weight, "dp", axis=1, tiled=True),
    )
    width = inputs.shape[1]
    clips = text_states.shape[0]
    local_heads = gathered_self_query.shape[1] // HD

    def heads(value, length):
        return value.reshape(clips, length, local_heads, HD)

    def flatten(value):
        return value.reshape(-1, local_heads * HD)

    start = inputs.astype(jnp.float32)
    first_rows = spread_rows(norm_rows(start, norm_gains[0], norm_shifts[0]).astype(jnp.bfloat16))
    query1 = apply_projection(first_rows, gathered_self_query)
    first_key = apply_projection(first_rows, gathered_self_key)
    value1 = apply_projection(first_rows, gathered_self_value)
    mixed1, lse1 = lax.map(
        partial(attend, masked=True),
        (heads(query1, LEN), heads(first_key, LEN), heads(value1, LEN)),
    )
    mixed1 = flatten(mixed1)
    state1 = start + branch_total(mixed1, full_soutput)
    rows2 = spread_rows(norm_rows(state1, norm_gains[1], norm_shifts[1]).astype(jnp.bfloat16))
    query2 = apply_projection(rows2, full_cquery)
    text_flat = text_states.reshape(-1, width)
    key2 = apply_projection(text_flat, full_ckey)
    value2 = apply_projection(text_flat, full_cvalue)
    mixed2, lse2 = lax.map(
        partial(attend, masked=False), (heads(query2, LEN), heads(key2, TEXT), heads(value2, TEXT))
    )
    mixed2 = flatten(mixed2)
    state2 = state1 + branch_total(mixed2, full_coutput)
    rows3 = spread_rows(norm_rows(state2, norm_gains[2], norm_shifts[2]).astype(jnp.bfloat16))
    inner = jnp.dot(rows3, full_inner, preferred_element_type=jnp.float32)
    active_float, gelu_pull = jax.vjp(gelu_exact, inner)
    active = active_float.astype(jnp.bfloat16)
    result = state2 + branch_total(active, full_outer)
    output = result.astype(jnp.bfloat16)
    grad3 = cotangent.astype(jnp.float32)
    grads_outer = spread_grads(grad3)
    d_outer = transposed_times(active, grads_outer)
    d_inner = gelu_pull(times_t(grads_outer, full_outer))[0].astype(jnp.bfloat16)
    d_innerw = transposed_times(rows3, d_inner)
    back3 = normalized_total(((d_inner, full_inner),))
    d_state2, gain_three, shift_three = norm_back(state2, norm_gains[2], norm_shifts[2], back3)
    grad2 = grad3 + d_state2
    grads_cross = spread_grads(grad2)
    d_coutput = transposed_times(mixed2, grads_cross)
    d_mixed2 = times_t(grads_cross, full_coutput).astype(jnp.bfloat16)
    d_query2, d_key2, d_value2 = lax.map(
        partial(attend_back, masked=False),
        (heads(query2, LEN), heads(key2, TEXT), heads(value2, TEXT), lse2, heads(d_mixed2, LEN)),
    )
    d_query2 = flatten(d_query2)
    d_key2 = flatten(d_key2)
    d_value2 = flatten(d_value2)
    d_cquery = transposed_times(rows2, d_query2)
    d_ckey = transposed_times(text_flat, d_key2)
    d_cvalue = transposed_times(text_flat, d_value2)
    text_terms = (times_t(d_key2, full_ckey) + times_t(d_value2, full_cvalue)).reshape(
        clips, TEXT, width
    )
    text_grad = lax.psum_scatter(
        text_terms.astype(jnp.bfloat16), "tensor", scatter_dimension=2, tiled=True
    ).astype(jnp.float32)
    back2 = normalized_total(((d_query2, full_cquery),))
    d_state1, gain_two, shift_two = norm_back(state1, norm_gains[1], norm_shifts[1], back2)
    grad1 = grad2 + d_state1
    grads_self = spread_grads(grad1)
    d_soutput = transposed_times(mixed1, grads_self)
    d_mixed1 = times_t(grads_self, full_soutput).astype(jnp.bfloat16)
    first_query_grad, first_key_grad, first_value_grad = lax.map(
        partial(attend_back, masked=True),
        (heads(query1, LEN), heads(first_key, LEN), heads(value1, LEN), lse1, heads(d_mixed1, LEN)),
    )
    first_query_grad = flatten(first_query_grad)
    first_key_grad = flatten(first_key_grad)
    first_value_grad = flatten(first_value_grad)
    d_squery = transposed_times(first_rows, first_query_grad)
    self_key_partial = transposed_times(first_rows, first_key_grad)
    d_svalue = transposed_times(first_rows, first_value_grad)
    first_backward = normalized_total(
        (
            (first_query_grad, gathered_self_query),
            (first_key_grad, gathered_self_key),
            (first_value_grad, gathered_self_value),
        )
    )
    d_start, gain_one, shift_one = norm_back(start, norm_gains[0], norm_shifts[0], first_backward)
    input_grad = grad1 + d_start
    gains_grad, shifts_grad = lax.psum(
        (
            jnp.stack([gain_one, gain_two, gain_three]),
            jnp.stack([shift_one, shift_two, shift_three]),
        ),
        ("dp", "tensor"),
    )
    summed = (
        lax.psum_scatter(
            d_squery.astype(jnp.bfloat16), "dp", scatter_dimension=0, tiled=True
        ).astype(jnp.float32),
        lax.psum_scatter(
            self_key_partial.astype(jnp.bfloat16), "dp", scatter_dimension=0, tiled=True
        ).astype(jnp.float32),
        lax.psum_scatter(
            d_svalue.astype(jnp.bfloat16), "dp", scatter_dimension=0, tiled=True
        ).astype(jnp.float32),
        lax.psum_scatter(
            d_soutput.astype(jnp.bfloat16), "dp", scatter_dimension=1, tiled=True
        ).astype(jnp.float32),
        lax.psum_scatter(
            d_cquery.astype(jnp.bfloat16), "dp", scatter_dimension=0, tiled=True
        ).astype(jnp.float32),
        lax.psum_scatter(d_ckey.astype(jnp.bfloat16), "dp", scatter_dimension=0, tiled=True).astype(
            jnp.float32
        ),
        lax.psum_scatter(
            d_cvalue.astype(jnp.bfloat16), "dp", scatter_dimension=0, tiled=True
        ).astype(jnp.float32),
        lax.psum_scatter(
            d_coutput.astype(jnp.bfloat16), "dp", scatter_dimension=1, tiled=True
        ).astype(jnp.float32),
        lax.psum_scatter(
            d_innerw.astype(jnp.bfloat16), "dp", scatter_dimension=0, tiled=True
        ).astype(jnp.float32),
        lax.psum_scatter(
            d_outer.astype(jnp.bfloat16), "dp", scatter_dimension=1, tiled=True
        ).astype(jnp.float32),
    )
    return (
        output,
        input_grad,
        text_grad,
        summed[0],
        summed[1],
        summed[2],
        summed[3],
        summed[4],
        summed[5],
        summed[6],
        summed[7],
        summed[8],
        summed[9],
        gains_grad,
        shifts_grad,
    )


BF = jnp.bfloat16
F32 = jnp.float32
NN = (((1,), (0,)), ((), ()))
NT = (((1,), (1,)), ((), ()))
TN = (((0,), (0,)), ((), ()))
QB = 256
PAIR = 128
QUAD = 256
CUTS = 2


def after(value, *ready):
    return lax.optimization_barrier((value,) + ready)[0]


def mm(left, right, dims):
    return lax.dot_general(left, right, dims, preferred_element_type=F32)


LIGHT = pl.CostEstimate(flops=1024, transcendentals=0, bytes_accessed=1024)
MIDDLE = pl.CostEstimate(flops=20_000_000_000, transcendentals=0, bytes_accessed=1024)
HEAVY = pl.CostEstimate(flops=10**15, transcendentals=0, bytes_accessed=1024)


def weight_kernel(side_ref, left_ref, right_ref, send_ref, keep_ref, *, shard):
    total = mm(left_ref[...], right_ref[...], TN).astype(BF)
    side = side_ref[0]
    for parity in range(2):
        even, odd = (keep_ref, send_ref) if parity == 0 else (send_ref, keep_ref)

        @pl.when(side == parity)
        def _():
            for at in range(total.shape[0] // shard):
                rows = total[at * shard : (at + 1) * shard, :]
                (odd if at % 2 else even)[at // 2] = rows


def weight_halves(side, left, right, shard, first=0, size=None):
    depth, width = left.shape
    size = size or right.shape[1]
    tile = next(t for t in (768, 1152, 512, 384, 256, 128) if size % t == 0 and first % t == 0)
    count = width // shard // 2
    shape = jax.ShapeDtypeStruct((count, shard, size), BF)
    out = pl.BlockSpec((count, shard, tile), lambda j, s: (0, 0, j))
    return pl.pallas_call(
        partial(weight_kernel, shard=shard),
        out_shape=(shape, shape),
        grid_spec=pltpu.PrefetchScalarGridSpec(
            num_scalar_prefetch=1,
            grid=(size // tile,),
            in_specs=[
                pl.BlockSpec((depth, width), lambda j, s: (0, 0)),
                pl.BlockSpec((depth, tile), lambda j, s: (0, first // tile + j)),
            ],
            out_specs=[out, out],
        ),
        name="weight_halves",
        cost_estimate=LIGHT,
    )(side, left, right)


def added(refs, at=slice(None)):
    total = refs[0][at].astype(F32)
    for ref in refs[1:]:
        total = total + ref[at].astype(F32)
    return total.astype(BF)


def pairs_per_step(count, row_bytes):
    while count > 1 and count % 2 == 0 and count * row_bytes > 5_000_000:
        count //= 2
    return count


def fold_kernel(side_ref, *refs, counts):
    send_ref, keep_ref = refs[-2:]
    side = side_ref[0]
    first, at = 0, 0
    for count in counts:
        terms = refs[at : at + count]
        size = terms[0].shape[2]
        for pair in range(keep_ref.shape[0]):
            for out_ref, bit in ((send_ref, 1 - side), (keep_ref, side)):
                out_ref[pair, :, first : first + size] = added(terms, 2 * pair + bit)
        first, at = first + size, at + count


def fold(side, *groups, cost=None):
    count, shard = groups[0][0].shape[0] // 2, groups[0][0].shape[1]
    sizes = [terms[0].shape[2] for terms in groups]
    row = sum(4 * shard * size * (len(terms) + 1) for size, terms in zip(sizes, groups))
    per = pairs_per_step(count, row)
    shape = jax.ShapeDtypeStruct((count, shard, sum(sizes)), BF)
    spec = lambda size: pl.BlockSpec((2 * per, shard, size), lambda j, s: (j, 0, 0))
    part = pl.BlockSpec((per, shard, sum(sizes)), lambda j, s: (j, 0, 0))
    return pl.pallas_call(
        partial(fold_kernel, counts=[len(terms) for terms in groups]),
        out_shape=(shape, shape),
        grid_spec=pltpu.PrefetchScalarGridSpec(
            num_scalar_prefetch=1,
            grid=(count // per,),
            in_specs=[spec(size) for size, terms in zip(sizes, groups) for _ in terms],
            out_specs=[part, part],
        ),
        name="fold",
        cost_estimate=cost or LIGHT,
    )(side, *[v for terms in groups for v in terms])


def totals_kernel(*refs, counts):
    out_ref = refs[-1]
    first, at = 0, 0
    for count in counts:
        size = refs[at].shape[2]
        out_ref[:, :, first : first + size] = added(refs[at : at + count])
        first, at = first + size, at + count


def totals(*groups):
    count, shard = groups[0][0].shape[:2]
    sizes = [terms[0].shape[2] for terms in groups]
    row = sum(2 * shard * size * (len(terms) + 1) for size, terms in zip(sizes, groups))
    per = pairs_per_step(count, row)
    spec = lambda size: pl.BlockSpec((per, shard, size), lambda j: (j, 0, 0))
    return pl.pallas_call(
        partial(totals_kernel, counts=[len(terms) for terms in groups]),
        grid=(count // per,),
        out_shape=jax.ShapeDtypeStruct((count, shard, sum(sizes)), BF),
        in_specs=[spec(size) for size, terms in zip(sizes, groups) for _ in terms],
        out_specs=spec(sum(sizes)),
        name="totals",
        cost_estimate=LIGHT,
    )(*[v for terms in groups for v in terms])


def pack_kernel(*refs, parts):
    out_ref = refs[-1]
    first = 0
    for which, begin, end, turned in parts:
        ref = refs[which]
        value = ref[begin:end, :].T if turned else ref[:, begin:end]
        out_ref[:, first : first + end - begin] = value
        first += end - begin


def pack(arrays, parts):
    shard = arrays[0].shape[0]
    return pl.pallas_call(
        partial(pack_kernel, parts=parts),
        out_shape=jax.ShapeDtypeStruct((shard, sum(end - begin for _, begin, end, _ in parts)), BF),
        name="pack",
        cost_estimate=LIGHT,
    )(*arrays)


def norm_sums_kernel(value_ref, *refs):
    sums_ref = refs[-1]
    incoming = refs[0][...].astype(F32)
    for ref in refs[1:-1]:
        incoming = incoming + ref[...].astype(F32)
    centred, scale = stats_of(value_ref[...].astype(F32))

    @pl.when(pl.program_id(0) == 0)
    def _():
        sums_ref[...] = jnp.zeros_like(sums_ref)

    sums_ref[0:1, :] += jnp.sum(incoming * (centred * scale), axis=0, keepdims=True)
    sums_ref[1:2, :] += jnp.sum(incoming, axis=0, keepdims=True)


def norm_sums(value, incoming):
    rows, width = value.shape
    tile = 256 if rows % 256 == 0 else 128
    spec = pl.BlockSpec((tile, width), lambda j: (j, 0))
    return pl.pallas_call(
        norm_sums_kernel,
        grid=(rows // tile,),
        out_shape=jax.ShapeDtypeStruct((8, width), F32),
        in_specs=[spec] * (1 + len(incoming)),
        out_specs=pl.BlockSpec((8, width), lambda j: (0, 0)),
        name="norm_sums",
        cost_estimate=LIGHT,
    )(value, *incoming)


def norm_back_kernel(value_ref, gain_ref, base_ref, *refs, parts):
    grad_ref, low_ref, sums_ref = refs[parts:]
    incoming = refs[0][...].astype(F32)
    for ref in refs[1:parts]:
        incoming = incoming + ref[...].astype(F32)
    centred, scale = stats_of(value_ref[...].astype(F32))
    hat = centred * scale
    scaled = incoming * gain_ref[...]
    mean = jnp.mean(scaled, axis=-1, keepdims=True)
    along = jnp.mean(scaled * hat, axis=-1, keepdims=True)
    grad = base_ref[...].astype(F32) + scale * (scaled - mean - hat * along)
    grad_ref[...] = grad
    low_ref[...] = grad.astype(BF)

    @pl.when(pl.program_id(0) == 0)
    def _():
        sums_ref[...] = jnp.zeros_like(sums_ref)

    sums_ref[0:1, :] += jnp.sum(incoming * hat, axis=0, keepdims=True)
    sums_ref[1:2, :] += jnp.sum(incoming, axis=0, keepdims=True)


def norm_back_rows(value, gain, base, incoming, cost=LIGHT):
    rows, width = value.shape
    tile = 256 if rows % 256 == 0 else 128
    spec = pl.BlockSpec((tile, width), lambda j: (j, 0))
    return pl.pallas_call(
        partial(norm_back_kernel, parts=len(incoming)),
        grid=(rows // tile,),
        out_shape=(
            jax.ShapeDtypeStruct((rows, width), F32),
            jax.ShapeDtypeStruct((rows, width), BF),
            jax.ShapeDtypeStruct((8, width), F32),
        ),
        in_specs=[spec, pl.BlockSpec((1, width), lambda j: (0, 0)), spec] + [spec] * len(incoming),
        out_specs=[spec, spec, pl.BlockSpec((8, width), lambda j: (0, 0))],
        name="norm_back",
        cost_estimate=cost,
    )(value, gain.reshape(1, width), base, *incoming)


def joint_kernel(*refs):
    right_ref, out_ref = refs[-2:]
    depth = refs[0].shape[1]
    total = None
    for i, ref in enumerate(refs[:-2]):
        term = mm(ref[...], right_ref[:, i * depth : (i + 1) * depth], NT)
        total = term if total is None else total + term
    out_ref[...] = total.astype(out_ref.dtype)


def joint_product(lefts, right, dtype, row, rows, cost):
    depth, size, tile = lefts[0].shape[1], right.shape[0], 512
    return pl.pallas_call(
        joint_kernel,
        grid=(size // tile,),
        out_shape=jax.ShapeDtypeStruct((rows, size), dtype),
        in_specs=[pl.BlockSpec((rows, depth), lambda j: (row, 0))] * len(lefts)
        + [pl.BlockSpec((tile, depth * len(lefts)), lambda j: (j, 0))],
        out_specs=pl.BlockSpec((rows, tile), lambda j: (0, j)),
        name="joint_product",
        cost_estimate=cost,
    )(*lefts, right)


def product_kernel(left_ref, right_ref, out_ref, *, dims):
    out_ref[...] = mm(left_ref[...], right_ref[...], dims).astype(out_ref.dtype)


def product(left, right, dims, dtype, row=0, rows=None, first=0, size=None, cost=LIGHT):
    rows = rows or left.shape[0]
    depth = left.shape[1]
    if dims is NN:
        size = size or right.shape[1]
        tile = next(t for t in (768, 512, 384, 256) if size % t == 0 and first % t == 0)
        right_spec = pl.BlockSpec((depth, tile), lambda j: (0, first // tile + j))
    else:
        size = right.shape[0]
        tile = 512
        right_spec = pl.BlockSpec((tile, depth), lambda j: (j, first // depth))
    return pl.pallas_call(
        partial(product_kernel, dims=dims),
        grid=(size // tile,),
        out_shape=jax.ShapeDtypeStruct((rows, size), dtype),
        in_specs=[pl.BlockSpec((rows, depth), lambda j: (row, 0)), right_spec],
        out_specs=pl.BlockSpec((rows, tile), lambda j: (0, j)),
        name="product",
        cost_estimate=cost,
    )(left, right)


def lanes_of(width, head):
    lane = lax.broadcasted_iota(jnp.int32, (1, width), 1)
    return (lane >= head * HD) & (lane < (head + 1) * HD)


def only(value, mask):
    return jnp.where(mask, value, jnp.zeros_like(value))


def pieces_of(block):
    start = block * QB
    found = [(0, start, False)] if block else []
    return found + [(start, start + QB, True)]


def causal():
    key = lax.broadcasted_iota(jnp.int32, (QB, QB), 0)
    place = lax.broadcasted_iota(jnp.int32, (QB, QB), 1)
    return key <= place


def to_places(t, ref, held, half):
    low = pl.multiple_of(t * half, half)
    high = pl.multiple_of((1 - t) * half, half)
    held[0:half, :] = ref[pl.ds(low, half), :]
    held[half : 2 * half, :] = ref[pl.ds(high, half), :]


def row_of(t, start, half):
    side = start // half
    base = (1 - t) * half if side else t * half
    return pl.multiple_of(base + start % half, QB)


def self_kernel(t_ref, q_ref, k_ref, v_ref, o_ref, lse_ref, qs, ks, vs):
    t = t_ref[0]
    length = q_ref.shape[0]
    half = length // 2
    for ref, held in ((q_ref, qs), (k_ref, ks), (v_ref, vs)):
        to_places(t, ref, held, half)
    allowed = causal()
    for block in range(length // QB):
        rows = slice(block * QB, (block + 1) * QB)
        query = qs[rows, :] * BF(0.125)
        mixed = []
        for head in range(2):
            mine = only(query, lanes_of(PAIR, head))
            parts = []
            for a, b, edge in pieces_of(block):
                score = mm(ks[a:b, :], mine, NT)
                parts.append(jnp.where(allowed, score, MASKED) if edge else score)
            top = jnp.max(parts[0], axis=0, keepdims=True)
            for part in parts[1:]:
                top = jnp.maximum(top, jnp.max(part, axis=0, keepdims=True))
            total, out = None, None
            for part, (a, b, edge) in zip(parts, pieces_of(block)):
                power = jnp.exp(part - top)
                added = jnp.sum(power, axis=0, keepdims=True)
                term = mm(vs[a:b, :], power.astype(BF), TN)
                total = added if total is None else total + added
                out = term if out is None else out + term
            lse_ref[0, head : head + 1, rows] = top + jnp.log(total)
            mixed.append(out[head * HD : (head + 1) * HD, :] / total)
        both = jnp.concatenate(mixed, axis=0)
        o_ref[pl.ds(row_of(t, block * QB, half), QB), :] = both.T.astype(BF)


def self_forward(t, qkv):
    length, width = qkv.shape
    pairs = width // (3 * PAIR)
    cut = pairs // CUTS
    spec = lambda part: pl.BlockSpec(
        (length, PAIR), lambda j, r: (0, (3 * (j // cut) + part) * cut + j % cut)
    )
    return pl.pallas_call(
        self_kernel,
        out_shape=(
            jax.ShapeDtypeStruct((length, pairs * PAIR), BF),
            jax.ShapeDtypeStruct((pairs, 8, length), F32),
        ),
        grid_spec=pltpu.PrefetchScalarGridSpec(
            num_scalar_prefetch=1,
            grid=(pairs,),
            in_specs=[spec(0), spec(1), spec(2)],
            out_specs=[
                pl.BlockSpec((length, PAIR), lambda j, s: (0, j)),
                pl.BlockSpec((1, 8, length), lambda j, s: (j, 0, 0)),
            ],
            scratch_shapes=[pltpu.VMEM((length, PAIR), BF)] * 3,
        ),
        name="self_attend",
        cost_estimate=LIGHT,
    )(t, qkv, qkv, qkv)


def self_back_kernel(
    t_ref, q_ref, k_ref, v_ref, o_ref, do_ref, lse_ref, out_ref, qs, ks, vs, os, dos, dk, dv, dkb, dvb
):
    t = t_ref[0]
    length = q_ref.shape[0]
    half = length // 2
    step = pl.program_id(1)

    @pl.when(step == 0)
    def _():
        for ref, held in ((q_ref, qs), (k_ref, ks), (v_ref, vs), (o_ref, os), (do_ref, dos)):
            to_places(t, ref, held, half)
        allowed = causal()
        blocks = length // QB
        for block in reversed(range(blocks)):
            rows = slice(block * QB, (block + 1) * QB)
            query = qs[rows, :] * BF(0.125)
            grad = dos[rows, :]
            product = (grad.astype(F32) * os[rows, :].astype(F32)).T
            mine = [only(query, lanes_of(PAIR, head)) for head in range(2)]
            mine_grad = [only(grad, lanes_of(PAIR, head)) for head in range(2)]
            both_query = jnp.concatenate(mine, axis=0)
            both_grad = jnp.concatenate(mine_grad, axis=0)
            d_query = [None, None]
            for a, b, edge in pieces_of(block):
                weights, d_scores = [], []
                for head in range(2):
                    drop = jnp.sum(product[head * HD : (head + 1) * HD, :], axis=0, keepdims=True)
                    score = mm(ks[a:b, :], mine[head], NT)
                    power = jnp.exp(score - lse_ref[0, head : head + 1, rows])
                    if edge:
                        power = jnp.where(allowed, power, 0.0)
                    d_power = mm(vs[a:b, :], mine_grad[head], NT)
                    d_score = (power * (d_power - drop)).astype(BF)
                    weights.append(power.astype(BF))
                    d_scores.append(d_score)
                    term = mm(ks[a:b, :], d_score, TN)
                    d_query[head] = term if d_query[head] is None else d_query[head] + term
                add_v = mm(jnp.concatenate(weights, axis=1), both_grad, NN)
                add_k = mm(jnp.concatenate(d_scores, axis=1), both_query, NN)
                if block == blocks - 1:
                    dv[a:b, :] = add_v
                    dk[a:b, :] = add_k
                else:
                    dv[a:b, :] += add_v
                    dk[a:b, :] += add_k
            both = jnp.concatenate([d_query[0][:HD, :], d_query[1][HD:, :]], axis=0) * 0.125
            out_ref[pl.ds(row_of(t, block * QB, half), QB), :] = both.T.astype(BF)
        for block in range(blocks):
            rows = slice(block * QB, (block + 1) * QB)
            place = row_of(t, block * QB, half)
            dkb[pl.ds(place, QB), :] = dk[rows, :].astype(BF)
            dvb[pl.ds(place, QB), :] = dv[rows, :].astype(BF)

    @pl.when(step == 1)
    def _():
        out_ref[...] = dkb[...]

    @pl.when(step == 2)
    def _():
        out_ref[...] = dvb[...]


def self_backward(t, qkv, mixed, d_mixed, lse, part):
    length, width = qkv.shape[0], qkv.shape[1] // CUTS
    pairs = width // (3 * PAIR)
    first = part * pairs
    spec = lambda kind: pl.BlockSpec(
        (length, PAIR), lambda j, s, r: (0, 3 * first + kind * pairs + j)
    )
    return pl.pallas_call(
        self_back_kernel,
        out_shape=jax.ShapeDtypeStruct((length, width), BF),
        grid_spec=pltpu.PrefetchScalarGridSpec(
            num_scalar_prefetch=1,
            grid=(pairs, 3),
            in_specs=[
                spec(0),
                spec(1),
                spec(2),
                pl.BlockSpec((length, PAIR), lambda j, s, r: (0, first + j)),
                pl.BlockSpec((length, PAIR), lambda j, s, r: (0, first + j)),
                pl.BlockSpec((1, 8, length), lambda j, s, r: (first + j, 0, 0)),
            ],
            out_specs=pl.BlockSpec((length, PAIR), lambda j, s, r: (0, s * pairs + j)),
            scratch_shapes=[pltpu.VMEM((length, PAIR), BF)] * 5
            + [pltpu.VMEM((length, PAIR), F32)] * 2
            + [pltpu.VMEM((length, PAIR), BF)] * 2,
        ),
        name="self_attend_back",
        cost_estimate=MIDDLE,
    )(t, qkv, qkv, qkv, mixed, d_mixed, lse)


def spread_heads(value):
    count = QUAD // HD
    return jnp.concatenate([only(value, lanes_of(QUAD, head)) for head in range(count)], axis=0)


def cross_kernel(q_ref, k_ref, v_ref, o_ref, lse_ref):
    keys = k_ref.shape[0]
    scores = mm(spread_heads(k_ref[...] * BF(0.125)), q_ref[...], NT)
    powers, totals = [], []
    for head in range(QUAD // HD):
        score = scores[head * keys : (head + 1) * keys, :]
        top = jnp.max(score, axis=0, keepdims=True)
        power = jnp.exp(score - top)
        total = jnp.sum(power, axis=0, keepdims=True)
        lse_ref[0, head : head + 1, :] = top + jnp.log(total)
        powers.append(power.astype(BF))
        totals.append(total)
    mixed = mm(spread_heads(v_ref[...]), jnp.concatenate(powers, axis=0), TN)
    scaled = [
        mixed[head * HD : (head + 1) * HD, :] / totals[head] for head in range(QUAD // HD)
    ]
    o_ref[...] = jnp.concatenate(scaled, axis=0).T.astype(BF)


def cross_specs(rows, keys, quads):
    return [
        pl.BlockSpec((rows, QUAD), lambda j: (0, j)),
        pl.BlockSpec((keys, QUAD), lambda j: (0, j)),
        pl.BlockSpec((keys, QUAD), lambda j: (0, j)),
    ]


def cross_forward(query, key, value):
    rows, width = query.shape
    keys = key.shape[0]
    quads = width // QUAD
    return pl.pallas_call(
        cross_kernel,
        grid=(quads,),
        out_shape=(
            jax.ShapeDtypeStruct((rows, width), BF),
            jax.ShapeDtypeStruct((quads, 8, rows), F32),
        ),
        in_specs=cross_specs(rows, keys, quads),
        out_specs=[
            pl.BlockSpec((rows, QUAD), lambda j: (0, j)),
            pl.BlockSpec((1, 8, rows), lambda j: (j, 0, 0)),
        ],
        name="cross_attend",
        cost_estimate=LIGHT,
    )(query, key, value)


def cross_back_kernel(q_ref, k_ref, v_ref, o_ref, do_ref, lse_ref, dq_ref, dk_ref, dv_ref):
    keys = k_ref.shape[0]
    count = QUAD // HD
    query, grad = q_ref[...], do_ref[...]
    key = spread_heads(k_ref[...] * BF(0.125))
    scores = mm(key, query, NT)
    d_powers = mm(spread_heads(v_ref[...]), grad, NT)
    product = (grad.astype(F32) * o_ref[...].astype(F32)).T
    weights, d_scores = [], []
    for head in range(count):
        group = slice(head * keys, (head + 1) * keys)
        drop = jnp.sum(product[head * HD : (head + 1) * HD, :], axis=0, keepdims=True)
        power = jnp.exp(scores[group, :] - lse_ref[0, head : head + 1, :])
        weights.append(power.astype(BF))
        d_scores.append((power * (d_powers[group, :] - drop)).astype(BF))
    weights = jnp.concatenate(weights, axis=0)
    d_scores = jnp.concatenate(d_scores, axis=0)
    dq_ref[...] = mm(key, d_scores, TN).T.astype(BF)
    d_key = mm(d_scores, query, NN)
    d_value = mm(weights, grad, NN)
    for ref, found, scale in ((dk_ref, d_key, 0.125), (dv_ref, d_value, 1.0)):
        total = None
        for head in range(count):
            term = only(found[head * keys : (head + 1) * keys, :], lanes_of(QUAD, head))
            total = term if total is None else total + term
        ref[...] = total * scale


def cross_backward(query, key, value, mixed, d_mixed, lse):
    rows, width = query.shape
    keys = key.shape[0]
    quads = width // QUAD
    wide = pl.BlockSpec((rows, QUAD), lambda j: (0, j))
    return pl.pallas_call(
        cross_back_kernel,
        grid=(quads,),
        out_shape=(
            jax.ShapeDtypeStruct((rows, width), BF),
            jax.ShapeDtypeStruct((keys, width), F32),
            jax.ShapeDtypeStruct((keys, width), F32),
        ),
        in_specs=cross_specs(rows, keys, quads)
        + [wide, wide, pl.BlockSpec((1, 8, rows), lambda j: (j, 0, 0))],
        out_specs=[
            wide,
            pl.BlockSpec((keys, QUAD), lambda j: (0, j)),
            pl.BlockSpec((keys, QUAD), lambda j: (0, j)),
        ],
        name="cross_attend_back",
        cost_estimate=LIGHT,
    )(query, key, value, mixed, d_mixed, lse)


FF_STEP = 1024
FF_PART = 256


def ffn_kernel(n_ref, g_ref, wi_ref, wo_ref, *refs):
    act_ref, din_ref = refs[-2:]
    for part in range(wi_ref.shape[1] // FF_PART):
        cols = slice(part * FF_PART, (part + 1) * FF_PART)
        inner = mm(n_ref[...], wi_ref[:, cols], NN)
        d_act = mm(g_ref[...], wo_ref[:, cols], NN)
        phi = 0.5 + 0.5 * lax.erf(inner * (1.0 / math.sqrt(2.0)))
        bell = jnp.exp(inner * inner * -0.5) * (1.0 / math.sqrt(2.0 * math.pi))
        act_ref[:, cols] = (inner * phi).astype(BF)
        din_ref[:, cols] = (d_act * (phi + inner * bell)).astype(BF)


def ffn_middle(normed, grads, weights, block, blocks, kept=()):
    rows, width = normed.shape
    hidden = weights.shape[1] // 2
    steps = hidden // FF_STEP
    out_shape = jax.ShapeDtypeStruct((rows * blocks, hidden), BF)
    whole = pl.BlockSpec((rows, width), lambda j: (0, 0))
    out_spec = pl.BlockSpec((rows, FF_STEP), lambda j: (block, j))
    return pl.pallas_call(
        ffn_kernel,
        grid=(steps,),
        out_shape=(out_shape, out_shape),
        in_specs=[
            whole,
            whole,
            pl.BlockSpec((width, FF_STEP), lambda j: (0, j)),
            pl.BlockSpec((width, FF_STEP), lambda j: (0, steps + j)),
        ]
        + [pl.BlockSpec(memory_space=pl.ANY)] * len(kept),
        out_specs=[out_spec, out_spec],
        input_output_aliases={4 + i: i for i in range(len(kept))},
        name="ffn_middle",
        cost_estimate=LIGHT,
    )(normed, grads, weights, weights, *kept)


def stats_of(value):
    mean = jnp.mean(value, axis=-1, keepdims=True)
    centred = value - mean
    spread = jnp.mean(centred * centred, axis=-1, keepdims=True)
    return centred, lax.rsqrt(spread + EPS)


def norm_grad(value, gain, incoming):
    centred, scale = stats_of(value)
    hat = centred * scale
    scaled = incoming * gain
    mean = jnp.mean(scaled, axis=-1, keepdims=True)
    along = jnp.mean(scaled * hat, axis=-1, keepdims=True)
    return (
        scale * (scaled - mean - hat * along),
        jnp.sum(incoming * hat, axis=0),
        jnp.sum(incoming, axis=0),
    )


def on_pair(
    inputs,
    text_states,
    self_query,
    self_key,
    self_value,
    self_output,
    cross_query,
    cross_key,
    cross_value,
    cross_output,
    inner_weight,
    outer_weight,
    norm_gains,
    norm_shifts,
    cotangent,
    *,
    groups,
):
    rows, width = inputs.shape
    half = width // 2
    hidden = inner_weight.shape[1]
    shard = self_query.shape[0]
    tensor = lax.axis_index("tensor").astype(jnp.uint32)
    place = lax.axis_index("dp").astype(jnp.uint32)
    one = jnp.uint32(1)
    bits = [(place >> i) & one for i in range((groups - 1).bit_length())]
    mine, theirs = tensor * jnp.uint32(half), (tensor ^ one) * jnp.uint32(half)
    zero = jnp.uint32(0)
    lines = [[i + 4 * j for j in range(groups // 4)] for i in range(4)]
    t_ref = tensor.astype(jnp.int32).reshape(1)

    def peer(value):
        return lax.ppermute(value, "tensor", [(0, 1), (1, 0)])

    def gather(packed):
        return lax.all_gather(packed, "dp", axis=0, tiled=True)

    swaps = [[(i, i ^ (1 << level)) for i in range(groups)] for level in range(len(bits))]

    def swap(send, level):
        return lax.ppermute(send, "dp", swaps[level])

    def line_sum(whole):
        whole = whole.reshape(-1, whole.shape[-1])
        return lax.psum_scatter(
            whole, "dp", scatter_dimension=0, tiled=True, axis_index_groups=lines
        )

    def line_step(send, keep, ready):
        return fold(side_refs[3], (after(keep, ready), swap(send, 2)))

    def line_end(send, keep):
        for level in range(3, len(bits)):
            got = swap(send, level)
            if level + 1 < len(bits):
                send, keep = fold(side_refs[level + 1], (keep, got))
        return (keep.astype(F32) + got.astype(F32)).reshape(shard, -1)

    part = half // CUTS
    pieces = [slice(i * part, (i + 1) * part) for i in range(CUTS)]
    side_refs = [bit.astype(jnp.int32).reshape(1) for bit in bits]
    start_x, side_refs, mine, theirs, t_ref = lax.optimization_barrier(
        (inputs, side_refs, mine, theirs, t_ref)
    )
    cross_two = jnp.concatenate([cross_query, cross_output.T], axis=1)
    cross_peer = peer(cross_two)
    taken = [(which, p.start, p.stop, False) for p in pieces for which in range(3)]
    taken += [(3, 0, half, True), (4, 0, half, False), (5, 0, half, False)]
    taken += [(6, 0, half, False), (7, 0, half, False), (6, half, width, False), (7, half, width, False)]
    first = gather(
        pack(
            [self_query, self_key, self_value, self_output, cross_key, cross_value]
            + [cross_two, cross_peer],
            taken,
        )
    )
    second = gather(pack([inner_weight, outer_weight], [(0, 0, hidden, False), (1, 0, hidden, True)]))
    inputs_peer = peer(after(start_x, cross_peer))
    grads_peer = peer(after(cotangent, inputs_peer))
    w_qkv = first[:, : 3 * half]
    w_self_out = first[:, 3 * half : 4 * half]
    w_text = first[:, 4 * half : 6 * half]
    w_cross_query = first[:, 6 * half : 8 * half]
    w_cross_out = first[:, 8 * half :]
    w_inner = second[:, :hidden]
    w_outer = second[:, hidden:]

    start = jnp.concatenate([inputs, inputs_peer], axis=0).astype(F32)
    normed1 = norm_rows(start, norm_gains[0], norm_shifts[0]).astype(BF)
    text = text_states.reshape(-1, width)
    text_own = mm(text, w_text, NN).astype(BF)
    grads3 = jnp.concatenate([cotangent, grads_peer], axis=0)
    normed1 = after(normed1, grads3, text_own)
    qkv = mm(normed1, w_qkv, NN).astype(BF)
    text_peer = peer(text_own)
    mixed1, lse1 = self_forward(t_ref, qkv)
    away = peer(mm(mixed1[rows:], w_self_out, NT).astype(BF))
    home = mm(mixed1[:rows], w_self_out, NT)
    key2 = jnp.concatenate([text_own[:, :half], text_peer[:, :half]], axis=1)
    value2 = jnp.concatenate([text_own[:, half:], text_peer[:, half:]], axis=1)
    state1 = inputs.astype(F32) + home + away.astype(F32)

    normed2 = norm_rows(state1, norm_gains[1], norm_shifts[1]).astype(BF)
    query2 = mm(normed2, w_cross_query, NN).astype(BF)
    mixed2, lse2 = cross_forward(query2, key2, value2)
    state2 = state1 + mm(mixed2, w_cross_out, NT)

    normed3 = norm_rows(state2, norm_gains[2], norm_shifts[2]).astype(BF)
    normed3_peer = peer(normed3)
    active, d_inner = ffn_middle(normed3, cotangent, second, 0, 2)
    back3_home = product(d_inner, second, NT, F32, row=0, rows=rows)
    out_home = product(active, second, NT, F32, row=0, rows=rows, first=hidden)
    normed3_peer = after(normed3_peer, back3_home, out_home)
    active, d_inner = ffn_middle(normed3_peer, grads_peer, second, 1, 2, (active, d_inner))
    back3_part = product(d_inner, second, NT, BF, row=1, rows=rows)
    back3_away = peer(back3_part)
    d_outer = mm(after(grads3, back3_part), active, TN).astype(BF)
    outer_sum = lax.psum_scatter(d_outer, "dp", scatter_dimension=0, tiled=True)
    rows3 = jnp.concatenate([normed3, after(normed3_peer, d_outer)], axis=0)
    last = rows3

    def weight_core(left, right, first=0, size=None):
        nonlocal last
        send, keep = weight_halves(side_refs[0], after(left, last), right, shard, first, size)
        last = send
        return send, keep

    inner = weight_core(rows3, d_inner)
    inner_got = swap(inner[0], 0)

    back3_away = after(back3_away, last)
    grad2, g2, sums3 = norm_back_rows(
        state2, norm_gains[2], cotangent, [back3_home, back3_away], HEAVY
    )
    d_mixed2 = product(g2, first, NN, BF, first=8 * half, size=width)
    inner = fold(side_refs[1], (after(inner[1], d_mixed2), inner_got))
    inner_got = swap(inner[0], 1)
    d_mixed2 = after(d_mixed2, inner[0])
    d_query2, d_key2, d_value2 = cross_backward(query2, key2, value2, mixed2, d_mixed2, lse2)
    d_text_send = jnp.concatenate([d_key2[:, half:], d_value2[:, half:]], axis=1).astype(BF)
    d_text_keep = jnp.concatenate([d_key2[:, :half], d_value2[:, :half]], axis=1)
    d_text_peer = peer(d_text_send)
    back2 = product(after(d_query2, d_text_send), first, NT, F32, first=6 * half)
    grad1, g1, sums2 = norm_back_rows(state1, norm_gains[1], grad2, [back2])
    g1_peer = peer(g1)

    out_part = product(after(active, g1), second, NT, BF, row=1, rows=rows, first=hidden)
    last = out_part

    def two(left, right):
        found = [weight_core(left, right, i * half, half) for i in range(2)]
        return [(keep, swap(send, 0)) for send, keep in found]

    co_own, co_away = two(g2, mixed2)
    cq_own, cq_away = two(normed2, d_query2)
    d_text = (d_text_keep + after(d_text_peer, last).astype(F32)).astype(BF)
    kv = two(text, d_text)
    grads1 = jnp.concatenate([g1, after(g1_peer, last)], axis=0)
    d_mixed1 = product(grads1, first, NN, BF, first=3 * half, size=half)
    co_send = totals((after(co_away[0], d_mixed1), co_away[1]))
    co_got = peer(co_send)
    cq_send = totals((after(cq_away[0], co_send), cq_away[1]))
    cq_got = peer(cq_send)
    inner = fold(side_refs[2], (after(inner[1], cq_send), inner_got))
    found0 = self_backward(t_ref, qkv, mixed1, after(d_mixed1, inner[0], outer_sum), lse1, 0)
    text_terms = mm(after(d_text, found0), w_text, NT).astype(BF)
    text_keep, text_send = (
        lax.dynamic_slice(
            text_terms, (zero, at), (text_terms.shape[0], half), allow_negative_indices=False
        )
        for at in (mine, theirs)
    )

    text_got = peer(text_send)
    out_away = peer(after(out_part, found0))
    last = found0
    qkv0 = weight_core(normed1, found0)
    qkv0_got = swap(qkv0[0], 0)
    so = weight_core(grads1, mixed1)
    so_got = swap(so[0], 0)
    kv = fold(side_refs[1], *[(after(keep, last), got) for keep, got in kv])
    kv_got = swap(kv[0], 1)
    cross = fold(
        side_refs[1],
        (after(co_own[0], kv[0]), co_own[1], co_got),
        (cq_own[0], cq_own[1], cq_got),
    )
    cross_got = swap(cross[0], 1)
    inner_first = after(inner[1], cross[0]), swap(inner[0], 2)
    inner = fold(side_refs[3], inner_first, cost=HEAVY)
    most = fold(side_refs[1], (after(qkv0[1], inner[0]), qkv0_got), (so[1], so_got))
    most_got = swap(most[0], 1)
    kv = totals((after(kv[1], most[0]), kv_got))
    found1 = self_backward(t_ref, qkv, mixed1, after(d_mixed1, kv), lse1, 1)
    last = found1
    qkv1 = weight_core(normed1, found1)
    qkv1_got = swap(qkv1[0], 0)
    cross = totals((after(cross[1], qkv1[0]), cross_got), (kv,))
    cross_sum = line_sum(cross)
    most = fold(side_refs[2], (after(most[1], cross), most_got))
    back1_part = joint_product([found0, after(found1, most[0])], first, BF, 1, rows, HEAVY)
    back1_away = peer(back1_part)
    qkv1 = fold(side_refs[1], (after(qkv1[1], back1_part), qkv1_got))
    qkv1_got = swap(qkv1[0], 1)
    back1_home = joint_product([found0, after(found1, qkv1[0])], first, F32, 0, rows, LIGHT)
    most = line_step(*most, back1_home)
    sums0 = norm_sums(after(inputs_peer, most[0]), [back1_part])
    qkv1 = fold(side_refs[2], (after(qkv1[1], sums0), qkv1_got))
    sums1 = sums0 + norm_sums(after(inputs, qkv1[0], cross_sum), [back1_home])
    qkv1 = line_step(*qkv1, sums1)
    input_grad, _, _ = norm_back_rows(
        inputs, norm_gains[0], grad1, [back1_home, after(back1_away, qkv1[0])]
    )
    inner_sum = line_end(inner[0], after(inner[1], back1_home))
    most_sum, qkv1_sum = line_end(*most), line_end(*qkv1)
    qkv0_sum, so_sum = most_sum[:, : 3 * part], most_sum[:, 3 * part :]
    output = (state2 + out_home + after(out_away, last).astype(F32)).astype(BF)
    text_grad = text_keep.astype(F32) + after(text_got, last).astype(F32)
    text_grad = text_grad.reshape(1, -1, half)
    qkv_sums = [qkv0_sum, qkv1_sum]

    small = jnp.stack([v[i] for i in range(2) for v in (sums1, sums2, sums3)])
    small = after(small, back1_away)
    small = small + peer(small)
    bit = 1
    while bit < groups:
        small = small + lax.ppermute(small, "dp", [(i, i ^ bit) for i in range(groups)])
        bit *= 2

    def joined(kind):
        return jnp.concatenate([v[:, kind * part : (kind + 1) * part] for v in qkv_sums], axis=1)

    return (
        output,
        input_grad,
        text_grad,
        joined(0),
        joined(1),
        joined(2),
        so_sum.T,
        cross_sum[:, half : 2 * half].astype(F32),
        cross_sum[:, 2 * half : 3 * half].astype(F32),
        cross_sum[:, 3 * half :].astype(F32),
        cross_sum[:, :half].astype(F32).T,
        inner_sum.astype(F32),
        outer_sum.astype(F32).T,
        small[:3],
        small[3:],
    )


def pairs_up(mesh, inputs, text_states, inner_weight):
    groups, sides = mesh.shape["dp"], mesh.shape["tensor"]
    width = inputs.shape[1]
    return (
        sides == 2
        and groups >= 16
        and groups & (groups - 1) == 0
        and text_states.shape[0] == groups
        and text_states.shape[1] == TEXT
        and inputs.shape[0] == groups * LEN
        and width % (2 * QUAD) == 0
        and width % (2 * CUTS * PAIR) == 0
        and width % (32 * groups) in (0, 16 * groups)
        and inner_weight.shape[1] % (2 * FF_STEP) == 0
    )


def solution(mesh):
    in_specs = (
        P(("dp", "tensor"), None),
        P("dp", None, None),
        P("dp", "tensor"),
        P("dp", "tensor"),
        P("dp", "tensor"),
        P("tensor", "dp"),
        P("dp", "tensor"),
        P("dp", "tensor"),
        P("dp", "tensor"),
        P("tensor", "dp"),
        P("dp", "tensor"),
        P("tensor", "dp"),
        P(),
        P(),
        P(("dp", "tensor"), None),
    )
    out_specs = (
        P(("dp", "tensor"), None),
        P(("dp", "tensor"), None),
        P("dp", None, "tensor"),
        P("dp", "tensor"),
        P("dp", "tensor"),
        P("dp", "tensor"),
        P("tensor", "dp"),
        P("dp", "tensor"),
        P("dp", "tensor"),
        P("dp", "tensor"),
        P("tensor", "dp"),
        P("dp", "tensor"),
        P("tensor", "dp"),
        P(),
        P(),
    )

    def layer(*args):
        body = on_device
        if pairs_up(mesh, args[0], args[1], args[10]):
            body = partial(on_pair, groups=mesh.shape["dp"])
        return jax.shard_map(
            body, mesh=mesh, in_specs=in_specs, out_specs=out_specs, check_vma=False
        )(*args)

    return layer
```

```python
from functools import partial
import math

import jax
import jax.numpy as jnp
from jax import lax
from jax.experimental import pallas as pl
from jax.experimental.pallas import tpu as pltpu
from jax.sharding import PartitionSpec as P

HD = 64
TEXT = 64
LEN = 1024


EPS = 1e-05
MASKED = -1e30


def norm_rows(value, gain, shift):
    mean = jnp.mean(value, axis=-1, keepdims=True)
    centred = value - mean
    spread = jnp.mean(centred * centred, axis=-1, keepdims=True)
    return centred * lax.rsqrt(spread + EPS) * gain + shift


def norm_back(value, gain, shift, incoming):
    ignored, pullback = jax.vjp(norm_rows, value, gain, shift)
    return pullback(incoming)


def gelu_exact(value):
    return jax.nn.gelu(value, approximate=False)


def transposed_times(left, right):
    return lax.dot_general(
        left, right, (((0,), (0,)), ((), ())), preferred_element_type=jnp.float32
    )


def times_t(left, right):
    return lax.dot_general(
        left, right, (((1,), (1,)), ((), ())), preferred_element_type=jnp.float32
    )


def apply_projection(left, right):
    return jnp.dot(left, right, preferred_element_type=jnp.float32).astype(jnp.bfloat16)


def scores_of(query, key, masked):
    scale = 1.0 / math.sqrt(HD)
    scores = jnp.einsum("qhd,khd->hqk", query, key, preferred_element_type=jnp.float32) * scale
    if masked:
        places = jnp.arange(query.shape[0])
        allowed = places[:, None] >= places[None, :]
        scores = jnp.where(allowed[None], scores, MASKED)
    return scores


def attend(block, masked):
    query, key, value = block
    scores = scores_of(query, key, masked)
    highest = jnp.max(scores, axis=-1, keepdims=True)
    total = jnp.sum(jnp.exp(scores - highest), axis=-1, keepdims=True)
    log_total = highest + jnp.log(total)
    weights = jnp.exp(scores - log_total).astype(jnp.bfloat16)
    mixed = jnp.einsum("hqk,khd->qhd", weights, value, preferred_element_type=jnp.float32)
    return (mixed.astype(jnp.bfloat16), log_total)


def attend_back(block, masked):
    query, key, value, log_total, grad_mixed = block
    scale = 1.0 / math.sqrt(HD)
    weights = jnp.exp(scores_of(query, key, masked) - log_total)
    rounded = weights.astype(jnp.bfloat16)
    d_value = jnp.einsum("hqk,qhd->khd", rounded, grad_mixed, preferred_element_type=jnp.float32)
    d_weights = jnp.einsum("qhd,khd->hqk", grad_mixed, value, preferred_element_type=jnp.float32)
    centred = d_weights - jnp.sum(weights * d_weights, axis=-1, keepdims=True)
    d_scores = (weights * centred).astype(jnp.bfloat16)
    d_query = jnp.einsum("hqk,khd->qhd", d_scores, key, preferred_element_type=jnp.float32) * scale
    d_key = jnp.einsum("hqk,qhd->khd", d_scores, query, preferred_element_type=jnp.float32) * scale
    return (d_query.astype(jnp.bfloat16), d_key.astype(jnp.bfloat16), d_value.astype(jnp.bfloat16))


def spread_rows(normed):
    return lax.all_gather(normed, "tensor", axis=0, tiled=True)


def spread_grads(grad):
    return lax.all_gather(grad.astype(jnp.bfloat16), "tensor", axis=0, tiled=True)


def branch_total(mixed, weight):
    return lax.psum_scatter(
        jnp.dot(mixed, weight, preferred_element_type=jnp.float32),
        "tensor",
        scatter_dimension=0,
        tiled=True,
    )


def normalized_total(pairs):
    total = None
    for grad, weight in pairs:
        added = times_t(grad, weight)
        total = added if total is None else total + added
    return lax.psum_scatter(total, "tensor", scatter_dimension=0, tiled=True)


def on_device(
    inputs,
    text_states,
    self_query,
    self_key,
    self_value,
    self_output,
    cross_query,
    cross_key,
    cross_value,
    cross_output,
    inner_weight,
    outer_weight,
    norm_gains,
    norm_shifts,
    cotangent,
):
    (
        gathered_self_query,
        gathered_self_key,
        gathered_self_value,
        full_soutput,
        full_cquery,
        full_ckey,
        full_cvalue,
        full_coutput,
        full_inner,
        full_outer,
    ) = (
        lax.all_gather(self_query, "dp", axis=0, tiled=True),
        lax.all_gather(self_key, "dp", axis=0, tiled=True),
        lax.all_gather(self_value, "dp", axis=0, tiled=True),
        lax.all_gather(self_output, "dp", axis=1, tiled=True),
        lax.all_gather(cross_query, "dp", axis=0, tiled=True),
        lax.all_gather(cross_key, "dp", axis=0, tiled=True),
        lax.all_gather(cross_value, "dp", axis=0, tiled=True),
        lax.all_gather(cross_output, "dp", axis=1, tiled=True),
        lax.all_gather(inner_weight, "dp", axis=0, tiled=True),
        lax.all_gather(outer_weight, "dp", axis=1, tiled=True),
    )
    width = inputs.shape[1]
    clips = text_states.shape[0]
    local_heads = gathered_self_query.shape[1] // HD

    def heads(value, length):
        return value.reshape(clips, length, local_heads, HD)

    def flatten(value):
        return value.reshape(-1, local_heads * HD)

    start = inputs.astype(jnp.float32)
    first_rows = spread_rows(norm_rows(start, norm_gains[0], norm_shifts[0]).astype(jnp.bfloat16))
    query1 = apply_projection(first_rows, gathered_self_query)
    first_key = apply_projection(first_rows, gathered_self_key)
    value1 = apply_projection(first_rows, gathered_self_value)
    mixed1, lse1 = lax.map(
        partial(attend, masked=True),
        (heads(query1, LEN), heads(first_key, LEN), heads(value1, LEN)),
    )
    mixed1 = flatten(mixed1)
    state1 = start + branch_total(mixed1, full_soutput)
    rows2 = spread_rows(norm_rows(state1, norm_gains[1], norm_shifts[1]).astype(jnp.bfloat16))
    query2 = apply_projection(rows2, full_cquery)
    text_flat = text_states.reshape(-1, width)
    key2 = apply_projection(text_flat, full_ckey)
    value2 = apply_projection(text_flat, full_cvalue)
    mixed2, lse2 = lax.map(
        partial(attend, masked=False), (heads(query2, LEN), heads(key2, TEXT), heads(value2, TEXT))
    )
    mixed2 = flatten(mixed2)
    state2 = state1 + branch_total(mixed2, full_coutput)
    rows3 = spread_rows(norm_rows(state2, norm_gains[2], norm_shifts[2]).astype(jnp.bfloat16))
    inner = jnp.dot(rows3, full_inner, preferred_element_type=jnp.float32)
    active_float, gelu_pull = jax.vjp(gelu_exact, inner)
    active = active_float.astype(jnp.bfloat16)
    result = state2 + branch_total(active, full_outer)
    output = result.astype(jnp.bfloat16)
    grad3 = cotangent.astype(jnp.float32)
    grads_outer = spread_grads(grad3)
    d_outer = transposed_times(active, grads_outer)
    d_inner = gelu_pull(times_t(grads_outer, full_outer))[0].astype(jnp.bfloat16)
    d_innerw = transposed_times(rows3, d_inner)
    back3 = normalized_total(((d_inner, full_inner),))
    d_state2, gain_three, shift_three = norm_back(state2, norm_gains[2], norm_shifts[2], back3)
    grad2 = grad3 + d_state2
    grads_cross = spread_grads(grad2)
    d_coutput = transposed_times(mixed2, grads_cross)
    d_mixed2 = times_t(grads_cross, full_coutput).astype(jnp.bfloat16)
    d_query2, d_key2, d_value2 = lax.map(
        partial(attend_back, masked=False),
        (heads(query2, LEN), heads(key2, TEXT), heads(value2, TEXT), lse2, heads(d_mixed2, LEN)),
    )
    d_query2 = flatten(d_query2)
    d_key2 = flatten(d_key2)
    d_value2 = flatten(d_value2)
    d_cquery = transposed_times(rows2, d_query2)
    d_ckey = transposed_times(text_flat, d_key2)
    d_cvalue = transposed_times(text_flat, d_value2)
    text_terms = (times_t(d_key2, full_ckey) + times_t(d_value2, full_cvalue)).reshape(
        clips, TEXT, width
    )
    text_grad = lax.psum_scatter(
        text_terms.astype(jnp.bfloat16), "tensor", scatter_dimension=2, tiled=True
    ).astype(jnp.float32)
    back2 = normalized_total(((d_query2, full_cquery),))
    d_state1, gain_two, shift_two = norm_back(state1, norm_gains[1], norm_shifts[1], back2)
    grad1 = grad2 + d_state1
    grads_self = spread_grads(grad1)
    d_soutput = transposed_times(mixed1, grads_self)
    d_mixed1 = times_t(grads_self, full_soutput).astype(jnp.bfloat16)
    first_query_grad, first_key_grad, first_value_grad = lax.map(
        partial(attend_back, masked=True),
        (heads(query1, LEN), heads(first_key, LEN), heads(value1, LEN), lse1, heads(d_mixed1, LEN)),
    )
    first_query_grad = flatten(first_query_grad)
    first_key_grad = flatten(first_key_grad)
    first_value_grad = flatten(first_value_grad)
    d_squery = transposed_times(first_rows, first_query_grad)
    self_key_partial = transposed_times(first_rows, first_key_grad)
    d_svalue = transposed_times(first_rows, first_value_grad)
    first_backward = normalized_total(
        (
            (first_query_grad, gathered_self_query),
            (first_key_grad, gathered_self_key),
            (first_value_grad, gathered_self_value),
        )
    )
    d_start, gain_one, shift_one = norm_back(start, norm_gains[0], norm_shifts[0], first_backward)
    input_grad = grad1 + d_start
    gains_grad, shifts_grad = lax.psum(
        (
            jnp.stack([gain_one, gain_two, gain_three]),
            jnp.stack([shift_one, shift_two, shift_three]),
        ),
        ("dp", "tensor"),
    )
    summed = (
        lax.psum_scatter(
            d_squery.astype(jnp.bfloat16), "dp", scatter_dimension=0, tiled=True
        ).astype(jnp.float32),
        lax.psum_scatter(
            self_key_partial.astype(jnp.bfloat16), "dp", scatter_dimension=0, tiled=True
        ).astype(jnp.float32),
        lax.psum_scatter(
            d_svalue.astype(jnp.bfloat16), "dp", scatter_dimension=0, tiled=True
        ).astype(jnp.float32),
        lax.psum_scatter(
            d_soutput.astype(jnp.bfloat16), "dp", scatter_dimension=1, tiled=True
        ).astype(jnp.float32),
        lax.psum_scatter(
            d_cquery.astype(jnp.bfloat16), "dp", scatter_dimension=0, tiled=True
        ).astype(jnp.float32),
        lax.psum_scatter(d_ckey.astype(jnp.bfloat16), "dp", scatter_dimension=0, tiled=True).astype(
            jnp.float32
        ),
        lax.psum_scatter(
            d_cvalue.astype(jnp.bfloat16), "dp", scatter_dimension=0, tiled=True
        ).astype(jnp.float32),
        lax.psum_scatter(
            d_coutput.astype(jnp.bfloat16), "dp", scatter_dimension=1, tiled=True
        ).astype(jnp.float32),
        lax.psum_scatter(
            d_innerw.astype(jnp.bfloat16), "dp", scatter_dimension=0, tiled=True
        ).astype(jnp.float32),
        lax.psum_scatter(
            d_outer.astype(jnp.bfloat16), "dp", scatter_dimension=1, tiled=True
        ).astype(jnp.float32),
    )
    return (
        output,
        input_grad,
        text_grad,
        summed[0],
        summed[1],
        summed[2],
        summed[3],
        summed[4],
        summed[5],
        summed[6],
        summed[7],
        summed[8],
        summed[9],
        gains_grad,
        shifts_grad,
    )


BF = jnp.bfloat16
F32 = jnp.float32
NN = (((1,), (0,)), ((), ()))
NT = (((1,), (1,)), ((), ()))
TN = (((0,), (0,)), ((), ()))
QB = 256
PAIR = 128
QUAD = 256
CUTS = 2


def after(value, *ready):
    return lax.optimization_barrier((value,) + ready)[0]


def mm(left, right, dims):
    return lax.dot_general(left, right, dims, preferred_element_type=F32)


LIGHT = pl.CostEstimate(flops=1024, transcendentals=0, bytes_accessed=1024)
MIDDLE = pl.CostEstimate(flops=20_000_000_000, transcendentals=0, bytes_accessed=1024)
HEAVY = pl.CostEstimate(flops=10**15, transcendentals=0, bytes_accessed=1024)


def weight_kernel(side_ref, left_ref, right_ref, send_ref, keep_ref, *, shard):
    total = mm(left_ref[...], right_ref[...], TN).astype(BF)
    side = side_ref[0]
    for parity in range(2):
        even, odd = (keep_ref, send_ref) if parity == 0 else (send_ref, keep_ref)

        @pl.when(side == parity)
        def _():
            for at in range(total.shape[0] // shard):
                rows = total[at * shard : (at + 1) * shard, :]
                (odd if at % 2 else even)[at // 2] = rows


def weight_halves(side, left, right, shard, first=0, size=None):
    depth, width = left.shape
    size = size or right.shape[1]
    tile = next(t for t in (768, 1152, 512, 384, 256, 128) if size % t == 0 and first % t == 0)
    count = width // shard // 2
    shape = jax.ShapeDtypeStruct((count, shard, size), BF)
    out = pl.BlockSpec((count, shard, tile), lambda j, s: (0, 0, j))
    return pl.pallas_call(
        partial(weight_kernel, shard=shard),
        out_shape=(shape, shape),
        grid_spec=pltpu.PrefetchScalarGridSpec(
            num_scalar_prefetch=1,
            grid=(size // tile,),
            in_specs=[
                pl.BlockSpec((depth, width), lambda j, s: (0, 0)),
                pl.BlockSpec((depth, tile), lambda j, s: (0, first // tile + j)),
            ],
            out_specs=[out, out],
        ),
        name="weight_halves",
        cost_estimate=LIGHT,
    )(side, left, right)


def added(refs, at=slice(None)):
    total = refs[0][at].astype(F32)
    for ref in refs[1:]:
        total = total + ref[at].astype(F32)
    return total.astype(BF)


def pairs_per_step(count, row_bytes):
    while count > 1 and count % 2 == 0 and count * row_bytes > 5_000_000:
        count //= 2
    return count


def fold_kernel(side_ref, *refs, counts, inner):
    send_ref, keep_ref = refs[-2:]
    side = side_ref[0]
    first, at = 0, 0
    for count in counts:
        terms = refs[at : at + count]
        size = terms[0].shape[2]
        for pair in range(keep_ref.shape[0]):
            for out_ref, bit in ((send_ref, 1 - side), (keep_ref, side)):
                row = (2 * (pair // inner) + bit) * inner + pair % inner
                out_ref[pair, :, first : first + size] = added(terms, row)
        first, at = first + size, at + count


def fold(side, *groups, cost=None, inner=1):
    count, shard = groups[0][0].shape[0] // 2, groups[0][0].shape[1]
    sizes = [terms[0].shape[2] for terms in groups]
    row = sum(4 * shard * size * (len(terms) + 1) for size, terms in zip(sizes, groups))
    per = count if inner > 1 else pairs_per_step(count, row)
    shape = jax.ShapeDtypeStruct((count, shard, sum(sizes)), BF)
    spec = lambda size: pl.BlockSpec((2 * per, shard, size), lambda j, s: (j, 0, 0))
    part = pl.BlockSpec((per, shard, sum(sizes)), lambda j, s: (j, 0, 0))
    return pl.pallas_call(
        partial(fold_kernel, counts=[len(terms) for terms in groups], inner=inner),
        out_shape=(shape, shape),
        grid_spec=pltpu.PrefetchScalarGridSpec(
            num_scalar_prefetch=1,
            grid=(count // per,),
            in_specs=[spec(size) for size, terms in zip(sizes, groups) for _ in terms],
            out_specs=[part, part],
        ),
        name="fold",
        cost_estimate=cost or LIGHT,
    )(side, *[v for terms in groups for v in terms])


def totals_kernel(*refs, counts):
    out_ref = refs[-1]
    first, at = 0, 0
    for count in counts:
        size = refs[at].shape[2]
        out_ref[:, :, first : first + size] = added(refs[at : at + count])
        first, at = first + size, at + count


def totals(*groups):
    count, shard = groups[0][0].shape[:2]
    sizes = [terms[0].shape[2] for terms in groups]
    row = sum(2 * shard * size * (len(terms) + 1) for size, terms in zip(sizes, groups))
    per = pairs_per_step(count, row)
    spec = lambda size: pl.BlockSpec((per, shard, size), lambda j: (j, 0, 0))
    return pl.pallas_call(
        partial(totals_kernel, counts=[len(terms) for terms in groups]),
        grid=(count // per,),
        out_shape=jax.ShapeDtypeStruct((count, shard, sum(sizes)), BF),
        in_specs=[spec(size) for size, terms in zip(sizes, groups) for _ in terms],
        out_specs=spec(sum(sizes)),
        name="totals",
        cost_estimate=LIGHT,
    )(*[v for terms in groups for v in terms])


def pack_kernel(*refs, parts):
    out_ref = refs[-1]
    first = 0
    for which, begin, end, turned in parts:
        ref = refs[which]
        value = ref[begin:end, :].T if turned else ref[:, begin:end]
        out_ref[:, first : first + end - begin] = value
        first += end - begin


def pack(arrays, parts):
    shard = arrays[0].shape[0]
    return pl.pallas_call(
        partial(pack_kernel, parts=parts),
        out_shape=jax.ShapeDtypeStruct((shard, sum(end - begin for _, begin, end, _ in parts)), BF),
        name="pack",
        cost_estimate=LIGHT,
    )(*arrays)


def norm_sums_kernel(value_ref, *refs):
    sums_ref = refs[-1]
    incoming = refs[0][...].astype(F32)
    for ref in refs[1:-1]:
        incoming = incoming + ref[...].astype(F32)
    centred, scale = stats_of(value_ref[...].astype(F32))

    @pl.when(pl.program_id(0) == 0)
    def _():
        sums_ref[...] = jnp.zeros_like(sums_ref)

    sums_ref[0:1, :] += jnp.sum(incoming * (centred * scale), axis=0, keepdims=True)
    sums_ref[1:2, :] += jnp.sum(incoming, axis=0, keepdims=True)


def norm_sums(value, incoming):
    rows, width = value.shape
    tile = 256 if rows % 256 == 0 else 128
    spec = pl.BlockSpec((tile, width), lambda j: (j, 0))
    return pl.pallas_call(
        norm_sums_kernel,
        grid=(rows // tile,),
        out_shape=jax.ShapeDtypeStruct((8, width), F32),
        in_specs=[spec] * (1 + len(incoming)),
        out_specs=pl.BlockSpec((8, width), lambda j: (0, 0)),
        name="norm_sums",
        cost_estimate=LIGHT,
    )(value, *incoming)


def norm_back_kernel(value_ref, gain_ref, base_ref, *refs, parts):
    grad_ref, low_ref, sums_ref = refs[parts:]
    incoming = refs[0][...].astype(F32)
    for ref in refs[1:parts]:
        incoming = incoming + ref[...].astype(F32)
    centred, scale = stats_of(value_ref[...].astype(F32))
    hat = centred * scale
    scaled = incoming * gain_ref[...]
    mean = jnp.mean(scaled, axis=-1, keepdims=True)
    along = jnp.mean(scaled * hat, axis=-1, keepdims=True)
    grad = base_ref[...].astype(F32) + scale * (scaled - mean - hat * along)
    grad_ref[...] = grad
    low_ref[...] = grad.astype(BF)

    @pl.when(pl.program_id(0) == 0)
    def _():
        sums_ref[...] = jnp.zeros_like(sums_ref)

    sums_ref[0:1, :] += jnp.sum(incoming * hat, axis=0, keepdims=True)
    sums_ref[1:2, :] += jnp.sum(incoming, axis=0, keepdims=True)


def norm_back_rows(value, gain, base, incoming, cost=LIGHT):
    rows, width = value.shape
    tile = 256 if rows % 256 == 0 else 128
    spec = pl.BlockSpec((tile, width), lambda j: (j, 0))
    return pl.pallas_call(
        partial(norm_back_kernel, parts=len(incoming)),
        grid=(rows // tile,),
        out_shape=(
            jax.ShapeDtypeStruct((rows, width), F32),
            jax.ShapeDtypeStruct((rows, width), BF),
            jax.ShapeDtypeStruct((8, width), F32),
        ),
        in_specs=[spec, pl.BlockSpec((1, width), lambda j: (0, 0)), spec] + [spec] * len(incoming),
        out_specs=[spec, spec, pl.BlockSpec((8, width), lambda j: (0, 0))],
        name="norm_back",
        cost_estimate=cost,
    )(value, gain.reshape(1, width), base, *incoming)


def joint_kernel(*refs):
    right_ref, out_ref = refs[-2:]
    depth = refs[0].shape[1]
    total = None
    for i, ref in enumerate(refs[:-2]):
        term = mm(ref[...], right_ref[:, i * depth : (i + 1) * depth], NT)
        total = term if total is None else total + term
    out_ref[...] = total.astype(out_ref.dtype)


def joint_product(lefts, right, dtype, row, rows, cost):
    depth, size, tile = lefts[0].shape[1], right.shape[0], 512
    return pl.pallas_call(
        joint_kernel,
        grid=(size // tile,),
        out_shape=jax.ShapeDtypeStruct((rows, size), dtype),
        in_specs=[pl.BlockSpec((rows, depth), lambda j: (row, 0))] * len(lefts)
        + [pl.BlockSpec((tile, depth * len(lefts)), lambda j: (j, 0))],
        out_specs=pl.BlockSpec((rows, tile), lambda j: (0, j)),
        name="joint_product",
        cost_estimate=cost,
    )(*lefts, right)


def product_kernel(left_ref, right_ref, out_ref, *, dims):
    out_ref[...] = mm(left_ref[...], right_ref[...], dims).astype(out_ref.dtype)


def product(left, right, dims, dtype, row=0, rows=None, first=0, size=None, cost=LIGHT):
    rows = rows or left.shape[0]
    depth = left.shape[1]
    if dims is NN:
        size = size or right.shape[1]
        tile = next(t for t in (768, 512, 384, 256) if size % t == 0 and first % t == 0)
        right_spec = pl.BlockSpec((depth, tile), lambda j: (0, first // tile + j))
    else:
        size = right.shape[0]
        tile = 512
        right_spec = pl.BlockSpec((tile, depth), lambda j: (j, first // depth))
    return pl.pallas_call(
        partial(product_kernel, dims=dims),
        grid=(size // tile,),
        out_shape=jax.ShapeDtypeStruct((rows, size), dtype),
        in_specs=[pl.BlockSpec((rows, depth), lambda j: (row, 0)), right_spec],
        out_specs=pl.BlockSpec((rows, tile), lambda j: (0, j)),
        name="product",
        cost_estimate=cost,
    )(left, right)


def lanes_of(width, head):
    lane = lax.broadcasted_iota(jnp.int32, (1, width), 1)
    return (lane >= head * HD) & (lane < (head + 1) * HD)


def only(value, mask):
    return jnp.where(mask, value, jnp.zeros_like(value))


def pieces_of(block):
    start = block * QB
    found = [(0, start, False)] if block else []
    return found + [(start, start + QB, True)]


def causal():
    key = lax.broadcasted_iota(jnp.int32, (QB, QB), 0)
    place = lax.broadcasted_iota(jnp.int32, (QB, QB), 1)
    return key <= place


def to_places(t, ref, held, half):
    low = pl.multiple_of(t * half, half)
    high = pl.multiple_of((1 - t) * half, half)
    held[0:half, :] = ref[pl.ds(low, half), :]
    held[half : 2 * half, :] = ref[pl.ds(high, half), :]


def row_of(t, start, half):
    side = start // half
    base = (1 - t) * half if side else t * half
    return pl.multiple_of(base + start % half, QB)


def self_kernel(t_ref, q_ref, k_ref, v_ref, o_ref, lse_ref, qs, ks, vs):
    t = t_ref[0]
    length = q_ref.shape[0]
    half = length // 2
    for ref, held in ((q_ref, qs), (k_ref, ks), (v_ref, vs)):
        to_places(t, ref, held, half)
    allowed = causal()
    for block in range(length // QB):
        rows = slice(block * QB, (block + 1) * QB)
        query = qs[rows, :] * BF(0.125)
        mixed = []
        for head in range(2):
            mine = only(query, lanes_of(PAIR, head))
            parts = []
            for a, b, edge in pieces_of(block):
                score = mm(ks[a:b, :], mine, NT)
                parts.append(jnp.where(allowed, score, MASKED) if edge else score)
            top = jnp.max(parts[0], axis=0, keepdims=True)
            for part in parts[1:]:
                top = jnp.maximum(top, jnp.max(part, axis=0, keepdims=True))
            total, out = None, None
            for part, (a, b, edge) in zip(parts, pieces_of(block)):
                power = jnp.exp(part - top)
                added = jnp.sum(power, axis=0, keepdims=True)
                term = mm(vs[a:b, :], power.astype(BF), TN)
                total = added if total is None else total + added
                out = term if out is None else out + term
            lse_ref[0, head : head + 1, rows] = top + jnp.log(total)
            mixed.append(out[head * HD : (head + 1) * HD, :] / total)
        both = jnp.concatenate(mixed, axis=0)
        o_ref[pl.ds(row_of(t, block * QB, half), QB), :] = both.T.astype(BF)


def self_forward(t, qkv):
    length, width = qkv.shape
    pairs = width // (3 * PAIR)
    cut = pairs // CUTS
    spec = lambda part: pl.BlockSpec(
        (length, PAIR), lambda j, r: (0, (3 * (j // cut) + part) * cut + j % cut)
    )
    return pl.pallas_call(
        self_kernel,
        out_shape=(
            jax.ShapeDtypeStruct((length, pairs * PAIR), BF),
            jax.ShapeDtypeStruct((pairs, 8, length), F32),
        ),
        grid_spec=pltpu.PrefetchScalarGridSpec(
            num_scalar_prefetch=1,
            grid=(pairs,),
            in_specs=[spec(0), spec(1), spec(2)],
            out_specs=[
                pl.BlockSpec((length, PAIR), lambda j, s: (0, j)),
                pl.BlockSpec((1, 8, length), lambda j, s: (j, 0, 0)),
            ],
            scratch_shapes=[pltpu.VMEM((length, PAIR), BF)] * 3,
        ),
        name="self_attend",
        cost_estimate=LIGHT,
    )(t, qkv, qkv, qkv)


def self_back_kernel(
    t_ref, q_ref, k_ref, v_ref, o_ref, do_ref, lse_ref, out_ref, qs, ks, vs, os, dos, dk, dv, dkb, dvb
):
    t = t_ref[0]
    length = q_ref.shape[0]
    half = length // 2
    step = pl.program_id(1)

    @pl.when(step == 0)
    def _():
        for ref, held in ((q_ref, qs), (k_ref, ks), (v_ref, vs), (o_ref, os), (do_ref, dos)):
            to_places(t, ref, held, half)
        allowed = causal()
        blocks = length // QB
        for block in reversed(range(blocks)):
            rows = slice(block * QB, (block + 1) * QB)
            query = qs[rows, :] * BF(0.125)
            grad = dos[rows, :]
            product = (grad.astype(F32) * os[rows, :].astype(F32)).T
            mine = [only(query, lanes_of(PAIR, head)) for head in range(2)]
            mine_grad = [only(grad, lanes_of(PAIR, head)) for head in range(2)]
            both_query = jnp.concatenate(mine, axis=0)
            both_grad = jnp.concatenate(mine_grad, axis=0)
            d_query = [None, None]
            for a, b, edge in pieces_of(block):
                weights, d_scores = [], []
                for head in range(2):
                    drop = jnp.sum(product[head * HD : (head + 1) * HD, :], axis=0, keepdims=True)
                    score = mm(ks[a:b, :], mine[head], NT)
                    power = jnp.exp(score - lse_ref[0, head : head + 1, rows])
                    if edge:
                        power = jnp.where(allowed, power, 0.0)
                    d_power = mm(vs[a:b, :], mine_grad[head], NT)
                    d_score = (power * (d_power - drop)).astype(BF)
                    weights.append(power.astype(BF))
                    d_scores.append(d_score)
                    term = mm(ks[a:b, :], d_score, TN)
                    d_query[head] = term if d_query[head] is None else d_query[head] + term
                add_v = mm(jnp.concatenate(weights, axis=1), both_grad, NN)
                add_k = mm(jnp.concatenate(d_scores, axis=1), both_query, NN)
                if block == blocks - 1:
                    dv[a:b, :] = add_v
                    dk[a:b, :] = add_k
                else:
                    dv[a:b, :] += add_v
                    dk[a:b, :] += add_k
            both = jnp.concatenate([d_query[0][:HD, :], d_query[1][HD:, :]], axis=0) * 0.125
            out_ref[pl.ds(row_of(t, block * QB, half), QB), :] = both.T.astype(BF)
        for block in range(blocks):
            rows = slice(block * QB, (block + 1) * QB)
            place = row_of(t, block * QB, half)
            dkb[pl.ds(place, QB), :] = dk[rows, :].astype(BF)
            dvb[pl.ds(place, QB), :] = dv[rows, :].astype(BF)

    @pl.when(step == 1)
    def _():
        out_ref[...] = dkb[...]

    @pl.when(step == 2)
    def _():
        out_ref[...] = dvb[...]


def self_backward(t, qkv, mixed, d_mixed, lse, part, cost):
    length, width = qkv.shape[0], qkv.shape[1] // CUTS
    pairs = width // (3 * PAIR)
    first = part * pairs
    spec = lambda kind: pl.BlockSpec(
        (length, PAIR), lambda j, s, r: (0, 3 * first + kind * pairs + j)
    )
    return pl.pallas_call(
        self_back_kernel,
        out_shape=jax.ShapeDtypeStruct((length, width), BF),
        grid_spec=pltpu.PrefetchScalarGridSpec(
            num_scalar_prefetch=1,
            grid=(pairs, 3),
            in_specs=[
                spec(0),
                spec(1),
                spec(2),
                pl.BlockSpec((length, PAIR), lambda j, s, r: (0, first + j)),
                pl.BlockSpec((length, PAIR), lambda j, s, r: (0, first + j)),
                pl.BlockSpec((1, 8, length), lambda j, s, r: (first + j, 0, 0)),
            ],
            out_specs=pl.BlockSpec((length, PAIR), lambda j, s, r: (0, s * pairs + j)),
            scratch_shapes=[pltpu.VMEM((length, PAIR), BF)] * 5
            + [pltpu.VMEM((length, PAIR), F32)] * 2
            + [pltpu.VMEM((length, PAIR), BF)] * 2,
        ),
        name="self_attend_back",
        cost_estimate=cost,
    )(t, qkv, qkv, qkv, mixed, d_mixed, lse)


def spread_heads(value):
    count = QUAD // HD
    return jnp.concatenate([only(value, lanes_of(QUAD, head)) for head in range(count)], axis=0)


def cross_kernel(q_ref, k_ref, v_ref, o_ref, lse_ref):
    keys = k_ref.shape[0]
    scores = mm(spread_heads(k_ref[...] * BF(0.125)), q_ref[...], NT)
    powers, totals = [], []
    for head in range(QUAD // HD):
        score = scores[head * keys : (head + 1) * keys, :]
        top = jnp.max(score, axis=0, keepdims=True)
        power = jnp.exp(score - top)
        total = jnp.sum(power, axis=0, keepdims=True)
        lse_ref[0, head : head + 1, :] = top + jnp.log(total)
        powers.append(power.astype(BF))
        totals.append(total)
    mixed = mm(spread_heads(v_ref[...]), jnp.concatenate(powers, axis=0), TN)
    scaled = [
        mixed[head * HD : (head + 1) * HD, :] / totals[head] for head in range(QUAD // HD)
    ]
    o_ref[...] = jnp.concatenate(scaled, axis=0).T.astype(BF)


def cross_specs(rows, keys, quads):
    return [
        pl.BlockSpec((rows, QUAD), lambda j: (0, j)),
        pl.BlockSpec((keys, QUAD), lambda j: (0, j)),
        pl.BlockSpec((keys, QUAD), lambda j: (0, j)),
    ]


def cross_forward(query, key, value):
    rows, width = query.shape
    keys = key.shape[0]
    quads = width // QUAD
    return pl.pallas_call(
        cross_kernel,
        grid=(quads,),
        out_shape=(
            jax.ShapeDtypeStruct((rows, width), BF),
            jax.ShapeDtypeStruct((quads, 8, rows), F32),
        ),
        in_specs=cross_specs(rows, keys, quads),
        out_specs=[
            pl.BlockSpec((rows, QUAD), lambda j: (0, j)),
            pl.BlockSpec((1, 8, rows), lambda j: (j, 0, 0)),
        ],
        name="cross_attend",
        cost_estimate=LIGHT,
    )(query, key, value)


def cross_back_kernel(q_ref, k_ref, v_ref, o_ref, do_ref, lse_ref, dq_ref, dk_ref, dv_ref):
    keys = k_ref.shape[0]
    count = QUAD // HD
    query, grad = q_ref[...], do_ref[...]
    key = spread_heads(k_ref[...] * BF(0.125))
    scores = mm(key, query, NT)
    d_powers = mm(spread_heads(v_ref[...]), grad, NT)
    product = (grad.astype(F32) * o_ref[...].astype(F32)).T
    weights, d_scores = [], []
    for head in range(count):
        group = slice(head * keys, (head + 1) * keys)
        drop = jnp.sum(product[head * HD : (head + 1) * HD, :], axis=0, keepdims=True)
        power = jnp.exp(scores[group, :] - lse_ref[0, head : head + 1, :])
        weights.append(power.astype(BF))
        d_scores.append((power * (d_powers[group, :] - drop)).astype(BF))
    weights = jnp.concatenate(weights, axis=0)
    d_scores = jnp.concatenate(d_scores, axis=0)
    dq_ref[...] = mm(key, d_scores, TN).T.astype(BF)
    d_key = mm(d_scores, query, NN)
    d_value = mm(weights, grad, NN)
    for ref, found, scale in ((dk_ref, d_key, 0.125), (dv_ref, d_value, 1.0)):
        total = None
        for head in range(count):
            term = only(found[head * keys : (head + 1) * keys, :], lanes_of(QUAD, head))
            total = term if total is None else total + term
        ref[...] = total * scale


def cross_backward(query, key, value, mixed, d_mixed, lse):
    rows, width = query.shape
    keys = key.shape[0]
    quads = width // QUAD
    wide = pl.BlockSpec((rows, QUAD), lambda j: (0, j))
    return pl.pallas_call(
        cross_back_kernel,
        grid=(quads,),
        out_shape=(
            jax.ShapeDtypeStruct((rows, width), BF),
            jax.ShapeDtypeStruct((keys, width), F32),
            jax.ShapeDtypeStruct((keys, width), F32),
        ),
        in_specs=cross_specs(rows, keys, quads)
        + [wide, wide, pl.BlockSpec((1, 8, rows), lambda j: (j, 0, 0))],
        out_specs=[
            wide,
            pl.BlockSpec((keys, QUAD), lambda j: (0, j)),
            pl.BlockSpec((keys, QUAD), lambda j: (0, j)),
        ],
        name="cross_attend_back",
        cost_estimate=LIGHT,
    )(query, key, value, mixed, d_mixed, lse)


FF_STEP = 1024
FF_PART = 256


def ffn_kernel(n_ref, g_ref, wi_ref, wo_ref, *refs):
    act_ref, din_ref = refs[-2:]
    for part in range(wi_ref.shape[1] // FF_PART):
        cols = slice(part * FF_PART, (part + 1) * FF_PART)
        inner = mm(n_ref[...], wi_ref[:, cols], NN)
        d_act = mm(g_ref[...], wo_ref[:, cols], NN)
        phi = 0.5 + 0.5 * lax.erf(inner * (1.0 / math.sqrt(2.0)))
        bell = jnp.exp(inner * inner * -0.5) * (1.0 / math.sqrt(2.0 * math.pi))
        act_ref[:, cols] = (inner * phi).astype(BF)
        din_ref[:, cols] = (d_act * (phi + inner * bell)).astype(BF)


def ffn_middle(normed, grads, weights, block, blocks, kept=()):
    rows, width = normed.shape
    hidden = weights.shape[1] // 2
    steps = hidden // FF_STEP
    out_shape = jax.ShapeDtypeStruct((rows * blocks, hidden), BF)
    whole = pl.BlockSpec((rows, width), lambda j: (0, 0))
    out_spec = pl.BlockSpec((rows, FF_STEP), lambda j: (block, j))
    return pl.pallas_call(
        ffn_kernel,
        grid=(steps,),
        out_shape=(out_shape, out_shape),
        in_specs=[
            whole,
            whole,
            pl.BlockSpec((width, FF_STEP), lambda j: (0, j)),
            pl.BlockSpec((width, FF_STEP), lambda j: (0, steps + j)),
        ]
        + [pl.BlockSpec(memory_space=pl.ANY)] * len(kept),
        out_specs=[out_spec, out_spec],
        input_output_aliases={4 + i: i for i in range(len(kept))},
        name="ffn_middle",
        cost_estimate=LIGHT,
    )(normed, grads, weights, weights, *kept)


def stats_of(value):
    mean = jnp.mean(value, axis=-1, keepdims=True)
    centred = value - mean
    spread = jnp.mean(centred * centred, axis=-1, keepdims=True)
    return centred, lax.rsqrt(spread + EPS)


def norm_grad(value, gain, incoming):
    centred, scale = stats_of(value)
    hat = centred * scale
    scaled = incoming * gain
    mean = jnp.mean(scaled, axis=-1, keepdims=True)
    along = jnp.mean(scaled * hat, axis=-1, keepdims=True)
    return (
        scale * (scaled - mean - hat * along),
        jnp.sum(incoming * hat, axis=0),
        jnp.sum(incoming, axis=0),
    )


def on_pair(
    inputs,
    text_states,
    self_query,
    self_key,
    self_value,
    self_output,
    cross_query,
    cross_key,
    cross_value,
    cross_output,
    inner_weight,
    outer_weight,
    norm_gains,
    norm_shifts,
    cotangent,
    *,
    groups,
):
    rows, width = inputs.shape
    half = width // 2
    hidden = inner_weight.shape[1]
    shard = self_query.shape[0]
    tensor = lax.axis_index("tensor").astype(jnp.uint32)
    place = lax.axis_index("dp").astype(jnp.uint32)
    one = jnp.uint32(1)
    bits = [(place >> i) & one for i in range((groups - 1).bit_length())]
    mine, theirs = tensor * jnp.uint32(half), (tensor ^ one) * jnp.uint32(half)
    zero = jnp.uint32(0)
    lines = [[i + 4 * j for j in range(groups // 4)] for i in range(4)]
    t_ref = tensor.astype(jnp.int32).reshape(1)

    def peer(value):
        return lax.ppermute(value, "tensor", [(0, 1), (1, 0)])

    def gather(packed):
        return lax.all_gather(packed, "dp", axis=0, tiled=True)

    swaps = [[(i, i ^ (1 << level)) for i in range(groups)] for level in range(len(bits))]

    def swap(send, level):
        return lax.ppermute(send, "dp", swaps[level])

    def line_sum(whole):
        whole = whole.reshape(-1, whole.shape[-1])
        return lax.psum_scatter(
            whole, "dp", scatter_dimension=0, tiled=True, axis_index_groups=lines
        )

    def line_step(send, keep, ready):
        return fold(side_refs[3], (after(keep, ready), swap(send, 2)))

    def line_end(send, keep):
        for level in range(3, len(bits)):
            got = swap(send, level)
            if level + 1 < len(bits):
                send, keep = fold(side_refs[level + 1], (keep, got))
        return (keep.astype(F32) + got.astype(F32)).reshape(shard, -1)

    part = half // CUTS
    pieces = [slice(i * part, (i + 1) * part) for i in range(CUTS)]
    side_refs = [bit.astype(jnp.int32).reshape(1) for bit in bits]
    start_x, side_refs, mine, theirs, t_ref = lax.optimization_barrier(
        (inputs, side_refs, mine, theirs, t_ref)
    )
    cross_two = jnp.concatenate([cross_query, cross_output.T], axis=1)
    cross_peer = peer(cross_two)
    taken = [(which, p.start, p.stop, False) for p in pieces for which in range(3)]
    taken += [(3, 0, half, True), (4, 0, half, False), (5, 0, half, False)]
    taken += [(6, 0, half, False), (7, 0, half, False), (6, half, width, False), (7, half, width, False)]
    first = gather(
        pack(
            [self_query, self_key, self_value, self_output, cross_key, cross_value]
            + [cross_two, cross_peer],
            taken,
        )
    )
    second = gather(pack([inner_weight, outer_weight], [(0, 0, hidden, False), (1, 0, hidden, True)]))
    inputs_peer = peer(after(start_x, cross_peer))
    grads_peer = peer(after(cotangent, inputs_peer))
    w_qkv = first[:, : 3 * half]
    w_self_out = first[:, 3 * half : 4 * half]
    w_text = first[:, 4 * half : 6 * half]
    w_cross_query = first[:, 6 * half : 8 * half]
    w_cross_out = first[:, 8 * half :]
    w_inner = second[:, :hidden]
    w_outer = second[:, hidden:]

    start = jnp.concatenate([inputs, inputs_peer], axis=0).astype(F32)
    normed1 = norm_rows(start, norm_gains[0], norm_shifts[0]).astype(BF)
    text = text_states.reshape(-1, width)
    text_own = mm(text, w_text, NN).astype(BF)
    grads3 = jnp.concatenate([cotangent, grads_peer], axis=0)
    normed1 = after(normed1, grads3, text_own)
    qkv = mm(normed1, w_qkv, NN).astype(BF)
    text_peer = peer(text_own)
    mixed1, lse1 = self_forward(t_ref, qkv)
    away = peer(mm(mixed1[rows:], w_self_out, NT).astype(BF))
    home = mm(mixed1[:rows], w_self_out, NT)
    key2 = jnp.concatenate([text_own[:, :half], text_peer[:, :half]], axis=1)
    value2 = jnp.concatenate([text_own[:, half:], text_peer[:, half:]], axis=1)
    state1 = inputs.astype(F32) + home + away.astype(F32)

    normed2 = norm_rows(state1, norm_gains[1], norm_shifts[1]).astype(BF)
    query2 = mm(normed2, w_cross_query, NN).astype(BF)
    mixed2, lse2 = cross_forward(query2, key2, value2)
    state2 = state1 + mm(mixed2, w_cross_out, NT)

    normed3 = norm_rows(state2, norm_gains[2], norm_shifts[2]).astype(BF)
    normed3_peer = peer(normed3)
    active, d_inner = ffn_middle(normed3, cotangent, second, 0, 2)
    back3_home = product(d_inner, second, NT, F32, row=0, rows=rows)
    out_home = product(active, second, NT, F32, row=0, rows=rows, first=hidden)
    normed3_peer = after(normed3_peer, back3_home, out_home)
    active, d_inner = ffn_middle(normed3_peer, grads_peer, second, 1, 2, (active, d_inner))
    back3_part = product(d_inner, second, NT, BF, row=1, rows=rows)
    back3_away = peer(back3_part)
    d_outer = mm(after(grads3, back3_part), active, TN).astype(BF)
    outer_sum = lax.psum_scatter(d_outer, "dp", scatter_dimension=0, tiled=True)
    rows3 = jnp.concatenate([normed3, after(normed3_peer, d_outer)], axis=0)
    last = rows3

    def weight_core(left, right, first=0, size=None):
        nonlocal last
        send, keep = weight_halves(side_refs[0], after(left, last), right, shard, first, size)
        last = send
        return send, keep

    inner = weight_core(rows3, d_inner)
    inner_got = swap(inner[0], 0)

    back3_away = after(back3_away, last)
    grad2, g2, sums3 = norm_back_rows(
        state2, norm_gains[2], cotangent, [back3_home, back3_away], HEAVY
    )
    d_mixed2 = product(g2, first, NN, BF, first=8 * half, size=width)
    inner = fold(side_refs[1], (after(inner[1], d_mixed2), inner_got))
    inner_got = swap(inner[0], 1)
    d_mixed2 = after(d_mixed2, inner[0])
    d_query2, d_key2, d_value2 = cross_backward(query2, key2, value2, mixed2, d_mixed2, lse2)
    d_text_send = jnp.concatenate([d_key2[:, half:], d_value2[:, half:]], axis=1).astype(BF)
    d_text_keep = jnp.concatenate([d_key2[:, :half], d_value2[:, :half]], axis=1)
    d_text_peer = peer(d_text_send)
    back2 = product(after(d_query2, d_text_send), first, NT, F32, first=6 * half)
    grad1, g1, sums2 = norm_back_rows(state1, norm_gains[1], grad2, [back2])
    d_text = (d_text_keep + after(d_text_peer, g1).astype(F32)).astype(BF)
    g1_peer = peer(after(g1, d_text))

    out_part = product(after(active, g1), second, NT, BF, row=1, rows=rows, first=hidden)
    last = out_part

    def two(left, right):
        found = [weight_core(left, right, i * half, half) for i in range(2)]
        return [(keep, swap(send, 0)) for send, keep in found]

    co_own, co_away = two(g2, mixed2)
    cq_own, cq_away = two(normed2, d_query2)
    co_send = totals((after(co_away[0], last), co_away[1]))
    co_got = peer(co_send)
    cq_send = totals((after(cq_away[0], co_send), cq_away[1]))
    cq_got = peer(cq_send)
    last = cq_send
    grads1 = jnp.concatenate([g1, after(g1_peer, last)], axis=0)
    d_mixed1 = product(grads1, first, NN, BF, first=3 * half, size=half)
    found0 = self_backward(t_ref, qkv, mixed1, d_mixed1, lse1, 0, LIGHT)
    text_terms = mm(after(d_text, found0), w_text, NT).astype(BF)
    text_keep, text_send = (
        lax.dynamic_slice(
            text_terms, (zero, at), (text_terms.shape[0], half), allow_negative_indices=False
        )
        for at in (mine, theirs)
    )

    text_got = peer(text_send)
    out_away = peer(after(out_part, found0))
    inner = fold(side_refs[2], (after(inner[1], found0, outer_sum), inner_got))
    last = inner[0]
    qkv0 = weight_core(normed1, found0)
    qkv0_got = swap(qkv0[0], 0)
    so = weight_core(grads1, mixed1)
    so_got = swap(so[0], 0)
    kv = two(text, d_text)
    cross = fold(
        side_refs[1],
        (after(co_own[0], last), co_own[1], co_got),
        (cq_own[0], cq_own[1], cq_got),
    )
    cross_got = swap(cross[0], 1)
    inner_first = after(inner[1], cross[0]), swap(inner[0], 2)
    inner = fold(side_refs[3], inner_first, cost=HEAVY)
    most = fold(
        side_refs[2], (after(qkv0[1], inner[0]), qkv0_got), (so[1], so_got), inner=2
    )
    most_got = swap(most[0], 2)
    kv = fold(side_refs[1], *[(after(keep, most[0]), got) for keep, got in kv])
    kv_got = swap(kv[0], 1)
    found1 = self_backward(t_ref, qkv, mixed1, after(d_mixed1, kv[0]), lse1, 1, MIDDLE)
    last = found1
    qkv1 = weight_core(normed1, found1)
    qkv1_got = swap(qkv1[0], 0)
    cross = totals((after(cross[1], qkv1[0]), cross_got), (kv[1], kv_got))
    cross_sum = line_sum(cross)
    most = fold(side_refs[3], (after(most[1], cross), most_got), inner=2)
    most_got = swap(most[0], 3)
    back1_part = joint_product([found0, after(found1, most[0])], first, BF, 1, rows, HEAVY)
    back1_away = peer(back1_part)
    qkv1 = fold(side_refs[1], (after(qkv1[1], back1_part), qkv1_got))
    qkv1_got = swap(qkv1[0], 1)
    back1_home = joint_product([found0, after(found1, qkv1[0])], first, F32, 0, rows, LIGHT)
    most = fold(side_refs[1], (after(most[1], back1_home), most_got))
    most_got = swap(most[0], 1)
    sums0 = norm_sums(after(inputs_peer, most[0]), [back1_part])
    qkv1 = fold(side_refs[2], (after(qkv1[1], sums0), qkv1_got))
    sums1 = sums0 + norm_sums(after(inputs, qkv1[0], cross_sum), [back1_home])
    qkv1 = line_step(*qkv1, sums1)
    input_grad, _, _ = norm_back_rows(
        inputs, norm_gains[0], grad1, [back1_home, after(back1_away, qkv1[0])]
    )
    inner_sum = line_end(inner[0], after(inner[1], back1_home))
    most_sum = (most[1].astype(F32) + most_got.astype(F32)).reshape(shard, -1)
    qkv1_sum = line_end(*qkv1)
    qkv0_sum, so_sum = most_sum[:, : 3 * part], most_sum[:, 3 * part :]
    output = (state2 + out_home + after(out_away, last).astype(F32)).astype(BF)
    text_grad = text_keep.astype(F32) + after(text_got, last).astype(F32)
    text_grad = text_grad.reshape(1, -1, half)
    qkv_sums = [qkv0_sum, qkv1_sum]

    small = jnp.stack([v[i] for i in range(2) for v in (sums1, sums2, sums3)])
    small = after(small, back1_away)
    small = small + peer(small)
    bit = 1
    while bit < groups:
        small = small + lax.ppermute(small, "dp", [(i, i ^ bit) for i in range(groups)])
        bit *= 2

    def joined(kind):
        return jnp.concatenate([v[:, kind * part : (kind + 1) * part] for v in qkv_sums], axis=1)

    return (
        output,
        input_grad,
        text_grad,
        joined(0),
        joined(1),
        joined(2),
        so_sum.T,
        cross_sum[:, half : 2 * half].astype(F32),
        cross_sum[:, 2 * half : 3 * half].astype(F32),
        cross_sum[:, 3 * half :].astype(F32),
        cross_sum[:, :half].astype(F32).T,
        inner_sum.astype(F32),
        outer_sum.astype(F32).T,
        small[:3],
        small[3:],
    )


def pairs_up(mesh, inputs, text_states, inner_weight):
    groups, sides = mesh.shape["dp"], mesh.shape["tensor"]
    width = inputs.shape[1]
    return (
        sides == 2
        and groups == 16
        and text_states.shape[0] == groups
        and text_states.shape[1] == TEXT
        and inputs.shape[0] == groups * LEN
        and width % (2 * QUAD) == 0
        and width % (2 * CUTS * PAIR) == 0
        and width % (32 * groups) in (0, 16 * groups)
        and inner_weight.shape[1] % (2 * FF_STEP) == 0
    )


def solution(mesh):
    in_specs = (
        P(("dp", "tensor"), None),
        P("dp", None, None),
        P("dp", "tensor"),
        P("dp", "tensor"),
        P("dp", "tensor"),
        P("tensor", "dp"),
        P("dp", "tensor"),
        P("dp", "tensor"),
        P("dp", "tensor"),
        P("tensor", "dp"),
        P("dp", "tensor"),
        P("tensor", "dp"),
        P(),
        P(),
        P(("dp", "tensor"), None),
    )
    out_specs = (
        P(("dp", "tensor"), None),
        P(("dp", "tensor"), None),
        P("dp", None, "tensor"),
        P("dp", "tensor"),
        P("dp", "tensor"),
        P("dp", "tensor"),
        P("tensor", "dp"),
        P("dp", "tensor"),
        P("dp", "tensor"),
        P("dp", "tensor"),
        P("tensor", "dp"),
        P("dp", "tensor"),
        P("tensor", "dp"),
        P(),
        P(),
    )

    def layer(*args):
        body = on_device
        if pairs_up(mesh, args[0], args[1], args[10]):
            body = partial(on_pair, groups=mesh.shape["dp"])
        return jax.shard_map(
            body, mesh=mesh, in_specs=in_specs, out_specs=out_specs, check_vma=False
        )(*args)

    return layer
```

```python
from functools import partial
import math

import jax
import jax.numpy as jnp
from jax import lax
from jax.experimental import pallas as pl
from jax.experimental.pallas import tpu as pltpu
from jax.sharding import PartitionSpec as P

HD = 64
TEXT = 64
LEN = 1024


EPS = 1e-05
MASKED = -1e30


def norm_rows(value, gain, shift):
    mean = jnp.mean(value, axis=-1, keepdims=True)
    centred = value - mean
    spread = jnp.mean(centred * centred, axis=-1, keepdims=True)
    return centred * lax.rsqrt(spread + EPS) * gain + shift


def norm_back(value, gain, shift, incoming):
    ignored, pullback = jax.vjp(norm_rows, value, gain, shift)
    return pullback(incoming)


def gelu_exact(value):
    return jax.nn.gelu(value, approximate=False)


def transposed_times(left, right):
    return lax.dot_general(
        left, right, (((0,), (0,)), ((), ())), preferred_element_type=jnp.float32
    )


def times_t(left, right):
    return lax.dot_general(
        left, right, (((1,), (1,)), ((), ())), preferred_element_type=jnp.float32
    )


def apply_projection(left, right):
    return jnp.dot(left, right, preferred_element_type=jnp.float32).astype(jnp.bfloat16)


def scores_of(query, key, masked):
    scale = 1.0 / math.sqrt(HD)
    scores = jnp.einsum("qhd,khd->hqk", query, key, preferred_element_type=jnp.float32) * scale
    if masked:
        places = jnp.arange(query.shape[0])
        allowed = places[:, None] >= places[None, :]
        scores = jnp.where(allowed[None], scores, MASKED)
    return scores


def attend(block, masked):
    query, key, value = block
    scores = scores_of(query, key, masked)
    highest = jnp.max(scores, axis=-1, keepdims=True)
    total = jnp.sum(jnp.exp(scores - highest), axis=-1, keepdims=True)
    log_total = highest + jnp.log(total)
    weights = jnp.exp(scores - log_total).astype(jnp.bfloat16)
    mixed = jnp.einsum("hqk,khd->qhd", weights, value, preferred_element_type=jnp.float32)
    return (mixed.astype(jnp.bfloat16), log_total)


def attend_back(block, masked):
    query, key, value, log_total, grad_mixed = block
    scale = 1.0 / math.sqrt(HD)
    weights = jnp.exp(scores_of(query, key, masked) - log_total)
    rounded = weights.astype(jnp.bfloat16)
    d_value = jnp.einsum("hqk,qhd->khd", rounded, grad_mixed, preferred_element_type=jnp.float32)
    d_weights = jnp.einsum("qhd,khd->hqk", grad_mixed, value, preferred_element_type=jnp.float32)
    centred = d_weights - jnp.sum(weights * d_weights, axis=-1, keepdims=True)
    d_scores = (weights * centred).astype(jnp.bfloat16)
    d_query = jnp.einsum("hqk,khd->qhd", d_scores, key, preferred_element_type=jnp.float32) * scale
    d_key = jnp.einsum("hqk,qhd->khd", d_scores, query, preferred_element_type=jnp.float32) * scale
    return (d_query.astype(jnp.bfloat16), d_key.astype(jnp.bfloat16), d_value.astype(jnp.bfloat16))


def spread_rows(normed):
    return lax.all_gather(normed, "tensor", axis=0, tiled=True)


def spread_grads(grad):
    return lax.all_gather(grad.astype(jnp.bfloat16), "tensor", axis=0, tiled=True)


def branch_total(mixed, weight):
    return lax.psum_scatter(
        jnp.dot(mixed, weight, preferred_element_type=jnp.float32),
        "tensor",
        scatter_dimension=0,
        tiled=True,
    )


def normalized_total(pairs):
    total = None
    for grad, weight in pairs:
        added = times_t(grad, weight)
        total = added if total is None else total + added
    return lax.psum_scatter(total, "tensor", scatter_dimension=0, tiled=True)


def on_device(
    inputs,
    text_states,
    self_query,
    self_key,
    self_value,
    self_output,
    cross_query,
    cross_key,
    cross_value,
    cross_output,
    inner_weight,
    outer_weight,
    norm_gains,
    norm_shifts,
    cotangent,
):
    (
        gathered_self_query,
        gathered_self_key,
        gathered_self_value,
        full_soutput,
        full_cquery,
        full_ckey,
        full_cvalue,
        full_coutput,
        full_inner,
        full_outer,
    ) = (
        lax.all_gather(self_query, "dp", axis=0, tiled=True),
        lax.all_gather(self_key, "dp", axis=0, tiled=True),
        lax.all_gather(self_value, "dp", axis=0, tiled=True),
        lax.all_gather(self_output, "dp", axis=1, tiled=True),
        lax.all_gather(cross_query, "dp", axis=0, tiled=True),
        lax.all_gather(cross_key, "dp", axis=0, tiled=True),
        lax.all_gather(cross_value, "dp", axis=0, tiled=True),
        lax.all_gather(cross_output, "dp", axis=1, tiled=True),
        lax.all_gather(inner_weight, "dp", axis=0, tiled=True),
        lax.all_gather(outer_weight, "dp", axis=1, tiled=True),
    )
    width = inputs.shape[1]
    clips = text_states.shape[0]
    local_heads = gathered_self_query.shape[1] // HD

    def heads(value, length):
        return value.reshape(clips, length, local_heads, HD)

    def flatten(value):
        return value.reshape(-1, local_heads * HD)

    start = inputs.astype(jnp.float32)
    first_rows = spread_rows(norm_rows(start, norm_gains[0], norm_shifts[0]).astype(jnp.bfloat16))
    query1 = apply_projection(first_rows, gathered_self_query)
    first_key = apply_projection(first_rows, gathered_self_key)
    value1 = apply_projection(first_rows, gathered_self_value)
    mixed1, lse1 = lax.map(
        partial(attend, masked=True),
        (heads(query1, LEN), heads(first_key, LEN), heads(value1, LEN)),
    )
    mixed1 = flatten(mixed1)
    state1 = start + branch_total(mixed1, full_soutput)
    rows2 = spread_rows(norm_rows(state1, norm_gains[1], norm_shifts[1]).astype(jnp.bfloat16))
    query2 = apply_projection(rows2, full_cquery)
    text_flat = text_states.reshape(-1, width)
    key2 = apply_projection(text_flat, full_ckey)
    value2 = apply_projection(text_flat, full_cvalue)
    mixed2, lse2 = lax.map(
        partial(attend, masked=False), (heads(query2, LEN), heads(key2, TEXT), heads(value2, TEXT))
    )
    mixed2 = flatten(mixed2)
    state2 = state1 + branch_total(mixed2, full_coutput)
    rows3 = spread_rows(norm_rows(state2, norm_gains[2], norm_shifts[2]).astype(jnp.bfloat16))
    inner = jnp.dot(rows3, full_inner, preferred_element_type=jnp.float32)
    active_float, gelu_pull = jax.vjp(gelu_exact, inner)
    active = active_float.astype(jnp.bfloat16)
    result = state2 + branch_total(active, full_outer)
    output = result.astype(jnp.bfloat16)
    grad3 = cotangent.astype(jnp.float32)
    grads_outer = spread_grads(grad3)
    d_outer = transposed_times(active, grads_outer)
    d_inner = gelu_pull(times_t(grads_outer, full_outer))[0].astype(jnp.bfloat16)
    d_innerw = transposed_times(rows3, d_inner)
    back3 = normalized_total(((d_inner, full_inner),))
    d_state2, gain_three, shift_three = norm_back(state2, norm_gains[2], norm_shifts[2], back3)
    grad2 = grad3 + d_state2
    grads_cross = spread_grads(grad2)
    d_coutput = transposed_times(mixed2, grads_cross)
    d_mixed2 = times_t(grads_cross, full_coutput).astype(jnp.bfloat16)
    d_query2, d_key2, d_value2 = lax.map(
        partial(attend_back, masked=False),
        (heads(query2, LEN), heads(key2, TEXT), heads(value2, TEXT), lse2, heads(d_mixed2, LEN)),
    )
    d_query2 = flatten(d_query2)
    d_key2 = flatten(d_key2)
    d_value2 = flatten(d_value2)
    d_cquery = transposed_times(rows2, d_query2)
    d_ckey = transposed_times(text_flat, d_key2)
    d_cvalue = transposed_times(text_flat, d_value2)
    text_terms = (times_t(d_key2, full_ckey) + times_t(d_value2, full_cvalue)).reshape(
        clips, TEXT, width
    )
    text_grad = lax.psum_scatter(
        text_terms.astype(jnp.bfloat16), "tensor", scatter_dimension=2, tiled=True
    ).astype(jnp.float32)
    back2 = normalized_total(((d_query2, full_cquery),))
    d_state1, gain_two, shift_two = norm_back(state1, norm_gains[1], norm_shifts[1], back2)
    grad1 = grad2 + d_state1
    grads_self = spread_grads(grad1)
    d_soutput = transposed_times(mixed1, grads_self)
    d_mixed1 = times_t(grads_self, full_soutput).astype(jnp.bfloat16)
    first_query_grad, first_key_grad, first_value_grad = lax.map(
        partial(attend_back, masked=True),
        (heads(query1, LEN), heads(first_key, LEN), heads(value1, LEN), lse1, heads(d_mixed1, LEN)),
    )
    first_query_grad = flatten(first_query_grad)
    first_key_grad = flatten(first_key_grad)
    first_value_grad = flatten(first_value_grad)
    d_squery = transposed_times(first_rows, first_query_grad)
    self_key_partial = transposed_times(first_rows, first_key_grad)
    d_svalue = transposed_times(first_rows, first_value_grad)
    first_backward = normalized_total(
        (
            (first_query_grad, gathered_self_query),
            (first_key_grad, gathered_self_key),
            (first_value_grad, gathered_self_value),
        )
    )
    d_start, gain_one, shift_one = norm_back(start, norm_gains[0], norm_shifts[0], first_backward)
    input_grad = grad1 + d_start
    gains_grad, shifts_grad = lax.psum(
        (
            jnp.stack([gain_one, gain_two, gain_three]),
            jnp.stack([shift_one, shift_two, shift_three]),
        ),
        ("dp", "tensor"),
    )
    summed = (
        lax.psum_scatter(
            d_squery.astype(jnp.bfloat16), "dp", scatter_dimension=0, tiled=True
        ).astype(jnp.float32),
        lax.psum_scatter(
            self_key_partial.astype(jnp.bfloat16), "dp", scatter_dimension=0, tiled=True
        ).astype(jnp.float32),
        lax.psum_scatter(
            d_svalue.astype(jnp.bfloat16), "dp", scatter_dimension=0, tiled=True
        ).astype(jnp.float32),
        lax.psum_scatter(
            d_soutput.astype(jnp.bfloat16), "dp", scatter_dimension=1, tiled=True
        ).astype(jnp.float32),
        lax.psum_scatter(
            d_cquery.astype(jnp.bfloat16), "dp", scatter_dimension=0, tiled=True
        ).astype(jnp.float32),
        lax.psum_scatter(d_ckey.astype(jnp.bfloat16), "dp", scatter_dimension=0, tiled=True).astype(
            jnp.float32
        ),
        lax.psum_scatter(
            d_cvalue.astype(jnp.bfloat16), "dp", scatter_dimension=0, tiled=True
        ).astype(jnp.float32),
        lax.psum_scatter(
            d_coutput.astype(jnp.bfloat16), "dp", scatter_dimension=1, tiled=True
        ).astype(jnp.float32),
        lax.psum_scatter(
            d_innerw.astype(jnp.bfloat16), "dp", scatter_dimension=0, tiled=True
        ).astype(jnp.float32),
        lax.psum_scatter(
            d_outer.astype(jnp.bfloat16), "dp", scatter_dimension=1, tiled=True
        ).astype(jnp.float32),
    )
    return (
        output,
        input_grad,
        text_grad,
        summed[0],
        summed[1],
        summed[2],
        summed[3],
        summed[4],
        summed[5],
        summed[6],
        summed[7],
        summed[8],
        summed[9],
        gains_grad,
        shifts_grad,
    )


BF = jnp.bfloat16
F32 = jnp.float32
NN = (((1,), (0,)), ((), ()))
NT = (((1,), (1,)), ((), ()))
TN = (((0,), (0,)), ((), ()))
QB = 256
PAIR = 128
QUAD = 256
CUTS = 2


def after(value, *ready):
    return lax.optimization_barrier((value,) + ready)[0]


def mm(left, right, dims):
    return lax.dot_general(left, right, dims, preferred_element_type=F32)


LIGHT = pl.CostEstimate(flops=1024, transcendentals=0, bytes_accessed=1024)
MIDDLE = pl.CostEstimate(flops=20_000_000_000, transcendentals=0, bytes_accessed=1024)
HEAVY = pl.CostEstimate(flops=10**15, transcendentals=0, bytes_accessed=1024)


def weight_kernel(side_ref, left_ref, right_ref, send_ref, keep_ref, *, shard):
    total = mm(left_ref[...], right_ref[...], TN).astype(BF)
    side = side_ref[0]
    for parity in range(2):
        even, odd = (keep_ref, send_ref) if parity == 0 else (send_ref, keep_ref)

        @pl.when(side == parity)
        def _():
            for at in range(total.shape[0] // shard):
                rows = total[at * shard : (at + 1) * shard, :]
                (odd if at % 2 else even)[at // 2] = rows


def weight_halves(side, left, right, shard, first=0, size=None):
    depth, width = left.shape
    size = size or right.shape[1]
    tile = next(t for t in (768, 1152, 512, 384, 256, 128) if size % t == 0 and first % t == 0)
    count = width // shard // 2
    shape = jax.ShapeDtypeStruct((count, shard, size), BF)
    out = pl.BlockSpec((count, shard, tile), lambda j, s: (0, 0, j))
    return pl.pallas_call(
        partial(weight_kernel, shard=shard),
        out_shape=(shape, shape),
        grid_spec=pltpu.PrefetchScalarGridSpec(
            num_scalar_prefetch=1,
            grid=(size // tile,),
            in_specs=[
                pl.BlockSpec((depth, width), lambda j, s: (0, 0)),
                pl.BlockSpec((depth, tile), lambda j, s: (0, first // tile + j)),
            ],
            out_specs=[out, out],
        ),
        name="weight_halves",
        cost_estimate=LIGHT,
    )(side, left, right)


def added(refs, at=slice(None)):
    total = refs[0][at].astype(F32)
    for ref in refs[1:]:
        total = total + ref[at].astype(F32)
    return total.astype(BF)


def pairs_per_step(count, row_bytes):
    while count > 1 and count % 2 == 0 and count * row_bytes > 5_000_000:
        count //= 2
    return count


def fold_kernel(side_ref, *refs, counts, inner):
    send_ref, keep_ref = refs[-2:]
    side = side_ref[0]
    first, at = 0, 0
    for count in counts:
        terms = refs[at : at + count]
        size = terms[0].shape[2]
        for pair in range(keep_ref.shape[0]):
            for out_ref, bit in ((send_ref, 1 - side), (keep_ref, side)):
                row = (2 * (pair // inner) + bit) * inner + pair % inner
                out_ref[pair, :, first : first + size] = added(terms, row)
        first, at = first + size, at + count


def fold(side, *groups, cost=None, inner=1):
    count, shard = groups[0][0].shape[0] // 2, groups[0][0].shape[1]
    sizes = [terms[0].shape[2] for terms in groups]
    row = sum(4 * shard * size * (len(terms) + 1) for size, terms in zip(sizes, groups))
    per = count if inner > 1 else pairs_per_step(count, row)
    shape = jax.ShapeDtypeStruct((count, shard, sum(sizes)), BF)
    spec = lambda size: pl.BlockSpec((2 * per, shard, size), lambda j, s: (j, 0, 0))
    part = pl.BlockSpec((per, shard, sum(sizes)), lambda j, s: (j, 0, 0))
    return pl.pallas_call(
        partial(fold_kernel, counts=[len(terms) for terms in groups], inner=inner),
        out_shape=(shape, shape),
        grid_spec=pltpu.PrefetchScalarGridSpec(
            num_scalar_prefetch=1,
            grid=(count // per,),
            in_specs=[spec(size) for size, terms in zip(sizes, groups) for _ in terms],
            out_specs=[part, part],
        ),
        name="fold",
        cost_estimate=cost or LIGHT,
    )(side, *[v for terms in groups for v in terms])


def totals_kernel(*refs, counts):
    out_ref = refs[-1]
    first, at = 0, 0
    for count in counts:
        size = refs[at].shape[2]
        out_ref[:, :, first : first + size] = added(refs[at : at + count])
        first, at = first + size, at + count


def totals(*groups):
    count, shard = groups[0][0].shape[:2]
    sizes = [terms[0].shape[2] for terms in groups]
    row = sum(2 * shard * size * (len(terms) + 1) for size, terms in zip(sizes, groups))
    per = pairs_per_step(count, row)
    spec = lambda size: pl.BlockSpec((per, shard, size), lambda j: (j, 0, 0))
    return pl.pallas_call(
        partial(totals_kernel, counts=[len(terms) for terms in groups]),
        grid=(count // per,),
        out_shape=jax.ShapeDtypeStruct((count, shard, sum(sizes)), BF),
        in_specs=[spec(size) for size, terms in zip(sizes, groups) for _ in terms],
        out_specs=spec(sum(sizes)),
        name="totals",
        cost_estimate=LIGHT,
    )(*[v for terms in groups for v in terms])


def pack_kernel(*refs, parts):
    out_ref = refs[-1]
    first = 0
    for which, begin, end, turned in parts:
        ref = refs[which]
        value = ref[begin:end, :].T if turned else ref[:, begin:end]
        out_ref[:, first : first + end - begin] = value
        first += end - begin


def pack(arrays, parts):
    shard = arrays[0].shape[0]
    return pl.pallas_call(
        partial(pack_kernel, parts=parts),
        out_shape=jax.ShapeDtypeStruct((shard, sum(end - begin for _, begin, end, _ in parts)), BF),
        name="pack",
        cost_estimate=LIGHT,
    )(*arrays)


def norm_sums_kernel(value_ref, *refs):
    sums_ref = refs[-1]
    incoming = refs[0][...].astype(F32)
    for ref in refs[1:-1]:
        incoming = incoming + ref[...].astype(F32)
    centred, scale = stats_of(value_ref[...].astype(F32))

    @pl.when(pl.program_id(0) == 0)
    def _():
        sums_ref[...] = jnp.zeros_like(sums_ref)

    sums_ref[0:1, :] += jnp.sum(incoming * (centred * scale), axis=0, keepdims=True)
    sums_ref[1:2, :] += jnp.sum(incoming, axis=0, keepdims=True)


def norm_sums(value, incoming):
    rows, width = value.shape
    tile = 256 if rows % 256 == 0 else 128
    spec = pl.BlockSpec((tile, width), lambda j: (j, 0))
    return pl.pallas_call(
        norm_sums_kernel,
        grid=(rows // tile,),
        out_shape=jax.ShapeDtypeStruct((8, width), F32),
        in_specs=[spec] * (1 + len(incoming)),
        out_specs=pl.BlockSpec((8, width), lambda j: (0, 0)),
        name="norm_sums",
        cost_estimate=LIGHT,
    )(value, *incoming)


def norm_back_kernel(value_ref, gain_ref, base_ref, *refs, parts):
    grad_ref, low_ref, sums_ref = refs[parts:]
    incoming = refs[0][...].astype(F32)
    for ref in refs[1:parts]:
        incoming = incoming + ref[...].astype(F32)
    centred, scale = stats_of(value_ref[...].astype(F32))
    hat = centred * scale
    scaled = incoming * gain_ref[...]
    mean = jnp.mean(scaled, axis=-1, keepdims=True)
    along = jnp.mean(scaled * hat, axis=-1, keepdims=True)
    grad = base_ref[...].astype(F32) + scale * (scaled - mean - hat * along)
    grad_ref[...] = grad
    low_ref[...] = grad.astype(BF)

    @pl.when(pl.program_id(0) == 0)
    def _():
        sums_ref[...] = jnp.zeros_like(sums_ref)

    sums_ref[0:1, :] += jnp.sum(incoming * hat, axis=0, keepdims=True)
    sums_ref[1:2, :] += jnp.sum(incoming, axis=0, keepdims=True)


def norm_back_rows(value, gain, base, incoming, cost=LIGHT):
    rows, width = value.shape
    tile = 256 if rows % 256 == 0 else 128
    spec = pl.BlockSpec((tile, width), lambda j: (j, 0))
    return pl.pallas_call(
        partial(norm_back_kernel, parts=len(incoming)),
        grid=(rows // tile,),
        out_shape=(
            jax.ShapeDtypeStruct((rows, width), F32),
            jax.ShapeDtypeStruct((rows, width), BF),
            jax.ShapeDtypeStruct((8, width), F32),
        ),
        in_specs=[spec, pl.BlockSpec((1, width), lambda j: (0, 0)), spec] + [spec] * len(incoming),
        out_specs=[spec, spec, pl.BlockSpec((8, width), lambda j: (0, 0))],
        name="norm_back",
        cost_estimate=cost,
    )(value, gain.reshape(1, width), base, *incoming)


def joint_kernel(*refs):
    right_ref, out_ref = refs[-2:]
    depth = refs[0].shape[1]
    total = None
    for i, ref in enumerate(refs[:-2]):
        term = mm(ref[...], right_ref[:, i * depth : (i + 1) * depth], NT)
        total = term if total is None else total + term
    out_ref[...] = total.astype(out_ref.dtype)


def joint_product(lefts, right, dtype, row, rows, cost):
    depth, size, tile = lefts[0].shape[1], right.shape[0], 512
    return pl.pallas_call(
        joint_kernel,
        grid=(size // tile,),
        out_shape=jax.ShapeDtypeStruct((rows, size), dtype),
        in_specs=[pl.BlockSpec((rows, depth), lambda j: (row, 0))] * len(lefts)
        + [pl.BlockSpec((tile, depth * len(lefts)), lambda j: (j, 0))],
        out_specs=pl.BlockSpec((rows, tile), lambda j: (0, j)),
        name="joint_product",
        cost_estimate=cost,
    )(*lefts, right)


def product_kernel(left_ref, right_ref, out_ref, *, dims):
    out_ref[...] = mm(left_ref[...], right_ref[...], dims).astype(out_ref.dtype)


def product(left, right, dims, dtype, row=0, rows=None, first=0, size=None, cost=LIGHT):
    rows = rows or left.shape[0]
    depth = left.shape[1]
    if dims is NN:
        size = size or right.shape[1]
        tile = next(t for t in (768, 512, 384, 256) if size % t == 0 and first % t == 0)
        right_spec = pl.BlockSpec((depth, tile), lambda j: (0, first // tile + j))
    else:
        size = right.shape[0]
        tile = 512
        right_spec = pl.BlockSpec((tile, depth), lambda j: (j, first // depth))
    return pl.pallas_call(
        partial(product_kernel, dims=dims),
        grid=(size // tile,),
        out_shape=jax.ShapeDtypeStruct((rows, size), dtype),
        in_specs=[pl.BlockSpec((rows, depth), lambda j: (row, 0)), right_spec],
        out_specs=pl.BlockSpec((rows, tile), lambda j: (0, j)),
        name="product",
        cost_estimate=cost,
    )(left, right)


def lanes_of(width, head):
    lane = lax.broadcasted_iota(jnp.int32, (1, width), 1)
    return (lane >= head * HD) & (lane < (head + 1) * HD)


def only(value, mask):
    return jnp.where(mask, value, jnp.zeros_like(value))


def pieces_of(block):
    start = block * QB
    found = [(0, start, False)] if block else []
    return found + [(start, start + QB, True)]


def causal():
    key = lax.broadcasted_iota(jnp.int32, (QB, QB), 0)
    place = lax.broadcasted_iota(jnp.int32, (QB, QB), 1)
    return key <= place


def to_places(t, ref, held, half):
    low = pl.multiple_of(t * half, half)
    high = pl.multiple_of((1 - t) * half, half)
    held[0:half, :] = ref[pl.ds(low, half), :]
    held[half : 2 * half, :] = ref[pl.ds(high, half), :]


def row_of(t, start, half):
    side = start // half
    base = (1 - t) * half if side else t * half
    return pl.multiple_of(base + start % half, QB)


def self_kernel(t_ref, q_ref, k_ref, v_ref, o_ref, lse_ref, qs, ks, vs):
    t = t_ref[0]
    length = q_ref.shape[0]
    half = length // 2
    for ref, held in ((q_ref, qs), (k_ref, ks), (v_ref, vs)):
        to_places(t, ref, held, half)
    allowed = causal()
    for block in range(length // QB):
        rows = slice(block * QB, (block + 1) * QB)
        query = qs[rows, :] * BF(0.125)
        mixed = []
        for head in range(2):
            mine = only(query, lanes_of(PAIR, head))
            parts = []
            for a, b, edge in pieces_of(block):
                score = mm(ks[a:b, :], mine, NT)
                parts.append(jnp.where(allowed, score, MASKED) if edge else score)
            top = jnp.max(parts[0], axis=0, keepdims=True)
            for part in parts[1:]:
                top = jnp.maximum(top, jnp.max(part, axis=0, keepdims=True))
            total, out = None, None
            for part, (a, b, edge) in zip(parts, pieces_of(block)):
                power = jnp.exp(part - top)
                added = jnp.sum(power, axis=0, keepdims=True)
                term = mm(vs[a:b, :], power.astype(BF), TN)
                total = added if total is None else total + added
                out = term if out is None else out + term
            lse_ref[0, head : head + 1, rows] = top + jnp.log(total)
            mixed.append(out[head * HD : (head + 1) * HD, :] / total)
        both = jnp.concatenate(mixed, axis=0)
        o_ref[pl.ds(row_of(t, block * QB, half), QB), :] = both.T.astype(BF)


def self_forward(t, qkv):
    length, width = qkv.shape
    pairs = width // (3 * PAIR)
    cut = pairs // CUTS
    spec = lambda part: pl.BlockSpec(
        (length, PAIR), lambda j, r: (0, (3 * (j // cut) + part) * cut + j % cut)
    )
    return pl.pallas_call(
        self_kernel,
        out_shape=(
            jax.ShapeDtypeStruct((length, pairs * PAIR), BF),
            jax.ShapeDtypeStruct((pairs, 8, length), F32),
        ),
        grid_spec=pltpu.PrefetchScalarGridSpec(
            num_scalar_prefetch=1,
            grid=(pairs,),
            in_specs=[spec(0), spec(1), spec(2)],
            out_specs=[
                pl.BlockSpec((length, PAIR), lambda j, s: (0, j)),
                pl.BlockSpec((1, 8, length), lambda j, s: (j, 0, 0)),
            ],
            scratch_shapes=[pltpu.VMEM((length, PAIR), BF)] * 3,
        ),
        name="self_attend",
        cost_estimate=LIGHT,
    )(t, qkv, qkv, qkv)


def self_back_kernel(
    t_ref, q_ref, k_ref, v_ref, o_ref, do_ref, lse_ref, out_ref, qs, ks, vs, os, dos, dk, dv, dkb, dvb
):
    t = t_ref[0]
    length = q_ref.shape[0]
    half = length // 2
    step = pl.program_id(1)

    @pl.when(step == 0)
    def _():
        for ref, held in ((q_ref, qs), (k_ref, ks), (v_ref, vs), (o_ref, os), (do_ref, dos)):
            to_places(t, ref, held, half)
        allowed = causal()
        blocks = length // QB
        for block in reversed(range(blocks)):
            rows = slice(block * QB, (block + 1) * QB)
            query = qs[rows, :] * BF(0.125)
            grad = dos[rows, :]
            product = (grad.astype(F32) * os[rows, :].astype(F32)).T
            mine = [only(query, lanes_of(PAIR, head)) for head in range(2)]
            mine_grad = [only(grad, lanes_of(PAIR, head)) for head in range(2)]
            both_query = jnp.concatenate(mine, axis=0)
            both_grad = jnp.concatenate(mine_grad, axis=0)
            d_query = [None, None]
            for a, b, edge in pieces_of(block):
                weights, d_scores = [], []
                for head in range(2):
                    drop = jnp.sum(product[head * HD : (head + 1) * HD, :], axis=0, keepdims=True)
                    score = mm(ks[a:b, :], mine[head], NT)
                    power = jnp.exp(score - lse_ref[0, head : head + 1, rows])
                    if edge:
                        power = jnp.where(allowed, power, 0.0)
                    d_power = mm(vs[a:b, :], mine_grad[head], NT)
                    d_score = (power * (d_power - drop)).astype(BF)
                    weights.append(power.astype(BF))
                    d_scores.append(d_score)
                    term = mm(ks[a:b, :], d_score, TN)
                    d_query[head] = term if d_query[head] is None else d_query[head] + term
                add_v = mm(jnp.concatenate(weights, axis=1), both_grad, NN)
                add_k = mm(jnp.concatenate(d_scores, axis=1), both_query, NN)
                if block == blocks - 1:
                    dv[a:b, :] = add_v
                    dk[a:b, :] = add_k
                else:
                    dv[a:b, :] += add_v
                    dk[a:b, :] += add_k
            both = jnp.concatenate([d_query[0][:HD, :], d_query[1][HD:, :]], axis=0) * 0.125
            out_ref[pl.ds(row_of(t, block * QB, half), QB), :] = both.T.astype(BF)
        for block in range(blocks):
            rows = slice(block * QB, (block + 1) * QB)
            place = row_of(t, block * QB, half)
            dkb[pl.ds(place, QB), :] = dk[rows, :].astype(BF)
            dvb[pl.ds(place, QB), :] = dv[rows, :].astype(BF)

    @pl.when(step == 1)
    def _():
        out_ref[...] = dkb[...]

    @pl.when(step == 2)
    def _():
        out_ref[...] = dvb[...]


def self_backward(t, qkv, mixed, d_mixed, lse, part, cost):
    length, width = qkv.shape[0], qkv.shape[1] // CUTS
    pairs = width // (3 * PAIR)
    first = part * pairs
    spec = lambda kind: pl.BlockSpec(
        (length, PAIR), lambda j, s, r: (0, 3 * first + kind * pairs + j)
    )
    return pl.pallas_call(
        self_back_kernel,
        out_shape=jax.ShapeDtypeStruct((length, width), BF),
        grid_spec=pltpu.PrefetchScalarGridSpec(
            num_scalar_prefetch=1,
            grid=(pairs, 3),
            in_specs=[
                spec(0),
                spec(1),
                spec(2),
                pl.BlockSpec((length, PAIR), lambda j, s, r: (0, first + j)),
                pl.BlockSpec((length, PAIR), lambda j, s, r: (0, first + j)),
                pl.BlockSpec((1, 8, length), lambda j, s, r: (first + j, 0, 0)),
            ],
            out_specs=pl.BlockSpec((length, PAIR), lambda j, s, r: (0, s * pairs + j)),
            scratch_shapes=[pltpu.VMEM((length, PAIR), BF)] * 5
            + [pltpu.VMEM((length, PAIR), F32)] * 2
            + [pltpu.VMEM((length, PAIR), BF)] * 2,
        ),
        name="self_attend_back",
        cost_estimate=cost,
    )(t, qkv, qkv, qkv, mixed, d_mixed, lse)


def spread_heads(value):
    count = QUAD // HD
    return jnp.concatenate([only(value, lanes_of(QUAD, head)) for head in range(count)], axis=0)


def cross_kernel(q_ref, k_ref, v_ref, o_ref, lse_ref):
    keys = k_ref.shape[0]
    scores = mm(spread_heads(k_ref[...] * BF(0.125)), q_ref[...], NT)
    powers, totals = [], []
    for head in range(QUAD // HD):
        score = scores[head * keys : (head + 1) * keys, :]
        top = jnp.max(score, axis=0, keepdims=True)
        power = jnp.exp(score - top)
        total = jnp.sum(power, axis=0, keepdims=True)
        lse_ref[0, head : head + 1, :] = top + jnp.log(total)
        powers.append(power.astype(BF))
        totals.append(total)
    mixed = mm(spread_heads(v_ref[...]), jnp.concatenate(powers, axis=0), TN)
    scaled = [
        mixed[head * HD : (head + 1) * HD, :] / totals[head] for head in range(QUAD // HD)
    ]
    o_ref[...] = jnp.concatenate(scaled, axis=0).T.astype(BF)


def cross_specs(rows, keys, quads):
    return [
        pl.BlockSpec((rows, QUAD), lambda j: (0, j)),
        pl.BlockSpec((keys, QUAD), lambda j: (0, j)),
        pl.BlockSpec((keys, QUAD), lambda j: (0, j)),
    ]


def cross_forward(query, key, value):
    rows, width = query.shape
    keys = key.shape[0]
    quads = width // QUAD
    return pl.pallas_call(
        cross_kernel,
        grid=(quads,),
        out_shape=(
            jax.ShapeDtypeStruct((rows, width), BF),
            jax.ShapeDtypeStruct((quads, 8, rows), F32),
        ),
        in_specs=cross_specs(rows, keys, quads),
        out_specs=[
            pl.BlockSpec((rows, QUAD), lambda j: (0, j)),
            pl.BlockSpec((1, 8, rows), lambda j: (j, 0, 0)),
        ],
        name="cross_attend",
        cost_estimate=LIGHT,
    )(query, key, value)


def cross_back_kernel(q_ref, k_ref, v_ref, o_ref, do_ref, lse_ref, dq_ref, dk_ref, dv_ref):
    keys = k_ref.shape[0]
    count = QUAD // HD
    query, grad = q_ref[...], do_ref[...]
    key = spread_heads(k_ref[...] * BF(0.125))
    scores = mm(key, query, NT)
    d_powers = mm(spread_heads(v_ref[...]), grad, NT)
    product = (grad.astype(F32) * o_ref[...].astype(F32)).T
    weights, d_scores = [], []
    for head in range(count):
        group = slice(head * keys, (head + 1) * keys)
        drop = jnp.sum(product[head * HD : (head + 1) * HD, :], axis=0, keepdims=True)
        power = jnp.exp(scores[group, :] - lse_ref[0, head : head + 1, :])
        weights.append(power.astype(BF))
        d_scores.append((power * (d_powers[group, :] - drop)).astype(BF))
    weights = jnp.concatenate(weights, axis=0)
    d_scores = jnp.concatenate(d_scores, axis=0)
    dq_ref[...] = mm(key, d_scores, TN).T.astype(BF)
    d_key = mm(d_scores, query, NN)
    d_value = mm(weights, grad, NN)
    for ref, found, scale in ((dk_ref, d_key, 0.125), (dv_ref, d_value, 1.0)):
        total = None
        for head in range(count):
            term = only(found[head * keys : (head + 1) * keys, :], lanes_of(QUAD, head))
            total = term if total is None else total + term
        ref[...] = total * scale


def cross_backward(query, key, value, mixed, d_mixed, lse):
    rows, width = query.shape
    keys = key.shape[0]
    quads = width // QUAD
    wide = pl.BlockSpec((rows, QUAD), lambda j: (0, j))
    return pl.pallas_call(
        cross_back_kernel,
        grid=(quads,),
        out_shape=(
            jax.ShapeDtypeStruct((rows, width), BF),
            jax.ShapeDtypeStruct((keys, width), F32),
            jax.ShapeDtypeStruct((keys, width), F32),
        ),
        in_specs=cross_specs(rows, keys, quads)
        + [wide, wide, pl.BlockSpec((1, 8, rows), lambda j: (j, 0, 0))],
        out_specs=[
            wide,
            pl.BlockSpec((keys, QUAD), lambda j: (0, j)),
            pl.BlockSpec((keys, QUAD), lambda j: (0, j)),
        ],
        name="cross_attend_back",
        cost_estimate=LIGHT,
    )(query, key, value, mixed, d_mixed, lse)


FF_STEP = 1024
FF_PART = 256


def ffn_kernel(n_ref, g_ref, wi_ref, wo_ref, *refs):
    act_ref, din_ref = refs[-2:]
    for part in range(wi_ref.shape[1] // FF_PART):
        cols = slice(part * FF_PART, (part + 1) * FF_PART)
        inner = mm(n_ref[...], wi_ref[:, cols], NN)
        d_act = mm(g_ref[...], wo_ref[:, cols], NN)
        phi = 0.5 + 0.5 * lax.erf(inner * (1.0 / math.sqrt(2.0)))
        bell = jnp.exp(inner * inner * -0.5) * (1.0 / math.sqrt(2.0 * math.pi))
        act_ref[:, cols] = (inner * phi).astype(BF)
        din_ref[:, cols] = (d_act * (phi + inner * bell)).astype(BF)


def ffn_middle(normed, grads, weights, block, blocks, kept=()):
    rows, width = normed.shape
    hidden = weights.shape[1] // 2
    steps = hidden // FF_STEP
    out_shape = jax.ShapeDtypeStruct((rows * blocks, hidden), BF)
    whole = pl.BlockSpec((rows, width), lambda j: (0, 0))
    out_spec = pl.BlockSpec((rows, FF_STEP), lambda j: (block, j))
    return pl.pallas_call(
        ffn_kernel,
        grid=(steps,),
        out_shape=(out_shape, out_shape),
        in_specs=[
            whole,
            whole,
            pl.BlockSpec((width, FF_STEP), lambda j: (0, j)),
            pl.BlockSpec((width, FF_STEP), lambda j: (0, steps + j)),
        ]
        + [pl.BlockSpec(memory_space=pl.ANY)] * len(kept),
        out_specs=[out_spec, out_spec],
        input_output_aliases={4 + i: i for i in range(len(kept))},
        name="ffn_middle",
        cost_estimate=LIGHT,
    )(normed, grads, weights, weights, *kept)


def stats_of(value):
    mean = jnp.mean(value, axis=-1, keepdims=True)
    centred = value - mean
    spread = jnp.mean(centred * centred, axis=-1, keepdims=True)
    return centred, lax.rsqrt(spread + EPS)


def norm_grad(value, gain, incoming):
    centred, scale = stats_of(value)
    hat = centred * scale
    scaled = incoming * gain
    mean = jnp.mean(scaled, axis=-1, keepdims=True)
    along = jnp.mean(scaled * hat, axis=-1, keepdims=True)
    return (
        scale * (scaled - mean - hat * along),
        jnp.sum(incoming * hat, axis=0),
        jnp.sum(incoming, axis=0),
    )


def on_pair(
    inputs,
    text_states,
    self_query,
    self_key,
    self_value,
    self_output,
    cross_query,
    cross_key,
    cross_value,
    cross_output,
    inner_weight,
    outer_weight,
    norm_gains,
    norm_shifts,
    cotangent,
    *,
    groups,
):
    rows, width = inputs.shape
    half = width // 2
    hidden = inner_weight.shape[1]
    shard = self_query.shape[0]
    tensor = lax.axis_index("tensor").astype(jnp.uint32)
    place = lax.axis_index("dp").astype(jnp.uint32)
    one = jnp.uint32(1)
    bits = [(place >> i) & one for i in range((groups - 1).bit_length())]
    mine, theirs = tensor * jnp.uint32(half), (tensor ^ one) * jnp.uint32(half)
    zero = jnp.uint32(0)
    lines = [[i + 4 * j for j in range(groups // 4)] for i in range(4)]
    t_ref = tensor.astype(jnp.int32).reshape(1)

    def peer(value):
        return lax.ppermute(value, "tensor", [(0, 1), (1, 0)])

    def gather(packed):
        return lax.all_gather(packed, "dp", axis=0, tiled=True)

    swaps = [[(i, i ^ (1 << level)) for i in range(groups)] for level in range(len(bits))]

    def swap(send, level):
        return lax.ppermute(send, "dp", swaps[level])

    def line_sum(whole):
        whole = whole.reshape(-1, whole.shape[-1])
        return lax.psum_scatter(
            whole, "dp", scatter_dimension=0, tiled=True, axis_index_groups=lines
        )

    def line_step(send, keep, ready):
        return fold(side_refs[3], (after(keep, ready), swap(send, 2)))

    def line_end(send, keep):
        for level in range(3, len(bits)):
            got = swap(send, level)
            if level + 1 < len(bits):
                send, keep = fold(side_refs[level + 1], (keep, got))
        return (keep.astype(F32) + got.astype(F32)).reshape(shard, -1)

    part = half // CUTS
    pieces = [slice(i * part, (i + 1) * part) for i in range(CUTS)]
    side_refs = [bit.astype(jnp.int32).reshape(1) for bit in bits]
    start_x, side_refs, mine, theirs, t_ref = lax.optimization_barrier(
        (inputs, side_refs, mine, theirs, t_ref)
    )
    cross_two = jnp.concatenate([cross_query, cross_output.T], axis=1)
    cross_peer = peer(cross_two)
    taken = [(which, p.start, p.stop, False) for p in pieces for which in range(3)]
    taken += [(3, 0, half, True), (4, 0, half, False), (5, 0, half, False)]
    taken += [(6, 0, half, False), (7, 0, half, False), (6, half, width, False), (7, half, width, False)]
    first = gather(
        pack(
            [self_query, self_key, self_value, self_output, cross_key, cross_value]
            + [cross_two, cross_peer],
            taken,
        )
    )
    second = gather(pack([inner_weight, outer_weight], [(0, 0, hidden, False), (1, 0, hidden, True)]))
    inputs_peer = peer(after(start_x, cross_peer))
    grads_peer = peer(after(cotangent, inputs_peer))
    w_qkv = first[:, : 3 * half]
    w_self_out = first[:, 3 * half : 4 * half]
    w_text = first[:, 4 * half : 6 * half]
    w_cross_query = first[:, 6 * half : 8 * half]
    w_cross_out = first[:, 8 * half :]
    w_inner = second[:, :hidden]
    w_outer = second[:, hidden:]

    start = jnp.concatenate([inputs, inputs_peer], axis=0).astype(F32)
    normed1 = norm_rows(start, norm_gains[0], norm_shifts[0]).astype(BF)
    text = text_states.reshape(-1, width)
    text_own = mm(text, w_text, NN).astype(BF)
    grads3 = jnp.concatenate([cotangent, grads_peer], axis=0)
    normed1 = after(normed1, grads3, text_own)
    qkv = mm(normed1, w_qkv, NN).astype(BF)
    text_peer = peer(text_own)
    mixed1, lse1 = self_forward(t_ref, qkv)
    away = peer(mm(mixed1[rows:], w_self_out, NT).astype(BF))
    home = mm(mixed1[:rows], w_self_out, NT)
    key2 = jnp.concatenate([text_own[:, :half], text_peer[:, :half]], axis=1)
    value2 = jnp.concatenate([text_own[:, half:], text_peer[:, half:]], axis=1)
    state1 = inputs.astype(F32) + home + away.astype(F32)

    normed2 = norm_rows(state1, norm_gains[1], norm_shifts[1]).astype(BF)
    query2 = mm(normed2, w_cross_query, NN).astype(BF)
    mixed2, lse2 = cross_forward(query2, key2, value2)
    state2 = state1 + mm(mixed2, w_cross_out, NT)

    normed3 = norm_rows(state2, norm_gains[2], norm_shifts[2]).astype(BF)
    normed3_peer = peer(normed3)
    active, d_inner = ffn_middle(normed3, cotangent, second, 0, 2)
    back3_home = product(d_inner, second, NT, F32, row=0, rows=rows)
    out_home = product(active, second, NT, F32, row=0, rows=rows, first=hidden)
    normed3_peer = after(normed3_peer, back3_home, out_home)
    active, d_inner = ffn_middle(normed3_peer, grads_peer, second, 1, 2, (active, d_inner))
    back3_part = product(d_inner, second, NT, BF, row=1, rows=rows)
    back3_away = peer(back3_part)
    d_outer = mm(after(grads3, back3_part), active, TN).astype(BF)
    outer_sum = lax.psum_scatter(d_outer, "dp", scatter_dimension=0, tiled=True)
    rows3 = jnp.concatenate([normed3, after(normed3_peer, d_outer)], axis=0)
    last = rows3

    def weight_core(left, right, first=0, size=None):
        nonlocal last
        send, keep = weight_halves(side_refs[0], after(left, last), right, shard, first, size)
        last = send
        return send, keep

    inner = weight_core(rows3, d_inner)
    inner_got = swap(inner[0], 0)

    back3_away = after(back3_away, last)
    grad2, g2, sums3 = norm_back_rows(
        state2, norm_gains[2], cotangent, [back3_home, back3_away], HEAVY
    )
    d_mixed2 = product(g2, first, NN, BF, first=8 * half, size=width)
    inner = fold(side_refs[1], (after(inner[1], d_mixed2), inner_got))
    inner_got = swap(inner[0], 1)
    d_mixed2 = after(d_mixed2, inner[0])
    d_query2, d_key2, d_value2 = cross_backward(query2, key2, value2, mixed2, d_mixed2, lse2)
    d_text_send = jnp.concatenate([d_key2[:, half:], d_value2[:, half:]], axis=1).astype(BF)
    d_text_keep = jnp.concatenate([d_key2[:, :half], d_value2[:, :half]], axis=1)
    d_text_peer = peer(d_text_send)
    back2 = product(after(d_query2, d_text_send), first, NT, F32, first=6 * half)
    grad1, g1, sums2 = norm_back_rows(state1, norm_gains[1], grad2, [back2])
    d_text = (d_text_keep + after(d_text_peer, g1).astype(F32)).astype(BF)
    g1_peer = peer(after(g1, d_text))

    out_part = product(after(active, g1), second, NT, BF, row=1, rows=rows, first=hidden)
    last = out_part

    def two(left, right):
        found = [weight_core(left, right, i * half, half) for i in range(2)]
        return [(keep, swap(send, 0)) for send, keep in found]

    co_own, co_away = two(g2, mixed2)
    cq_own, cq_away = two(normed2, d_query2)
    co_send = totals((after(co_away[0], last), co_away[1]))
    co_got = peer(co_send)
    cq_send = totals((after(cq_away[0], co_send), cq_away[1]))
    cq_got = peer(cq_send)
    last = cq_send
    grads1 = jnp.concatenate([g1, after(g1_peer, last)], axis=0)
    d_mixed1 = product(grads1, first, NN, BF, first=3 * half, size=half)
    found0 = self_backward(t_ref, qkv, mixed1, d_mixed1, lse1, 0, LIGHT)
    text_terms = mm(after(d_text, found0), w_text, NT).astype(BF)
    text_keep, text_send = (
        lax.dynamic_slice(
            text_terms, (zero, at), (text_terms.shape[0], half), allow_negative_indices=False
        )
        for at in (mine, theirs)
    )

    text_got = peer(text_send)
    out_away = peer(after(out_part, found0))
    inner = fold(side_refs[2], (after(inner[1], found0, outer_sum), inner_got))
    last = inner[0]
    qkv0 = weight_core(normed1, found0)
    qkv0_got = swap(qkv0[0], 0)
    so = weight_core(grads1, mixed1)
    so_got = swap(so[0], 0)
    kv = two(text, d_text)
    cross = fold(
        side_refs[1],
        (after(co_own[0], last), co_own[1], co_got),
        (cq_own[0], cq_own[1], cq_got),
    )
    cross_got = swap(cross[0], 1)
    inner_first = after(inner[1], cross[0]), swap(inner[0], 2)
    inner = fold(side_refs[3], inner_first, cost=HEAVY)
    most = fold(
        side_refs[2], (after(qkv0[1], inner[0]), qkv0_got), (so[1], so_got), inner=2
    )
    most_got = swap(most[0], 2)
    kv = fold(side_refs[1], *[(after(keep, most[0]), got) for keep, got in kv])
    kv_got = swap(kv[0], 1)
    found1 = self_backward(t_ref, qkv, mixed1, after(d_mixed1, kv[0]), lse1, 1, MIDDLE)
    last = found1
    qkv1 = weight_core(normed1, found1)
    qkv1_got = swap(qkv1[0], 0)
    cross = totals((after(cross[1], qkv1[0]), cross_got), (kv[1], kv_got))
    cross_sum = line_sum(cross)
    inner_sum = line_end(inner[0], after(inner[1], cross))
    most = fold(side_refs[3], (after(most[1], inner_sum), most_got), inner=2)
    most_got = swap(most[0], 3)
    back1_part = joint_product([found0, after(found1, most[0])], first, BF, 1, rows, HEAVY)
    back1_away = peer(back1_part)
    qkv1 = fold(side_refs[1], (after(qkv1[1], back1_part), qkv1_got))
    qkv1_got = swap(qkv1[0], 1)
    back1_home = joint_product([found0, after(found1, qkv1[0])], first, F32, 0, rows, LIGHT)
    qkv1 = fold(side_refs[2], (after(qkv1[1], back1_home), qkv1_got))
    sums0 = norm_sums(after(inputs_peer, qkv1[0]), [back1_part])
    sums1 = sums0 + norm_sums(after(inputs, sums0), [back1_home])
    most = fold(side_refs[1], (after(most[1], sums1), most_got))
    most_got = swap(most[0], 1)
    qkv1 = line_step(*qkv1, most[0])
    input_grad, _, _ = norm_back_rows(
        inputs, norm_gains[0], grad1, [back1_home, after(back1_away, qkv1[0], cross_sum)]
    )
    most_sum = (most[1].astype(F32) + most_got.astype(F32)).reshape(shard, -1)
    qkv1_sum = line_end(*qkv1)
    qkv0_sum, so_sum = most_sum[:, : 3 * part], most_sum[:, 3 * part :]
    output = (state2 + out_home + after(out_away, last).astype(F32)).astype(BF)
    text_grad = text_keep.astype(F32) + after(text_got, last).astype(F32)
    text_grad = text_grad.reshape(1, -1, half)
    qkv_sums = [qkv0_sum, qkv1_sum]

    small = jnp.stack([v[i] for i in range(2) for v in (sums1, sums2, sums3)])
    small = after(small, back1_away)
    small = small + peer(small)
    bit = 1
    while bit < groups:
        small = small + lax.ppermute(small, "dp", [(i, i ^ bit) for i in range(groups)])
        bit *= 2

    def joined(kind):
        return jnp.concatenate([v[:, kind * part : (kind + 1) * part] for v in qkv_sums], axis=1)

    return (
        output,
        input_grad,
        text_grad,
        joined(0),
        joined(1),
        joined(2),
        so_sum.T,
        cross_sum[:, half : 2 * half].astype(F32),
        cross_sum[:, 2 * half : 3 * half].astype(F32),
        cross_sum[:, 3 * half :].astype(F32),
        cross_sum[:, :half].astype(F32).T,
        inner_sum.astype(F32),
        outer_sum.astype(F32).T,
        small[:3],
        small[3:],
    )


def pairs_up(mesh, inputs, text_states, inner_weight):
    groups, sides = mesh.shape["dp"], mesh.shape["tensor"]
    width = inputs.shape[1]
    return (
        sides == 2
        and groups == 16
        and text_states.shape[0] == groups
        and text_states.shape[1] == TEXT
        and inputs.shape[0] == groups * LEN
        and width % (2 * QUAD) == 0
        and width % (2 * CUTS * PAIR) == 0
        and width % (32 * groups) in (0, 16 * groups)
        and inner_weight.shape[1] % (2 * FF_STEP) == 0
    )


def solution(mesh):
    in_specs = (
        P(("dp", "tensor"), None),
        P("dp", None, None),
        P("dp", "tensor"),
        P("dp", "tensor"),
        P("dp", "tensor"),
        P("tensor", "dp"),
        P("dp", "tensor"),
        P("dp", "tensor"),
        P("dp", "tensor"),
        P("tensor", "dp"),
        P("dp", "tensor"),
        P("tensor", "dp"),
        P(),
        P(),
        P(("dp", "tensor"), None),
    )
    out_specs = (
        P(("dp", "tensor"), None),
        P(("dp", "tensor"), None),
        P("dp", None, "tensor"),
        P("dp", "tensor"),
        P("dp", "tensor"),
        P("dp", "tensor"),
        P("tensor", "dp"),
        P("dp", "tensor"),
        P("dp", "tensor"),
        P("dp", "tensor"),
        P("tensor", "dp"),
        P("dp", "tensor"),
        P("tensor", "dp"),
        P(),
        P(),
    )

    def layer(*args):
        body = on_device
        if pairs_up(mesh, args[0], args[1], args[10]):
            body = partial(on_pair, groups=mesh.shape["dp"])
        return jax.shard_map(
            body, mesh=mesh, in_specs=in_specs, out_specs=out_specs, check_vma=False
        )(*args)

    return layer
```

```python
from functools import partial
import math

import jax
import jax.numpy as jnp
from jax import lax
from jax.experimental import pallas as pl
from jax.experimental.pallas import tpu as pltpu
from jax.sharding import PartitionSpec as P

HD = 64
TEXT = 64
LEN = 1024


EPS = 1e-05
MASKED = -1e30


def norm_rows(value, gain, shift):
    mean = jnp.mean(value, axis=-1, keepdims=True)
    centred = value - mean
    spread = jnp.mean(centred * centred, axis=-1, keepdims=True)
    return centred * lax.rsqrt(spread + EPS) * gain + shift


def norm_back(value, gain, shift, incoming):
    ignored, pullback = jax.vjp(norm_rows, value, gain, shift)
    return pullback(incoming)


def gelu_exact(value):
    return jax.nn.gelu(value, approximate=False)


def transposed_times(left, right):
    return lax.dot_general(
        left, right, (((0,), (0,)), ((), ())), preferred_element_type=jnp.float32
    )


def times_t(left, right):
    return lax.dot_general(
        left, right, (((1,), (1,)), ((), ())), preferred_element_type=jnp.float32
    )


def apply_projection(left, right):
    return jnp.dot(left, right, preferred_element_type=jnp.float32).astype(jnp.bfloat16)


def scores_of(query, key, masked):
    scale = 1.0 / math.sqrt(HD)
    scores = jnp.einsum("qhd,khd->hqk", query, key, preferred_element_type=jnp.float32) * scale
    if masked:
        places = jnp.arange(query.shape[0])
        allowed = places[:, None] >= places[None, :]
        scores = jnp.where(allowed[None], scores, MASKED)
    return scores


def attend(block, masked):
    query, key, value = block
    scores = scores_of(query, key, masked)
    highest = jnp.max(scores, axis=-1, keepdims=True)
    total = jnp.sum(jnp.exp(scores - highest), axis=-1, keepdims=True)
    log_total = highest + jnp.log(total)
    weights = jnp.exp(scores - log_total).astype(jnp.bfloat16)
    mixed = jnp.einsum("hqk,khd->qhd", weights, value, preferred_element_type=jnp.float32)
    return (mixed.astype(jnp.bfloat16), log_total)


def attend_back(block, masked):
    query, key, value, log_total, grad_mixed = block
    scale = 1.0 / math.sqrt(HD)
    weights = jnp.exp(scores_of(query, key, masked) - log_total)
    rounded = weights.astype(jnp.bfloat16)
    d_value = jnp.einsum("hqk,qhd->khd", rounded, grad_mixed, preferred_element_type=jnp.float32)
    d_weights = jnp.einsum("qhd,khd->hqk", grad_mixed, value, preferred_element_type=jnp.float32)
    centred = d_weights - jnp.sum(weights * d_weights, axis=-1, keepdims=True)
    d_scores = (weights * centred).astype(jnp.bfloat16)
    d_query = jnp.einsum("hqk,khd->qhd", d_scores, key, preferred_element_type=jnp.float32) * scale
    d_key = jnp.einsum("hqk,qhd->khd", d_scores, query, preferred_element_type=jnp.float32) * scale
    return (d_query.astype(jnp.bfloat16), d_key.astype(jnp.bfloat16), d_value.astype(jnp.bfloat16))


def spread_rows(normed):
    return lax.all_gather(normed, "tensor", axis=0, tiled=True)


def spread_grads(grad):
    return lax.all_gather(grad.astype(jnp.bfloat16), "tensor", axis=0, tiled=True)


def branch_total(mixed, weight):
    return lax.psum_scatter(
        jnp.dot(mixed, weight, preferred_element_type=jnp.float32),
        "tensor",
        scatter_dimension=0,
        tiled=True,
    )


def normalized_total(pairs):
    total = None
    for grad, weight in pairs:
        added = times_t(grad, weight)
        total = added if total is None else total + added
    return lax.psum_scatter(total, "tensor", scatter_dimension=0, tiled=True)


def on_device(
    inputs,
    text_states,
    self_query,
    self_key,
    self_value,
    self_output,
    cross_query,
    cross_key,
    cross_value,
    cross_output,
    inner_weight,
    outer_weight,
    norm_gains,
    norm_shifts,
    cotangent,
):
    (
        gathered_self_query,
        gathered_self_key,
        gathered_self_value,
        full_soutput,
        full_cquery,
        full_ckey,
        full_cvalue,
        full_coutput,
        full_inner,
        full_outer,
    ) = (
        lax.all_gather(self_query, "dp", axis=0, tiled=True),
        lax.all_gather(self_key, "dp", axis=0, tiled=True),
        lax.all_gather(self_value, "dp", axis=0, tiled=True),
        lax.all_gather(self_output, "dp", axis=1, tiled=True),
        lax.all_gather(cross_query, "dp", axis=0, tiled=True),
        lax.all_gather(cross_key, "dp", axis=0, tiled=True),
        lax.all_gather(cross_value, "dp", axis=0, tiled=True),
        lax.all_gather(cross_output, "dp", axis=1, tiled=True),
        lax.all_gather(inner_weight, "dp", axis=0, tiled=True),
        lax.all_gather(outer_weight, "dp", axis=1, tiled=True),
    )
    width = inputs.shape[1]
    clips = text_states.shape[0]
    local_heads = gathered_self_query.shape[1] // HD

    def heads(value, length):
        return value.reshape(clips, length, local_heads, HD)

    def flatten(value):
        return value.reshape(-1, local_heads * HD)

    start = inputs.astype(jnp.float32)
    first_rows = spread_rows(norm_rows(start, norm_gains[0], norm_shifts[0]).astype(jnp.bfloat16))
    query1 = apply_projection(first_rows, gathered_self_query)
    first_key = apply_projection(first_rows, gathered_self_key)
    value1 = apply_projection(first_rows, gathered_self_value)
    mixed1, lse1 = lax.map(
        partial(attend, masked=True),
        (heads(query1, LEN), heads(first_key, LEN), heads(value1, LEN)),
    )
    mixed1 = flatten(mixed1)
    state1 = start + branch_total(mixed1, full_soutput)
    rows2 = spread_rows(norm_rows(state1, norm_gains[1], norm_shifts[1]).astype(jnp.bfloat16))
    query2 = apply_projection(rows2, full_cquery)
    text_flat = text_states.reshape(-1, width)
    key2 = apply_projection(text_flat, full_ckey)
    value2 = apply_projection(text_flat, full_cvalue)
    mixed2, lse2 = lax.map(
        partial(attend, masked=False), (heads(query2, LEN), heads(key2, TEXT), heads(value2, TEXT))
    )
    mixed2 = flatten(mixed2)
    state2 = state1 + branch_total(mixed2, full_coutput)
    rows3 = spread_rows(norm_rows(state2, norm_gains[2], norm_shifts[2]).astype(jnp.bfloat16))
    inner = jnp.dot(rows3, full_inner, preferred_element_type=jnp.float32)
    active_float, gelu_pull = jax.vjp(gelu_exact, inner)
    active = active_float.astype(jnp.bfloat16)
    result = state2 + branch_total(active, full_outer)
    output = result.astype(jnp.bfloat16)
    grad3 = cotangent.astype(jnp.float32)
    grads_outer = spread_grads(grad3)
    d_outer = transposed_times(active, grads_outer)
    d_inner = gelu_pull(times_t(grads_outer, full_outer))[0].astype(jnp.bfloat16)
    d_innerw = transposed_times(rows3, d_inner)
    back3 = normalized_total(((d_inner, full_inner),))
    d_state2, gain_three, shift_three = norm_back(state2, norm_gains[2], norm_shifts[2], back3)
    grad2 = grad3 + d_state2
    grads_cross = spread_grads(grad2)
    d_coutput = transposed_times(mixed2, grads_cross)
    d_mixed2 = times_t(grads_cross, full_coutput).astype(jnp.bfloat16)
    d_query2, d_key2, d_value2 = lax.map(
        partial(attend_back, masked=False),
        (heads(query2, LEN), heads(key2, TEXT), heads(value2, TEXT), lse2, heads(d_mixed2, LEN)),
    )
    d_query2 = flatten(d_query2)
    d_key2 = flatten(d_key2)
    d_value2 = flatten(d_value2)
    d_cquery = transposed_times(rows2, d_query2)
    d_ckey = transposed_times(text_flat, d_key2)
    d_cvalue = transposed_times(text_flat, d_value2)
    text_terms = (times_t(d_key2, full_ckey) + times_t(d_value2, full_cvalue)).reshape(
        clips, TEXT, width
    )
    text_grad = lax.psum_scatter(
        text_terms.astype(jnp.bfloat16), "tensor", scatter_dimension=2, tiled=True
    ).astype(jnp.float32)
    back2 = normalized_total(((d_query2, full_cquery),))
    d_state1, gain_two, shift_two = norm_back(state1, norm_gains[1], norm_shifts[1], back2)
    grad1 = grad2 + d_state1
    grads_self = spread_grads(grad1)
    d_soutput = transposed_times(mixed1, grads_self)
    d_mixed1 = times_t(grads_self, full_soutput).astype(jnp.bfloat16)
    first_query_grad, first_key_grad, first_value_grad = lax.map(
        partial(attend_back, masked=True),
        (heads(query1, LEN), heads(first_key, LEN), heads(value1, LEN), lse1, heads(d_mixed1, LEN)),
    )
    first_query_grad = flatten(first_query_grad)
    first_key_grad = flatten(first_key_grad)
    first_value_grad = flatten(first_value_grad)
    d_squery = transposed_times(first_rows, first_query_grad)
    self_key_partial = transposed_times(first_rows, first_key_grad)
    d_svalue = transposed_times(first_rows, first_value_grad)
    first_backward = normalized_total(
        (
            (first_query_grad, gathered_self_query),
            (first_key_grad, gathered_self_key),
            (first_value_grad, gathered_self_value),
        )
    )
    d_start, gain_one, shift_one = norm_back(start, norm_gains[0], norm_shifts[0], first_backward)
    input_grad = grad1 + d_start
    gains_grad, shifts_grad = lax.psum(
        (
            jnp.stack([gain_one, gain_two, gain_three]),
            jnp.stack([shift_one, shift_two, shift_three]),
        ),
        ("dp", "tensor"),
    )
    summed = (
        lax.psum_scatter(
            d_squery.astype(jnp.bfloat16), "dp", scatter_dimension=0, tiled=True
        ).astype(jnp.float32),
        lax.psum_scatter(
            self_key_partial.astype(jnp.bfloat16), "dp", scatter_dimension=0, tiled=True
        ).astype(jnp.float32),
        lax.psum_scatter(
            d_svalue.astype(jnp.bfloat16), "dp", scatter_dimension=0, tiled=True
        ).astype(jnp.float32),
        lax.psum_scatter(
            d_soutput.astype(jnp.bfloat16), "dp", scatter_dimension=1, tiled=True
        ).astype(jnp.float32),
        lax.psum_scatter(
            d_cquery.astype(jnp.bfloat16), "dp", scatter_dimension=0, tiled=True
        ).astype(jnp.float32),
        lax.psum_scatter(d_ckey.astype(jnp.bfloat16), "dp", scatter_dimension=0, tiled=True).astype(
            jnp.float32
        ),
        lax.psum_scatter(
            d_cvalue.astype(jnp.bfloat16), "dp", scatter_dimension=0, tiled=True
        ).astype(jnp.float32),
        lax.psum_scatter(
            d_coutput.astype(jnp.bfloat16), "dp", scatter_dimension=1, tiled=True
        ).astype(jnp.float32),
        lax.psum_scatter(
            d_innerw.astype(jnp.bfloat16), "dp", scatter_dimension=0, tiled=True
        ).astype(jnp.float32),
        lax.psum_scatter(
            d_outer.astype(jnp.bfloat16), "dp", scatter_dimension=1, tiled=True
        ).astype(jnp.float32),
    )
    return (
        output,
        input_grad,
        text_grad,
        summed[0],
        summed[1],
        summed[2],
        summed[3],
        summed[4],
        summed[5],
        summed[6],
        summed[7],
        summed[8],
        summed[9],
        gains_grad,
        shifts_grad,
    )


BF = jnp.bfloat16
F32 = jnp.float32
NN = (((1,), (0,)), ((), ()))
NT = (((1,), (1,)), ((), ()))
TN = (((0,), (0,)), ((), ()))
QB = 256
PAIR = 128
QUAD = 256
CUTS = 2


def after(value, *ready):
    return lax.optimization_barrier((value,) + ready)[0]


def mm(left, right, dims):
    return lax.dot_general(left, right, dims, preferred_element_type=F32)


LIGHT = pl.CostEstimate(flops=1024, transcendentals=0, bytes_accessed=1024)
MIDDLE = pl.CostEstimate(flops=20_000_000_000, transcendentals=0, bytes_accessed=1024)
HEAVY = pl.CostEstimate(flops=10**15, transcendentals=0, bytes_accessed=1024)


def weight_kernel(side_ref, left_ref, right_ref, send_ref, keep_ref, *, shard):
    total = mm(left_ref[...], right_ref[...], TN).astype(BF)
    side = side_ref[0]
    for parity in range(2):
        even, odd = (keep_ref, send_ref) if parity == 0 else (send_ref, keep_ref)

        @pl.when(side == parity)
        def _():
            for at in range(total.shape[0] // shard):
                rows = total[at * shard : (at + 1) * shard, :]
                (odd if at % 2 else even)[at // 2] = rows


def weight_halves(side, left, right, shard, first=0, size=None):
    depth, width = left.shape
    size = size or right.shape[1]
    tile = next(t for t in (768, 1152, 512, 384, 256, 128) if size % t == 0 and first % t == 0)
    count = width // shard // 2
    shape = jax.ShapeDtypeStruct((count, shard, size), BF)
    out = pl.BlockSpec((count, shard, tile), lambda j, s: (0, 0, j))
    return pl.pallas_call(
        partial(weight_kernel, shard=shard),
        out_shape=(shape, shape),
        grid_spec=pltpu.PrefetchScalarGridSpec(
            num_scalar_prefetch=1,
            grid=(size // tile,),
            in_specs=[
                pl.BlockSpec((depth, width), lambda j, s: (0, 0)),
                pl.BlockSpec((depth, tile), lambda j, s: (0, first // tile + j)),
            ],
            out_specs=[out, out],
        ),
        name="weight_halves",
        cost_estimate=LIGHT,
    )(side, left, right)


def added(refs, at=slice(None)):
    total = refs[0][at].astype(F32)
    for ref in refs[1:]:
        total = total + ref[at].astype(F32)
    return total.astype(BF)


def pairs_per_step(count, row_bytes):
    while count > 1 and count % 2 == 0 and count * row_bytes > 5_000_000:
        count //= 2
    return count


def fold_kernel(side_ref, *refs, counts, inner):
    send_ref, keep_ref = refs[-2:]
    side = side_ref[0]
    first, at = 0, 0
    for count in counts:
        terms = refs[at : at + count]
        size = terms[0].shape[2]
        for pair in range(keep_ref.shape[0]):
            for out_ref, bit in ((send_ref, 1 - side), (keep_ref, side)):
                row = (2 * (pair // inner) + bit) * inner + pair % inner
                out_ref[pair, :, first : first + size] = added(terms, row)
        first, at = first + size, at + count


def fold(side, *groups, cost=None, inner=1):
    count, shard = groups[0][0].shape[0] // 2, groups[0][0].shape[1]
    sizes = [terms[0].shape[2] for terms in groups]
    row = sum(4 * shard * size * (len(terms) + 1) for size, terms in zip(sizes, groups))
    per = count if inner > 1 else pairs_per_step(count, row)
    shape = jax.ShapeDtypeStruct((count, shard, sum(sizes)), BF)
    spec = lambda size: pl.BlockSpec((2 * per, shard, size), lambda j, s: (j, 0, 0))
    part = pl.BlockSpec((per, shard, sum(sizes)), lambda j, s: (j, 0, 0))
    return pl.pallas_call(
        partial(fold_kernel, counts=[len(terms) for terms in groups], inner=inner),
        out_shape=(shape, shape),
        grid_spec=pltpu.PrefetchScalarGridSpec(
            num_scalar_prefetch=1,
            grid=(count // per,),
            in_specs=[spec(size) for size, terms in zip(sizes, groups) for _ in terms],
            out_specs=[part, part],
        ),
        name="fold",
        cost_estimate=cost or LIGHT,
    )(side, *[v for terms in groups for v in terms])


def totals_kernel(*refs, counts):
    out_ref = refs[-1]
    first, at = 0, 0
    for count in counts:
        size = refs[at].shape[2]
        out_ref[:, :, first : first + size] = added(refs[at : at + count])
        first, at = first + size, at + count


def totals(*groups):
    count, shard = groups[0][0].shape[:2]
    sizes = [terms[0].shape[2] for terms in groups]
    row = sum(2 * shard * size * (len(terms) + 1) for size, terms in zip(sizes, groups))
    per = pairs_per_step(count, row)
    spec = lambda size: pl.BlockSpec((per, shard, size), lambda j: (j, 0, 0))
    return pl.pallas_call(
        partial(totals_kernel, counts=[len(terms) for terms in groups]),
        grid=(count // per,),
        out_shape=jax.ShapeDtypeStruct((count, shard, sum(sizes)), BF),
        in_specs=[spec(size) for size, terms in zip(sizes, groups) for _ in terms],
        out_specs=spec(sum(sizes)),
        name="totals",
        cost_estimate=LIGHT,
    )(*[v for terms in groups for v in terms])


def pack_kernel(*refs, parts):
    out_ref = refs[-1]
    first = 0
    for which, begin, end, turned in parts:
        ref = refs[which]
        value = ref[begin:end, :].T if turned else ref[:, begin:end]
        out_ref[:, first : first + end - begin] = value
        first += end - begin


def pack(arrays, parts):
    shard = arrays[0].shape[0]
    return pl.pallas_call(
        partial(pack_kernel, parts=parts),
        out_shape=jax.ShapeDtypeStruct((shard, sum(end - begin for _, begin, end, _ in parts)), BF),
        name="pack",
        cost_estimate=LIGHT,
    )(*arrays)


def norm_sums_kernel(value_ref, *refs):
    sums_ref = refs[-1]
    incoming = refs[0][...].astype(F32)
    for ref in refs[1:-1]:
        incoming = incoming + ref[...].astype(F32)
    centred, scale = stats_of(value_ref[...].astype(F32))

    @pl.when(pl.program_id(0) == 0)
    def _():
        sums_ref[...] = jnp.zeros_like(sums_ref)

    sums_ref[0:1, :] += jnp.sum(incoming * (centred * scale), axis=0, keepdims=True)
    sums_ref[1:2, :] += jnp.sum(incoming, axis=0, keepdims=True)


def norm_sums(value, incoming):
    rows, width = value.shape
    tile = 256 if rows % 256 == 0 else 128
    spec = pl.BlockSpec((tile, width), lambda j: (j, 0))
    return pl.pallas_call(
        norm_sums_kernel,
        grid=(rows // tile,),
        out_shape=jax.ShapeDtypeStruct((8, width), F32),
        in_specs=[spec] * (1 + len(incoming)),
        out_specs=pl.BlockSpec((8, width), lambda j: (0, 0)),
        name="norm_sums",
        cost_estimate=LIGHT,
    )(value, *incoming)


def norm_back_kernel(value_ref, gain_ref, base_ref, *refs, parts):
    grad_ref, low_ref, sums_ref = refs[parts:]
    incoming = refs[0][...].astype(F32)
    for ref in refs[1:parts]:
        incoming = incoming + ref[...].astype(F32)
    centred, scale = stats_of(value_ref[...].astype(F32))
    hat = centred * scale
    scaled = incoming * gain_ref[...]
    mean = jnp.mean(scaled, axis=-1, keepdims=True)
    along = jnp.mean(scaled * hat, axis=-1, keepdims=True)
    grad = base_ref[...].astype(F32) + scale * (scaled - mean - hat * along)
    grad_ref[...] = grad
    low_ref[...] = grad.astype(BF)

    @pl.when(pl.program_id(0) == 0)
    def _():
        sums_ref[...] = jnp.zeros_like(sums_ref)

    sums_ref[0:1, :] += jnp.sum(incoming * hat, axis=0, keepdims=True)
    sums_ref[1:2, :] += jnp.sum(incoming, axis=0, keepdims=True)


def norm_back_rows(value, gain, base, incoming, cost=LIGHT):
    rows, width = value.shape
    tile = 256 if rows % 256 == 0 else 128
    spec = pl.BlockSpec((tile, width), lambda j: (j, 0))
    return pl.pallas_call(
        partial(norm_back_kernel, parts=len(incoming)),
        grid=(rows // tile,),
        out_shape=(
            jax.ShapeDtypeStruct((rows, width), F32),
            jax.ShapeDtypeStruct((rows, width), BF),
            jax.ShapeDtypeStruct((8, width), F32),
        ),
        in_specs=[spec, pl.BlockSpec((1, width), lambda j: (0, 0)), spec] + [spec] * len(incoming),
        out_specs=[spec, spec, pl.BlockSpec((8, width), lambda j: (0, 0))],
        name="norm_back",
        cost_estimate=cost,
    )(value, gain.reshape(1, width), base, *incoming)


def joint_kernel(*refs):
    right_ref, out_ref = refs[-2:]
    depth = refs[0].shape[1]
    total = None
    for i, ref in enumerate(refs[:-2]):
        term = mm(ref[...], right_ref[:, i * depth : (i + 1) * depth], NT)
        total = term if total is None else total + term
    out_ref[...] = total.astype(out_ref.dtype)


def joint_product(lefts, right, dtype, row, rows, cost):
    depth, size, tile = lefts[0].shape[1], right.shape[0], 512
    return pl.pallas_call(
        joint_kernel,
        grid=(size // tile,),
        out_shape=jax.ShapeDtypeStruct((rows, size), dtype),
        in_specs=[pl.BlockSpec((rows, depth), lambda j: (row, 0))] * len(lefts)
        + [pl.BlockSpec((tile, depth * len(lefts)), lambda j: (j, 0))],
        out_specs=pl.BlockSpec((rows, tile), lambda j: (0, j)),
        name="joint_product",
        cost_estimate=cost,
    )(*lefts, right)


def product_kernel(left_ref, right_ref, out_ref, *, dims):
    out_ref[...] = mm(left_ref[...], right_ref[...], dims).astype(out_ref.dtype)


def product(left, right, dims, dtype, row=0, rows=None, first=0, size=None, cost=LIGHT):
    rows = rows or left.shape[0]
    depth = left.shape[1]
    if dims is NN:
        size = size or right.shape[1]
        tile = next(t for t in (768, 512, 384, 256) if size % t == 0 and first % t == 0)
        right_spec = pl.BlockSpec((depth, tile), lambda j: (0, first // tile + j))
    else:
        size = right.shape[0]
        tile = 512
        right_spec = pl.BlockSpec((tile, depth), lambda j: (j, first // depth))
    return pl.pallas_call(
        partial(product_kernel, dims=dims),
        grid=(size // tile,),
        out_shape=jax.ShapeDtypeStruct((rows, size), dtype),
        in_specs=[pl.BlockSpec((rows, depth), lambda j: (row, 0)), right_spec],
        out_specs=pl.BlockSpec((rows, tile), lambda j: (0, j)),
        name="product",
        cost_estimate=cost,
    )(left, right)


def lanes_of(width, head):
    lane = lax.broadcasted_iota(jnp.int32, (1, width), 1)
    return (lane >= head * HD) & (lane < (head + 1) * HD)


def only(value, mask):
    return jnp.where(mask, value, jnp.zeros_like(value))


def pieces_of(block):
    start = block * QB
    found = [(0, start, False)] if block else []
    return found + [(start, start + QB, True)]


def causal():
    key = lax.broadcasted_iota(jnp.int32, (QB, QB), 0)
    place = lax.broadcasted_iota(jnp.int32, (QB, QB), 1)
    return key <= place


def to_places(t, ref, held, half):
    low = pl.multiple_of(t * half, half)
    high = pl.multiple_of((1 - t) * half, half)
    held[0:half, :] = ref[pl.ds(low, half), :]
    held[half : 2 * half, :] = ref[pl.ds(high, half), :]


def row_of(t, start, half):
    side = start // half
    base = (1 - t) * half if side else t * half
    return pl.multiple_of(base + start % half, QB)


def self_kernel(t_ref, q_ref, k_ref, v_ref, o_ref, lse_ref, qs, ks, vs):
    t = t_ref[0]
    length = q_ref.shape[0]
    half = length // 2
    for ref, held in ((q_ref, qs), (k_ref, ks), (v_ref, vs)):
        to_places(t, ref, held, half)
    allowed = causal()
    for block in range(length // QB):
        rows = slice(block * QB, (block + 1) * QB)
        query = qs[rows, :] * BF(0.125)
        mixed = []
        for head in range(2):
            mine = only(query, lanes_of(PAIR, head))
            parts = []
            for a, b, edge in pieces_of(block):
                score = mm(ks[a:b, :], mine, NT)
                parts.append(jnp.where(allowed, score, MASKED) if edge else score)
            top = jnp.max(parts[0], axis=0, keepdims=True)
            for part in parts[1:]:
                top = jnp.maximum(top, jnp.max(part, axis=0, keepdims=True))
            total, out = None, None
            for part, (a, b, edge) in zip(parts, pieces_of(block)):
                power = jnp.exp(part - top)
                added = jnp.sum(power, axis=0, keepdims=True)
                term = mm(vs[a:b, :], power.astype(BF), TN)
                total = added if total is None else total + added
                out = term if out is None else out + term
            lse_ref[0, head : head + 1, rows] = top + jnp.log(total)
            mixed.append(out[head * HD : (head + 1) * HD, :] / total)
        both = jnp.concatenate(mixed, axis=0)
        o_ref[pl.ds(row_of(t, block * QB, half), QB), :] = both.T.astype(BF)


def self_forward(t, qkv):
    length, width = qkv.shape
    pairs = width // (3 * PAIR)
    cut = pairs // CUTS
    spec = lambda part: pl.BlockSpec(
        (length, PAIR), lambda j, r: (0, (3 * (j // cut) + part) * cut + j % cut)
    )
    return pl.pallas_call(
        self_kernel,
        out_shape=(
            jax.ShapeDtypeStruct((length, pairs * PAIR), BF),
            jax.ShapeDtypeStruct((pairs, 8, length), F32),
        ),
        grid_spec=pltpu.PrefetchScalarGridSpec(
            num_scalar_prefetch=1,
            grid=(pairs,),
            in_specs=[spec(0), spec(1), spec(2)],
            out_specs=[
                pl.BlockSpec((length, PAIR), lambda j, s: (0, j)),
                pl.BlockSpec((1, 8, length), lambda j, s: (j, 0, 0)),
            ],
            scratch_shapes=[pltpu.VMEM((length, PAIR), BF)] * 3,
        ),
        name="self_attend",
        cost_estimate=LIGHT,
    )(t, qkv, qkv, qkv)


def self_back_kernel(
    t_ref, q_ref, k_ref, v_ref, o_ref, do_ref, lse_ref, out_ref, qs, ks, vs, os, dos, dk, dv, dkb, dvb
):
    t = t_ref[0]
    length = q_ref.shape[0]
    half = length // 2
    step = pl.program_id(1)

    @pl.when(step == 0)
    def _():
        for ref, held in ((q_ref, qs), (k_ref, ks), (v_ref, vs), (o_ref, os), (do_ref, dos)):
            to_places(t, ref, held, half)
        allowed = causal()
        blocks = length // QB
        for block in reversed(range(blocks)):
            rows = slice(block * QB, (block + 1) * QB)
            query = qs[rows, :] * BF(0.125)
            grad = dos[rows, :]
            product = (grad.astype(F32) * os[rows, :].astype(F32)).T
            mine = [only(query, lanes_of(PAIR, head)) for head in range(2)]
            mine_grad = [only(grad, lanes_of(PAIR, head)) for head in range(2)]
            both_query = jnp.concatenate(mine, axis=0)
            both_grad = jnp.concatenate(mine_grad, axis=0)
            d_query = [None, None]
            for a, b, edge in pieces_of(block):
                weights, d_scores = [], []
                for head in range(2):
                    drop = jnp.sum(product[head * HD : (head + 1) * HD, :], axis=0, keepdims=True)
                    score = mm(ks[a:b, :], mine[head], NT)
                    power = jnp.exp(score - lse_ref[0, head : head + 1, rows])
                    if edge:
                        power = jnp.where(allowed, power, 0.0)
                    d_power = mm(vs[a:b, :], mine_grad[head], NT)
                    d_score = (power * (d_power - drop)).astype(BF)
                    weights.append(power.astype(BF))
                    d_scores.append(d_score)
                    term = mm(ks[a:b, :], d_score, TN)
                    d_query[head] = term if d_query[head] is None else d_query[head] + term
                add_v = mm(jnp.concatenate(weights, axis=1), both_grad, NN)
                add_k = mm(jnp.concatenate(d_scores, axis=1), both_query, NN)
                if block == blocks - 1:
                    dv[a:b, :] = add_v
                    dk[a:b, :] = add_k
                else:
                    dv[a:b, :] += add_v
                    dk[a:b, :] += add_k
            both = jnp.concatenate([d_query[0][:HD, :], d_query[1][HD:, :]], axis=0) * 0.125
            out_ref[pl.ds(row_of(t, block * QB, half), QB), :] = both.T.astype(BF)
        for block in range(blocks):
            rows = slice(block * QB, (block + 1) * QB)
            place = row_of(t, block * QB, half)
            dkb[pl.ds(place, QB), :] = dk[rows, :].astype(BF)
            dvb[pl.ds(place, QB), :] = dv[rows, :].astype(BF)

    @pl.when(step == 1)
    def _():
        out_ref[...] = dkb[...]

    @pl.when(step == 2)
    def _():
        out_ref[...] = dvb[...]


def self_backward(t, qkv, mixed, d_mixed, lse, part, cost):
    length, width = qkv.shape[0], qkv.shape[1] // CUTS
    pairs = width // (3 * PAIR)
    first = part * pairs
    spec = lambda kind: pl.BlockSpec(
        (length, PAIR), lambda j, s, r: (0, 3 * first + kind * pairs + j)
    )
    return pl.pallas_call(
        self_back_kernel,
        out_shape=jax.ShapeDtypeStruct((length, width), BF),
        grid_spec=pltpu.PrefetchScalarGridSpec(
            num_scalar_prefetch=1,
            grid=(pairs, 3),
            in_specs=[
                spec(0),
                spec(1),
                spec(2),
                pl.BlockSpec((length, PAIR), lambda j, s, r: (0, first + j)),
                pl.BlockSpec((length, PAIR), lambda j, s, r: (0, first + j)),
                pl.BlockSpec((1, 8, length), lambda j, s, r: (first + j, 0, 0)),
            ],
            out_specs=pl.BlockSpec((length, PAIR), lambda j, s, r: (0, s * pairs + j)),
            scratch_shapes=[pltpu.VMEM((length, PAIR), BF)] * 5
            + [pltpu.VMEM((length, PAIR), F32)] * 2
            + [pltpu.VMEM((length, PAIR), BF)] * 2,
        ),
        name="self_attend_back",
        cost_estimate=cost,
    )(t, qkv, qkv, qkv, mixed, d_mixed, lse)


def spread_heads(value):
    count = QUAD // HD
    return jnp.concatenate([only(value, lanes_of(QUAD, head)) for head in range(count)], axis=0)


def cross_kernel(q_ref, k_ref, v_ref, o_ref, lse_ref):
    keys = k_ref.shape[0]
    scores = mm(spread_heads(k_ref[...] * BF(0.125)), q_ref[...], NT)
    powers, totals = [], []
    for head in range(QUAD // HD):
        score = scores[head * keys : (head + 1) * keys, :]
        top = jnp.max(score, axis=0, keepdims=True)
        power = jnp.exp(score - top)
        total = jnp.sum(power, axis=0, keepdims=True)
        lse_ref[0, head : head + 1, :] = top + jnp.log(total)
        powers.append(power.astype(BF))
        totals.append(total)
    mixed = mm(spread_heads(v_ref[...]), jnp.concatenate(powers, axis=0), TN)
    scaled = [
        mixed[head * HD : (head + 1) * HD, :] / totals[head] for head in range(QUAD // HD)
    ]
    o_ref[...] = jnp.concatenate(scaled, axis=0).T.astype(BF)


def cross_specs(rows, keys, quads):
    return [
        pl.BlockSpec((rows, QUAD), lambda j: (0, j)),
        pl.BlockSpec((keys, QUAD), lambda j: (0, j)),
        pl.BlockSpec((keys, QUAD), lambda j: (0, j)),
    ]


def cross_forward(query, key, value):
    rows, width = query.shape
    keys = key.shape[0]
    quads = width // QUAD
    return pl.pallas_call(
        cross_kernel,
        grid=(quads,),
        out_shape=(
            jax.ShapeDtypeStruct((rows, width), BF),
            jax.ShapeDtypeStruct((quads, 8, rows), F32),
        ),
        in_specs=cross_specs(rows, keys, quads),
        out_specs=[
            pl.BlockSpec((rows, QUAD), lambda j: (0, j)),
            pl.BlockSpec((1, 8, rows), lambda j: (j, 0, 0)),
        ],
        name="cross_attend",
        cost_estimate=LIGHT,
    )(query, key, value)


def cross_back_kernel(q_ref, k_ref, v_ref, o_ref, do_ref, lse_ref, dq_ref, dk_ref, dv_ref):
    keys = k_ref.shape[0]
    count = QUAD // HD
    query, grad = q_ref[...], do_ref[...]
    key = spread_heads(k_ref[...] * BF(0.125))
    scores = mm(key, query, NT)
    d_powers = mm(spread_heads(v_ref[...]), grad, NT)
    product = (grad.astype(F32) * o_ref[...].astype(F32)).T
    weights, d_scores = [], []
    for head in range(count):
        group = slice(head * keys, (head + 1) * keys)
        drop = jnp.sum(product[head * HD : (head + 1) * HD, :], axis=0, keepdims=True)
        power = jnp.exp(scores[group, :] - lse_ref[0, head : head + 1, :])
        weights.append(power.astype(BF))
        d_scores.append((power * (d_powers[group, :] - drop)).astype(BF))
    weights = jnp.concatenate(weights, axis=0)
    d_scores = jnp.concatenate(d_scores, axis=0)
    dq_ref[...] = mm(key, d_scores, TN).T.astype(BF)
    d_key = mm(d_scores, query, NN)
    d_value = mm(weights, grad, NN)
    for ref, found, scale in ((dk_ref, d_key, 0.125), (dv_ref, d_value, 1.0)):
        total = None
        for head in range(count):
            term = only(found[head * keys : (head + 1) * keys, :], lanes_of(QUAD, head))
            total = term if total is None else total + term
        ref[...] = total * scale


def cross_backward(query, key, value, mixed, d_mixed, lse):
    rows, width = query.shape
    keys = key.shape[0]
    quads = width // QUAD
    wide = pl.BlockSpec((rows, QUAD), lambda j: (0, j))
    return pl.pallas_call(
        cross_back_kernel,
        grid=(quads,),
        out_shape=(
            jax.ShapeDtypeStruct((rows, width), BF),
            jax.ShapeDtypeStruct((keys, width), F32),
            jax.ShapeDtypeStruct((keys, width), F32),
        ),
        in_specs=cross_specs(rows, keys, quads)
        + [wide, wide, pl.BlockSpec((1, 8, rows), lambda j: (j, 0, 0))],
        out_specs=[
            wide,
            pl.BlockSpec((keys, QUAD), lambda j: (0, j)),
            pl.BlockSpec((keys, QUAD), lambda j: (0, j)),
        ],
        name="cross_attend_back",
        cost_estimate=LIGHT,
    )(query, key, value, mixed, d_mixed, lse)


FF_STEP = 1024
FF_PART = 256


def ffn_kernel(n_ref, g_ref, wi_ref, wo_ref, *refs):
    act_ref, din_ref = refs[-2:]
    for part in range(wi_ref.shape[1] // FF_PART):
        cols = slice(part * FF_PART, (part + 1) * FF_PART)
        inner = mm(n_ref[...], wi_ref[:, cols], NN)
        d_act = mm(g_ref[...], wo_ref[:, cols], NN)
        phi = 0.5 + 0.5 * lax.erf(inner * (1.0 / math.sqrt(2.0)))
        bell = jnp.exp(inner * inner * -0.5) * (1.0 / math.sqrt(2.0 * math.pi))
        act_ref[:, cols] = (inner * phi).astype(BF)
        din_ref[:, cols] = (d_act * (phi + inner * bell)).astype(BF)


def ffn_middle(normed, grads, weights, block, blocks, kept=()):
    rows, width = normed.shape
    hidden = weights.shape[1] // 2
    steps = hidden // FF_STEP
    out_shape = jax.ShapeDtypeStruct((rows * blocks, hidden), BF)
    whole = pl.BlockSpec((rows, width), lambda j: (0, 0))
    out_spec = pl.BlockSpec((rows, FF_STEP), lambda j: (block, j))
    return pl.pallas_call(
        ffn_kernel,
        grid=(steps,),
        out_shape=(out_shape, out_shape),
        in_specs=[
            whole,
            whole,
            pl.BlockSpec((width, FF_STEP), lambda j: (0, j)),
            pl.BlockSpec((width, FF_STEP), lambda j: (0, steps + j)),
        ]
        + [pl.BlockSpec(memory_space=pl.ANY)] * len(kept),
        out_specs=[out_spec, out_spec],
        input_output_aliases={4 + i: i for i in range(len(kept))},
        name="ffn_middle",
        cost_estimate=LIGHT,
    )(normed, grads, weights, weights, *kept)


def stats_of(value):
    mean = jnp.mean(value, axis=-1, keepdims=True)
    centred = value - mean
    spread = jnp.mean(centred * centred, axis=-1, keepdims=True)
    return centred, lax.rsqrt(spread + EPS)


def norm_grad(value, gain, incoming):
    centred, scale = stats_of(value)
    hat = centred * scale
    scaled = incoming * gain
    mean = jnp.mean(scaled, axis=-1, keepdims=True)
    along = jnp.mean(scaled * hat, axis=-1, keepdims=True)
    return (
        scale * (scaled - mean - hat * along),
        jnp.sum(incoming * hat, axis=0),
        jnp.sum(incoming, axis=0),
    )


def on_pair(
    inputs,
    text_states,
    self_query,
    self_key,
    self_value,
    self_output,
    cross_query,
    cross_key,
    cross_value,
    cross_output,
    inner_weight,
    outer_weight,
    norm_gains,
    norm_shifts,
    cotangent,
    *,
    groups,
):
    rows, width = inputs.shape
    half = width // 2
    hidden = inner_weight.shape[1]
    shard = self_query.shape[0]
    tensor = lax.axis_index("tensor").astype(jnp.uint32)
    place = lax.axis_index("dp").astype(jnp.uint32)
    one = jnp.uint32(1)
    bits = [(place >> i) & one for i in range((groups - 1).bit_length())]
    mine, theirs = tensor * jnp.uint32(half), (tensor ^ one) * jnp.uint32(half)
    zero = jnp.uint32(0)
    lines = [[i + 4 * j for j in range(groups // 4)] for i in range(4)]
    t_ref = tensor.astype(jnp.int32).reshape(1)

    def peer(value):
        return lax.ppermute(value, "tensor", [(0, 1), (1, 0)])

    def gather(packed):
        return lax.all_gather(packed, "dp", axis=0, tiled=True)

    swaps = [[(i, i ^ (1 << level)) for i in range(groups)] for level in range(len(bits))]

    def swap(send, level):
        return lax.ppermute(send, "dp", swaps[level])

    def line_sum(whole):
        whole = whole.reshape(-1, whole.shape[-1])
        return lax.psum_scatter(
            whole, "dp", scatter_dimension=0, tiled=True, axis_index_groups=lines
        )

    def line_step(send, keep, ready):
        return fold(side_refs[3], (after(keep, ready), swap(send, 2)))

    def line_end(send, keep):
        for level in range(3, len(bits)):
            got = swap(send, level)
            if level + 1 < len(bits):
                send, keep = fold(side_refs[level + 1], (keep, got))
        return (keep.astype(F32) + got.astype(F32)).reshape(shard, -1)

    part = half // CUTS
    pieces = [slice(i * part, (i + 1) * part) for i in range(CUTS)]
    side_refs = [bit.astype(jnp.int32).reshape(1) for bit in bits]
    start_x, side_refs, mine, theirs, t_ref = lax.optimization_barrier(
        (inputs, side_refs, mine, theirs, t_ref)
    )
    cross_two = jnp.concatenate([cross_query, cross_output.T], axis=1)
    cross_peer = peer(cross_two)
    taken = [(which, p.start, p.stop, False) for p in pieces for which in range(3)]
    taken += [(3, 0, half, True), (4, 0, half, False), (5, 0, half, False)]
    taken += [(6, 0, half, False), (7, 0, half, False), (6, half, width, False), (7, half, width, False)]
    first = gather(
        pack(
            [self_query, self_key, self_value, self_output, cross_key, cross_value]
            + [cross_two, cross_peer],
            taken,
        )
    )
    second = gather(pack([inner_weight, outer_weight], [(0, 0, hidden, False), (1, 0, hidden, True)]))
    inputs_peer = peer(after(start_x, cross_peer))
    grads_peer = peer(after(cotangent, inputs_peer))
    w_qkv = first[:, : 3 * half]
    w_self_out = first[:, 3 * half : 4 * half]
    w_text = first[:, 4 * half : 6 * half]
    w_cross_query = first[:, 6 * half : 8 * half]
    w_cross_out = first[:, 8 * half :]
    w_inner = second[:, :hidden]
    w_outer = second[:, hidden:]

    start = jnp.concatenate([inputs, inputs_peer], axis=0).astype(F32)
    normed1 = norm_rows(start, norm_gains[0], norm_shifts[0]).astype(BF)
    text = text_states.reshape(-1, width)
    text_own = mm(text, w_text, NN).astype(BF)
    grads3 = jnp.concatenate([cotangent, grads_peer], axis=0)
    normed1 = after(normed1, grads3, text_own)
    qkv = mm(normed1, w_qkv, NN).astype(BF)
    text_peer = peer(text_own)
    mixed1, lse1 = self_forward(t_ref, qkv)
    away = peer(mm(mixed1[rows:], w_self_out, NT).astype(BF))
    home = mm(mixed1[:rows], w_self_out, NT)
    key2 = jnp.concatenate([text_own[:, :half], text_peer[:, :half]], axis=1)
    value2 = jnp.concatenate([text_own[:, half:], text_peer[:, half:]], axis=1)
    state1 = inputs.astype(F32) + home + away.astype(F32)

    normed2 = norm_rows(state1, norm_gains[1], norm_shifts[1]).astype(BF)
    query2 = mm(normed2, w_cross_query, NN).astype(BF)
    mixed2, lse2 = cross_forward(query2, key2, value2)
    state2 = state1 + mm(mixed2, w_cross_out, NT)

    normed3 = norm_rows(state2, norm_gains[2], norm_shifts[2]).astype(BF)
    normed3_peer = peer(normed3)
    active, d_inner = ffn_middle(normed3, cotangent, second, 0, 2)
    back3_home = product(d_inner, second, NT, F32, row=0, rows=rows)
    out_home = product(active, second, NT, F32, row=0, rows=rows, first=hidden)
    normed3_peer = after(normed3_peer, back3_home, out_home)
    active, d_inner = ffn_middle(normed3_peer, grads_peer, second, 1, 2, (active, d_inner))
    back3_part = product(d_inner, second, NT, BF, row=1, rows=rows)
    back3_away = peer(back3_part)
    d_outer = mm(after(grads3, back3_part), active, TN).astype(BF)
    outer_sum = lax.psum_scatter(d_outer, "dp", scatter_dimension=0, tiled=True)
    rows3 = jnp.concatenate([normed3, after(normed3_peer, d_outer)], axis=0)
    last = rows3

    def weight_core(left, right, first=0, size=None):
        nonlocal last
        send, keep = weight_halves(side_refs[0], after(left, last), right, shard, first, size)
        last = send
        return send, keep

    inner = weight_core(rows3, d_inner)
    inner_got = swap(inner[0], 0)

    back3_away = after(back3_away, last)
    grad2, g2, sums3 = norm_back_rows(
        state2, norm_gains[2], cotangent, [back3_home, back3_away], HEAVY
    )
    d_mixed2 = product(g2, first, NN, BF, first=8 * half, size=width)
    inner = fold(side_refs[1], (after(inner[1], d_mixed2), inner_got))
    inner_got = swap(inner[0], 1)
    d_mixed2 = after(d_mixed2, inner[0])
    d_query2, d_key2, d_value2 = cross_backward(query2, key2, value2, mixed2, d_mixed2, lse2)
    d_text_send = jnp.concatenate([d_key2[:, half:], d_value2[:, half:]], axis=1).astype(BF)
    d_text_keep = jnp.concatenate([d_key2[:, :half], d_value2[:, :half]], axis=1)
    d_text_peer = peer(d_text_send)
    back2 = product(after(d_query2, d_text_send), first, NT, F32, first=6 * half)
    grad1, g1, sums2 = norm_back_rows(state1, norm_gains[1], grad2, [back2])
    d_text = (d_text_keep + after(d_text_peer, g1).astype(F32)).astype(BF)
    g1_peer = peer(after(g1, d_text))

    out_part = product(after(active, g1), second, NT, BF, row=1, rows=rows, first=hidden)
    last = out_part

    def two(left, right):
        found = [weight_core(left, right, i * half, half) for i in range(2)]
        return [(keep, swap(send, 0)) for send, keep in found]

    co_own, co_away = two(g2, mixed2)
    cq_own, cq_away = two(normed2, d_query2)
    co_send = totals((after(co_away[0], last), co_away[1]))
    co_got = peer(co_send)
    cq_send = totals((after(cq_away[0], co_send), cq_away[1]))
    cq_got = peer(cq_send)
    last = cq_send
    grads1 = jnp.concatenate([g1, after(g1_peer, last)], axis=0)
    d_mixed1 = product(grads1, first, NN, BF, first=3 * half, size=half)
    found0 = self_backward(t_ref, qkv, mixed1, d_mixed1, lse1, 0, LIGHT)
    text_terms = mm(after(d_text, found0), w_text, NT).astype(BF)
    text_keep, text_send = (
        lax.dynamic_slice(
            text_terms, (zero, at), (text_terms.shape[0], half), allow_negative_indices=False
        )
        for at in (mine, theirs)
    )

    text_got = peer(text_send)
    out_away = peer(after(out_part, found0))
    inner = fold(side_refs[2], (after(inner[1], found0, outer_sum), inner_got))
    last = inner[0]
    qkv0 = weight_core(normed1, found0)
    qkv0_got = swap(qkv0[0], 0)
    so = weight_core(grads1, mixed1)
    so_got = swap(so[0], 0)
    kv = two(text, d_text)
    cross = fold(
        side_refs[1],
        (after(co_own[0], last), co_own[1], co_got),
        (cq_own[0], cq_own[1], cq_got),
    )
    cross_got = swap(cross[0], 1)
    inner_first = after(inner[1], cross[0]), swap(inner[0], 2)
    inner = fold(side_refs[3], inner_first, cost=HEAVY)
    most = fold(side_refs[1], (after(qkv0[1], inner[0]), qkv0_got), (so[1], so_got))
    most_got = swap(most[0], 1)
    kv = fold(side_refs[1], *[(after(keep, most[0]), got) for keep, got in kv])
    kv_got = swap(kv[0], 1)
    found1 = self_backward(t_ref, qkv, mixed1, after(d_mixed1, kv[0]), lse1, 1, MIDDLE)
    last = found1
    qkv1 = weight_core(normed1, found1)
    qkv1_got = swap(qkv1[0], 0)
    cross = totals((after(cross[1], qkv1[0]), cross_got), (kv[1], kv_got))
    cross_sum = line_sum(cross)
    inner_sum = line_end(inner[0], after(inner[1], cross))
    most = fold(side_refs[2], (after(most[1], inner_sum), most_got))
    back1_part = joint_product([found0, after(found1, most[0])], first, BF, 1, rows, HEAVY)
    back1_away = peer(back1_part)
    qkv1 = fold(side_refs[1], (after(qkv1[1], back1_part), qkv1_got))
    qkv1_got = swap(qkv1[0], 1)
    back1_home = joint_product([found0, after(found1, qkv1[0])], first, F32, 0, rows, LIGHT)
    qkv1 = fold(side_refs[2], (after(qkv1[1], back1_home), qkv1_got))
    sums0 = norm_sums(after(inputs_peer, qkv1[0]), [back1_part])
    sums1 = sums0 + norm_sums(after(inputs, sums0), [back1_home])
    most = line_step(*most, sums1)
    qkv1 = line_step(*qkv1, most[0])
    input_grad, _, _ = norm_back_rows(
        inputs, norm_gains[0], grad1, [back1_home, after(back1_away, qkv1[0], cross_sum)]
    )
    most_sum, qkv1_sum = line_end(*most), line_end(*qkv1)
    qkv0_sum, so_sum = most_sum[:, : 3 * part], most_sum[:, 3 * part :]
    output = (state2 + out_home + after(out_away, last).astype(F32)).astype(BF)
    text_grad = text_keep.astype(F32) + after(text_got, last).astype(F32)
    text_grad = text_grad.reshape(1, -1, half)
    qkv_sums = [qkv0_sum, qkv1_sum]

    small = jnp.stack([v[i] for i in range(2) for v in (sums1, sums2, sums3)])
    small = after(small, back1_away)
    small = small + peer(small)
    bit = 1
    while bit < groups:
        small = small + lax.ppermute(small, "dp", [(i, i ^ bit) for i in range(groups)])
        bit *= 2

    def joined(kind):
        return jnp.concatenate([v[:, kind * part : (kind + 1) * part] for v in qkv_sums], axis=1)

    return (
        output,
        input_grad,
        text_grad,
        joined(0),
        joined(1),
        joined(2),
        so_sum.T,
        cross_sum[:, half : 2 * half].astype(F32),
        cross_sum[:, 2 * half : 3 * half].astype(F32),
        cross_sum[:, 3 * half :].astype(F32),
        cross_sum[:, :half].astype(F32).T,
        inner_sum.astype(F32),
        outer_sum.astype(F32).T,
        small[:3],
        small[3:],
    )


def pairs_up(mesh, inputs, text_states, inner_weight):
    groups, sides = mesh.shape["dp"], mesh.shape["tensor"]
    width = inputs.shape[1]
    return (
        sides == 2
        and groups == 16
        and text_states.shape[0] == groups
        and text_states.shape[1] == TEXT
        and inputs.shape[0] == groups * LEN
        and width % (2 * QUAD) == 0
        and width % (2 * CUTS * PAIR) == 0
        and width % (32 * groups) in (0, 16 * groups)
        and inner_weight.shape[1] % (2 * FF_STEP) == 0
    )


def solution(mesh):
    in_specs = (
        P(("dp", "tensor"), None),
        P("dp", None, None),
        P("dp", "tensor"),
        P("dp", "tensor"),
        P("dp", "tensor"),
        P("tensor", "dp"),
        P("dp", "tensor"),
        P("dp", "tensor"),
        P("dp", "tensor"),
        P("tensor", "dp"),
        P("dp", "tensor"),
        P("tensor", "dp"),
        P(),
        P(),
        P(("dp", "tensor"), None),
    )
    out_specs = (
        P(("dp", "tensor"), None),
        P(("dp", "tensor"), None),
        P("dp", None, "tensor"),
        P("dp", "tensor"),
        P("dp", "tensor"),
        P("dp", "tensor"),
        P("tensor", "dp"),
        P("dp", "tensor"),
        P("dp", "tensor"),
        P("dp", "tensor"),
        P("tensor", "dp"),
        P("dp", "tensor"),
        P("tensor", "dp"),
        P(),
        P(),
    )

    def layer(*args):
        body = on_device
        if pairs_up(mesh, args[0], args[1], args[10]):
            body = partial(on_pair, groups=mesh.shape["dp"])
        return jax.shard_map(
            body, mesh=mesh, in_specs=in_specs, out_specs=out_specs, check_vma=False
        )(*args)

    return layer
```
